256 devices in a mesh: dp: 32 (over z, y), ep: 8 (over x, core).
Axes of the slice: x: 4, y: 4, z: 8, core: 2. Of those that a mesh axis runs over, the one named last changes fastest.
Arguments:
- states: bfloat16 [2048, 16, 128, 128], P(('dp', 'ep')), may hold values from -4 to 4
- query_rows: bfloat16 [2048, 4, 1024], P(('dp', 'ep')), may hold values from -6 to 6
- key_rows: bfloat16 [2048, 4, 1024], P(('dp', 'ep')), may hold values from -6 to 6
- value_rows: bfloat16 [2048, 4, 2048], P(('dp', 'ep')), may hold values from -6 to 6
- gate_rows: bfloat16 [2048, 4, 2048], P(('dp', 'ep')), may hold values from -6 to 6
- beta_logit: bfloat16 [2048, 4, 16], P(('dp', 'ep')), may hold values from -6 to 6
- decay_logit: bfloat16 [2048, 4, 16], P(('dp', 'ep')), may hold values from -8 to 8
- residual: bfloat16 [2048, 4, 2048], P(('dp', 'ep')), may hold values from -6 to 6
- route_ids: int32 [2048, 4, 10], P(('dp', 'ep')), may hold values from 0 to 255, all different within a row; in each aligned block of 32 rows (0 to 31, 32 to 63, ..., all dimensions but the last counted through in order) at most 3 rows name the same one
- route_prob: float32 [2048, 4, 10], P(('dp', 'ep')), may hold values from 0.05 to 1
- out_weight: bfloat16 [2048, 2048], P(None, 'ep'), may hold values from -0.125 to 0.125
- core_gain: float32 [128], replicated, may hold values from 0.1 to 1.9
- moe_gain: float32 [2048], replicated, may hold values from 0.1 to 1.9
- gate_up: bfloat16 [256, 2048, 512], P(('dp', 'ep')), may hold values from -0.125 to 0.125
- down_weight: bfloat16 [256, 256, 2048], P(('dp', 'ep')), may hold values from -0.375 to 0.375
- new_home: int32 [2048], P(('dp', 'ep')), may hold values from 0 to 2047, as said below
Outputs:
- mixed_out: bfloat16 [2048, 4, 2048], P(('dp', 'ep'))
- moved_out: bfloat16 [2048, 16, 128, 128], P(('dp', 'ep'))
The draws below stay inside these ranges and needn't reach their ends.
Inputs may be any that keep to these rules, and one draw needn't show every extreme that they name: `route_ids`: each row names 10 different experts; among the 32 rows of one device (its requests, each with its 4 tokens) no expert is named more than 3 times, a bound that some block reaches. `new_home`: A permutation of the request positions; a request stays among the 8 devices of its dp index, and every device hands exactly 1 of its requests to each device of that group, itself included.
All inputs are finite; a program needn't handle non-finite values.
Results may differ from the reference program's by a relative error of at most 0.01.
Values may be sent and summed in bfloat16 or wider, within the bound.
A program may use at most 128 MiB of HBM per device.

```python
import math
import jax
import jax.numpy as jnp
import numpy as np
from jax import lax

D = 2048
VH = 16
HD = 128
FE = 256
TOP = 10
STEPS = 4
REQ_DEV = 8
KH = 8
REQS = 2048
EXPERTS = 256
CAP = 3
MIG_CAP = 1
N_DP = 32
N_EP = 8
DEVICES = 256


def draw_new_home(key, part):
    key_shift, key_place = jax.random.split(jax.random.fold_in(key, 7))
    shifts = jax.vmap(lambda subkey: jax.random.permutation(subkey, N_EP))(jax.random.split(key_shift, N_DP))
    places = jax.vmap(lambda subkey: jax.random.permutation(subkey, REQ_DEV))(jax.random.split(key_place, N_DP * N_EP))
    places = places.reshape(N_DP, N_EP, REQ_DEV)
    groups = jnp.arange(N_DP, dtype=jnp.int32)[:, None, None]
    source = jnp.arange(N_EP, dtype=jnp.int32)[None, :, None]
    request = jnp.arange(REQ_DEV, dtype=jnp.int32)[None, None, :]
    blocks = request // MIG_CAP
    offset = shifts[groups, blocks]
    target = (source + offset) % N_EP
    positions = places[groups, target, request]
    new_place = (groups * N_EP + target) * REQ_DEV + positions
    return new_place.reshape(-1).astype(jnp.int32)


def shard_levels(rng, extent, cuts, smallest, high):
    factor_of, own = 1.0, jax.random.fold_in(rng, 6)
    for dim, blocks in cuts:
        heights = jnp.exp(jax.random.uniform(jax.random.fold_in(own, dim), (blocks,), jnp.float32, smallest / len(cuts), high / len(cuts)))
        factor_of = factor_of * jnp.repeat(heights, extent[dim] // blocks).reshape([-1 if axis == dim else 1 for axis in range(len(extent))])
    return factor_of


def deal_out(key, own, number, rows, number_of, top, reach, lean):
    order = jax.random.permutation(key, number_of)
    crowded, ordinary = portions_of(number_of, rows * top, reach, lean, True), portions_of(number_of, rows * top, reach, lean, False)
    places = jnp.arange(number_of)

    def named(sizes, turn):
        used = int((sizes > 0).sum())
        fixed = max(1, used // 4)
        passed = fixed + (places - fixed + turn * (used - fixed)) % max(1, number_of - fixed)
        return jnp.zeros((number_of,), jnp.int32).at[order[jnp.where(places < fixed, places, passed)]].set(jnp.asarray(sizes, jnp.int32))

    sizes = jnp.where(number % 4 == 0, named(crowded, number // 4), named(ordinary, number - number // 4 - 1))
    mixed = jax.random.permutation(jax.random.fold_in(own, 3), number_of)
    donor, sink = mixed[0:number_of // 2 * 2:2], mixed[1:number_of // 2 * 2:2]
    margin = jnp.minimum(sizes[donor] - 1, reach - sizes[sink]) // 2
    margin = jnp.where((donor == order[0]) | (sink == order[0]) | (sizes[sink] == 0), 0, jnp.maximum(margin, 0))
    passed = jax.random.randint(jax.random.fold_in(own, 4), (number_of // 2,), 0, 1 << 20) % (margin + 1)
    sizes = sizes.at[donor].add(-passed).at[sink].add(passed)
    members = jnp.searchsorted(jnp.cumsum(sizes), jnp.arange(rows * top), side="right").astype(jnp.int32)
    table = members.reshape(top, rows).T
    table = table[jax.random.permutation(jax.random.fold_in(own, 1), rows)]
    turn = jax.random.randint(jax.random.fold_in(own, 2), (rows, 1), 0, top)
    return jnp.take_along_axis(table, (jnp.arange(top)[None, :] + turn) % top, axis=1)


def portions_of(amount, total, reach, skew, full):
    portions = [(1 << 20) // math.isqrt(standing ** skew) + 1 for standing in range(1, amount + 1)]
    largest = reach if full else min(reach, max(-(-total // amount), total * portions[0] // sum(portions)))
    least = 1 if total - largest >= amount - 1 else 0
    given, surplus = [largest] + [least] * (amount - 1), total - largest - least * (amount - 1)
    while surplus > 0:
        movable = [i for i in range(1, amount) if given[i] < largest] or [i for i in range(1, amount) if given[i] < reach]
        whole, left = sum([portions[i] for i in movable]), surplus
        for i in movable:
            extra = min(reach - given[i], max(1, left * portions[i] // whole), surplus)
            given[i] = given[i] + extra
            surplus = surplus - extra
    return np.array(given)


def bell_draw(own_key, extent, spread, bound, cuts=(), held_as=jnp.bfloat16):
    values = jax.random.normal(own_key, extent, jnp.float32) * spread
    if len(cuts) > 0:
        values = shard_levels(own_key, extent, cuts, -0.22, 0.18) * values
    return jnp.clip(values, min=-bound, max=bound).astype(held_as)


def setup_inputs(seed: int = 0) -> dict:
    key_of = jax.random.split(jax.random.key(seed), 17)
    states = bell_draw(key_of[0], (REQS, VH, HD, HD), 0.5, 4.0, ((0, 256),))
    query_rows = bell_draw(key_of[1], (REQS, STEPS, KH * HD), 1.0, 6.0, ((0, 256),))
    key_rows = bell_draw(key_of[2], (REQS, STEPS, KH * HD), 1.0, 6.0, ((0, 256),))
    value_rows = bell_draw(key_of[3], (REQS, STEPS, VH * HD), 1.0, 6.0, ((0, 256),))
    gate_rows = bell_draw(key_of[4], (REQS, STEPS, VH * HD), 1.0, 6.0, ((0, 256),))
    beta_logit = bell_draw(key_of[5], (REQS, STEPS, VH), 1.5, 6.0, ((0, 256),))
    decay_logit = bell_draw(key_of[6], (REQS, STEPS, VH), 2.0, 8.0, ((0, 256),))
    residual = bell_draw(key_of[7], (REQS, STEPS, D), 1.0, 6.0, ((0, 256),))
    route_ids_keys = jax.random.split(jax.random.fold_in(key_of[8], 1), REQS * STEPS // (REQ_DEV * STEPS))
    route_ids_turns = jax.random.permutation(jax.random.fold_in(key_of[8], 3), REQS * STEPS // (REQ_DEV * STEPS))
    route_ids = jax.vmap(lambda own, number: deal_out(jax.random.fold_in(key_of[8], 2), own, number, REQ_DEV * STEPS, EXPERTS, TOP, CAP, 2))(route_ids_keys, route_ids_turns).reshape((REQS, STEPS, TOP))
    route_prob = jnp.clip(jnp.exp(math.log(1.0) - 2.9957323 * jax.random.uniform(key_of[9], (REQS, STEPS, TOP), jnp.float32) ** shard_levels(key_of[9], (REQS, STEPS, TOP), ((0, 256),), -0.2, 0.2)), 0.05, 1.0)
    out_weight = bell_draw(key_of[10], (VH * HD, D), (VH * HD) ** -0.5, 0.125, ((1, 8),))
    core_gain = jnp.clip(1.0 + 0.18 * jax.random.normal(key_of[11], (HD,), jnp.float32), 0.1, 1.9)
    moe_gain = jnp.clip(1.0 + 0.18 * jax.random.normal(key_of[12], (D,), jnp.float32), 0.1, 1.9)
    gate_up = bell_draw(key_of[13], (EXPERTS, D, 2 * FE), D ** -0.5, 0.125, ((0, 256),))
    down_weight = bell_draw(key_of[14], (EXPERTS, FE, D), FE ** -0.5, 0.375, ((0, 256),))
    new_home = draw_new_home(jax.random.fold_in(key_of[16], 71), 0)
    return {"states": states, "query_rows": query_rows, "key_rows": key_rows, "value_rows": value_rows, "gate_rows": gate_rows, "beta_logit": beta_logit, "decay_logit": decay_logit, "residual": residual, "route_ids": route_ids, "route_prob": route_prob, "out_weight": out_weight, "core_gain": core_gain, "moe_gain": moe_gain, "gate_up": gate_up, "down_weight": down_weight, "new_home": new_home}


epsilon = 1e-06

def unit_rows(values):
    return values * lax.rsqrt(lax.optimization_barrier(jnp.sum(values * values, -1, keepdims=True)) + epsilon)

def delta_block(state_in, query_rows, key_rows, value_rows, gate_rows, beta_logit, decay_logit, core_gain):
    batch_size = state_in.shape[0]
    head_count = decay_logit.shape[-1]
    head_width = state_in.shape[-1]
    key_heads = query_rows.shape[-1] // head_width
    repeats = head_count // key_heads
    memory_state = state_in.astype(jnp.float32)
    outputs = []
    for position in range(query_rows.shape[1]):
        queries = unit_rows(query_rows[:, position].astype(jnp.float32).reshape(batch_size, key_heads, head_width))
        queries = jnp.repeat(queries, repeats, axis=1) * head_width ** (-0.5)
        key_units = unit_rows(key_rows[:, position].astype(jnp.float32).reshape(batch_size, key_heads, head_width))
        key_units = jnp.repeat(key_units, repeats, axis=1)
        values = value_rows[:, position].astype(jnp.float32).reshape(batch_size, head_count, head_width)
        decays = jax.nn.sigmoid(decay_logit[:, position].astype(jnp.float32))
        strength = jax.nn.sigmoid(beta_logit[:, position].astype(jnp.float32))
        memory_state = memory_state * decays[:, :, None, None]
        memory = jnp.einsum('bhkv,bhk->bhv', memory_state, key_units, precision=lax.Precision.HIGHEST)
        update = (values - memory) * strength[:, :, None]
        memory_state = memory_state + key_units[:, :, :, None] * update[:, :, None, :]
        reading = jnp.einsum('bhkv,bhk->bhv', memory_state, queries, precision=lax.Precision.HIGHEST)
        scaled = reading * lax.rsqrt(lax.optimization_barrier(jnp.mean(reading * reading, -1, keepdims=True)) + epsilon)
        gate_vals = gate_rows[:, position].astype(jnp.float32).reshape(batch_size, head_count, head_width)
        gated_out = scaled * core_gain * jax.nn.silu(gate_vals)
        outputs.append(gated_out.reshape(batch_size, head_count * head_width).astype(jnp.bfloat16))
    return (memory_state.astype(jnp.bfloat16), jnp.stack(outputs, axis=1))

def rms_scale(values, gain):
    return values * lax.rsqrt(lax.optimization_barrier(jnp.mean(values * values, -1, keepdims=True)) + epsilon) * gain

def expert_apply(chosen_rows, gate_up, down_weight):
    hidden_units = down_weight.shape[0]
    joined = jnp.dot(chosen_rows, gate_up, preferred_element_type=jnp.float32)
    active = (jax.nn.silu(joined[:, :hidden_units]) * joined[:, hidden_units:]).astype(jnp.bfloat16)
    return jnp.dot(active, down_weight, preferred_element_type=jnp.float32).astype(jnp.bfloat16)

def reference(states, query_rows, key_rows, value_rows, gate_rows, beta_logit, decay_logit, residual, route_ids, route_prob, out_weight, core_gain, moe_gain, gate_up, down_weight, new_home):

    def per_device(pieces):
        return delta_block(pieces[0], pieces[1], pieces[2], pieces[3], pieces[4], pieces[5], pieces[6], core_gain)
    shaped = tuple((array.reshape((DEVICES, REQ_DEV) + array.shape[1:]) for array in (states, query_rows, key_rows, value_rows, gate_rows, beta_logit, decay_logit)))
    fresh_states, core_out = lax.map(per_device, shaped)
    fresh_states = fresh_states.reshape(states.shape)
    core_out = core_out.reshape(REQS * STEPS, VH * HD)
    attention = jnp.dot(core_out, out_weight, preferred_element_type=jnp.float32).astype(jnp.bfloat16)
    hidden = (residual.reshape(REQS * STEPS, D).astype(jnp.float32) + attention.astype(jnp.float32)).astype(jnp.bfloat16)
    normed = rms_scale(hidden.astype(jnp.float32), moe_gain).astype(jnp.bfloat16)
    flat_ids = route_ids.reshape(-1).astype(jnp.int32)
    route_total = flat_ids.shape[0]
    sorted_routes = jnp.argsort(flat_ids, stable=True).astype(jnp.int32)
    counts = jnp.zeros((EXPERTS,), jnp.int32).at[flat_ids].add(1)
    starts = (jnp.cumsum(counts) - counts).astype(jnp.int32)
    most_rows = DEVICES * CAP
    padded_order = jnp.concatenate([sorted_routes, jnp.full((most_rows,), route_total, jnp.int32)])

    def expert_step(outputs, expert_index):
        picked = lax.dynamic_slice_in_dim(padded_order, starts[expert_index], most_rows)
        live_rows = jnp.arange(most_rows, dtype=jnp.int32) < counts[expert_index]
        picked = jnp.where(live_rows, picked, route_total).astype(jnp.int32)
        chosen_rows = normed[jnp.minimum(picked, route_total - 1) // TOP]
        result = expert_apply(chosen_rows, gate_up[expert_index], down_weight[expert_index])
        return (outputs.at[picked].set(result, mode='drop'), None)
    routed, _ = lax.scan(expert_step, jnp.zeros((route_total, D), jnp.bfloat16), jnp.arange(EXPERTS, dtype=jnp.int32))
    weights = route_prob.reshape(REQS * STEPS, TOP).astype(jnp.float32)
    weights = weights / lax.optimization_barrier(jnp.sum(weights, -1, keepdims=True))
    combined = lax.optimization_barrier(jnp.sum(routed.reshape(REQS * STEPS, TOP, D).astype(jnp.float32) * weights[:, :, None], axis=1))
    mixed_out = (hidden.astype(jnp.float32) + combined).astype(jnp.bfloat16).reshape(REQS, STEPS, D)
    moved_out = jnp.zeros_like(fresh_states).at[new_home].set(fresh_states)
    return (mixed_out, moved_out)
```

```python
import jax
import jax.numpy as jnp
from jax import lax
from jax.sharding import PartitionSpec as P

import functools
from jax.experimental import pallas as pl
from jax.experimental.pallas import tpu as pltpu

epsilon = 1e-06
f32 = jnp.float32
bf16 = jnp.bfloat16


def split2(x):
    hi = x.astype(bf16)
    lo = (x - hi.astype(f32)).astype(bf16)
    return hi, lo


def recur_kernel(s_ref, kq_ref, v_ref, g_ref, dec_ref, beta_ref, gain_ref, so_ref, co_ref, n_ref, r_ref, u_ref):
    heads = s_ref.shape[1]
    width = s_ref.shape[-1]
    steps = v_ref.shape[1]
    span = 2 * steps
    kq = kq_ref[0].astype(f32)
    kq = kq * lax.rsqrt(jnp.sum(kq * kq, -1, keepdims=True) + epsilon)
    row = lax.broadcasted_iota(jnp.int32, kq.shape, 0)
    kq = jnp.where(row % span >= steps, kq * width ** (-0.5), kq)
    n_ref[...] = kq
    for h in range(heads):
        p = n_ref[pl.ds(h * span, span), :]
        hi = p.astype(bf16).astype(f32)
        rest = p - hi
        mid = rest.astype(bf16).astype(f32)
        lo = rest - mid
        lhs = jnp.concatenate([hi, mid, lo], axis=0).astype(bf16)
        res = jnp.dot(lhs, s_ref[0, h], preferred_element_type=f32)
        r_ref[pl.ds(h * span, span), :] = (res[0:span] + res[span:2 * span]) + res[2 * span:3 * span]
    decay = jax.nn.sigmoid(dec_ref[0])
    strength = jax.nn.sigmoid(beta_ref[0])
    gain = gain_ref[...]
    keys = [n_ref[pl.ds(t, heads, stride=span), :] for t in range(steps)]
    queries = [n_ref[pl.ds(steps + t, heads, stride=span), :] for t in range(steps)]
    u_ref[...] = jnp.zeros(u_ref.shape, f32)
    updates = []
    carried = []
    total = None
    for t in range(steps):
        a_t = decay[:, t:t + 1]
        b_t = strength[:, t:t + 1]
        total = a_t if t == 0 else total * a_t
        carried = [c * a_t for c in carried]
        memory = total * r_ref[pl.ds(t, heads, stride=span), :]
        for j in range(t):
            kk = jnp.sum(keys[j] * keys[t], -1, keepdims=True)
            memory = memory + (carried[j] * kk) * updates[j]
        values = v_ref[0, t].astype(f32)
        update = (values - memory) * b_t
        updates.append(update)
        carried.append(jnp.ones_like(a_t))
        reading = total * r_ref[pl.ds(steps + t, heads, stride=span), :]
        for j in range(t + 1):
            qk = jnp.sum(keys[j] * queries[t], -1, keepdims=True)
            coef = qk if j == t else carried[j] * qk
            reading = reading + coef * updates[j]
        scaled = reading * lax.rsqrt(jnp.mean(reading * reading, -1, keepdims=True) + epsilon)
        gate_vals = g_ref[0, t].astype(f32)
        co_ref[0, t] = (scaled * gain * (gate_vals * jax.nn.sigmoid(gate_vals))).astype(co_ref.dtype)
    for j in range(steps):
        u_ref[pl.ds(j, heads, stride=span), :] = carried[j] * updates[j]
    for h in range(heads):
        kt = n_ref[pl.ds(h * span, span), :].T
        w = u_ref[pl.ds(h * span, span), :]
        k_hi, k_lo = split2(kt)
        w_hi, w_lo = split2(w)
        delta = (
            jnp.dot(k_hi, w_hi, preferred_element_type=f32)
            + jnp.dot(k_hi, w_lo, preferred_element_type=f32)
            + jnp.dot(k_lo, w_hi, preferred_element_type=f32)
        )
        so_ref[0, h] = (total[h:h + 1, :] * s_ref[0, h].astype(f32) + delta).astype(so_ref.dtype)


def recurrence(states, query_rows, key_rows, value_rows, gate_rows, beta_logit, decay_logit, core_gain):
    batch, heads, width, _ = states.shape
    steps = query_rows.shape[1]
    key_heads = query_rows.shape[-1] // width
    repeats = heads // key_heads
    span = 2 * steps
    kq = jnp.concatenate(
        [key_rows.reshape(batch, steps, key_heads, width), query_rows.reshape(batch, steps, key_heads, width)], axis=1
    )
    kq = jnp.repeat(kq.transpose(0, 2, 1, 3), repeats, axis=1).reshape(batch, heads * span, width)
    values = value_rows.reshape(batch, steps, heads, width)
    gates = gate_rows.reshape(batch, steps, heads, width)
    decay = decay_logit.astype(f32).transpose(0, 2, 1)
    beta = beta_logit.astype(f32).transpose(0, 2, 1)
    gain = core_gain.reshape(1, width)
    state_spec = pl.BlockSpec((1, heads, width, width), lambda i: (i, 0, 0, 0))
    row_spec = pl.BlockSpec((1, steps, heads, width), lambda i: (i, 0, 0, 0))
    coef_spec = pl.BlockSpec((1, heads, steps), lambda i: (i, 0, 0))
    fresh, core = pl.pallas_call(
        recur_kernel,
        grid=(batch,),
        in_specs=[
            state_spec,
            pl.BlockSpec((1, heads * span, width), lambda i: (i, 0, 0)),
            row_spec,
            row_spec,
            coef_spec,
            coef_spec,
            pl.BlockSpec((1, width), lambda i: (0, 0)),
        ],
        out_specs=[state_spec, row_spec],
        out_shape=[
            jax.ShapeDtypeStruct(states.shape, bf16),
            jax.ShapeDtypeStruct((batch, steps, heads, width), bf16),
        ],
        scratch_shapes=[pltpu.VMEM((heads * span, width), f32)] * 3,
    )(states, kq, values, gates, decay, beta, gain)
    return fresh, core.reshape(batch, steps, heads * width)


def unit_rows(values):
    return values * lax.rsqrt(jnp.sum(values * values, -1, keepdims=True) + epsilon)


def delta_block(
    state_in, query_rows, key_rows, value_rows, gate_rows, beta_logit, decay_logit, core_gain
):
    batch_size = state_in.shape[0]
    head_count = decay_logit.shape[-1]
    head_width = state_in.shape[-1]
    key_heads = query_rows.shape[-1] // head_width
    repeats = head_count // key_heads
    memory_state = state_in.astype(jnp.float32)
    outputs = []
    for position in range(query_rows.shape[1]):
        queries = unit_rows(
            query_rows[:, position].astype(jnp.float32).reshape(batch_size, key_heads, head_width)
        )
        queries = jnp.repeat(queries, repeats, axis=1) * head_width ** (-0.5)
        key_units = unit_rows(
            key_rows[:, position].astype(jnp.float32).reshape(batch_size, key_heads, head_width)
        )
        key_units = jnp.repeat(key_units, repeats, axis=1)
        values = (
            value_rows[:, position].astype(jnp.float32).reshape(batch_size, head_count, head_width)
        )
        decays = jax.nn.sigmoid(decay_logit[:, position].astype(jnp.float32))
        strength = jax.nn.sigmoid(beta_logit[:, position].astype(jnp.float32))
        memory_state = memory_state * decays[:, :, None, None]
        memory = jnp.einsum(
            "bhkv,bhk->bhv", memory_state, key_units, precision=lax.Precision.HIGHEST
        )
        update = (values - memory) * strength[:, :, None]
        memory_state = memory_state + key_units[:, :, :, None] * update[:, :, None, :]
        reading = jnp.einsum(
            "bhkv,bhk->bhv", memory_state, queries, precision=lax.Precision.HIGHEST
        )
        scaled = reading * lax.rsqrt(jnp.mean(reading * reading, -1, keepdims=True) + epsilon)
        gate_vals = (
            gate_rows[:, position].astype(jnp.float32).reshape(batch_size, head_count, head_width)
        )
        gated_out = scaled * core_gain * jax.nn.silu(gate_vals)
        outputs.append(gated_out.reshape(batch_size, head_count * head_width).astype(jnp.bfloat16))
    return (memory_state.astype(jnp.bfloat16), jnp.stack(outputs, axis=1))


def rms_scale(values, gain):
    return values * lax.rsqrt(jnp.mean(values * values, -1, keepdims=True) + epsilon) * gain


def expert_apply(chosen_rows, gate_up, down_weight):
    hidden_units = down_weight.shape[0]
    joined = jnp.dot(chosen_rows, gate_up, preferred_element_type=jnp.float32)
    active = (jax.nn.silu(joined[:, :hidden_units]) * joined[:, hidden_units:]).astype(jnp.bfloat16)
    return jnp.dot(active, down_weight, preferred_element_type=jnp.float32).astype(jnp.bfloat16)


def pack(values, positions, lane_count):
    zeroed = jnp.zeros(values.shape, values.dtype)
    placed = zeroed.at[positions].set(values)
    return placed.reshape((lane_count, values.shape[0] // lane_count) + values.shape[1:])


def unpack(values):
    return values.reshape((values.shape[0] * values.shape[1],) + values.shape[2:])


def shards(
    states,
    query_rows,
    key_rows,
    value_rows,
    gate_rows,
    beta_logit,
    decay_logit,
    residual,
    route_ids,
    route_prob,
    out_weight,
    core_gain,
    moe_gain,
    gate_up,
    down_weight,
    new_home,
):
    req_count = states.shape[0]
    step_count = query_rows.shape[1]
    model_width = residual.shape[-1]
    ep_size = lax.axis_size("ep")
    dp_size = lax.axis_size("dp")
    target = new_home // req_count % ep_size
    new_place = new_home % req_count
    order_ids = jnp.arange(req_count, dtype=jnp.int32)
    earlier = (target[:, None] == target[None, :]) & (order_ids[None, :] < order_ids[:, None])
    lane_rank = jnp.sum(earlier.astype(jnp.int32), axis=1)
    lane_cap = req_count // ep_size
    buffer_index = target * lane_cap + lane_rank
    fresh_states, core_out = recurrence(
        states, query_rows, key_rows, value_rows, gate_rows, beta_logit, decay_logit, core_gain
    )
    received = (
        lax.all_to_all(
            pack(fresh_states, buffer_index, ep_size), "ep", split_axis=0, concat_axis=0, tiled=True
        ),
        lax.all_to_all(
            pack(new_place, buffer_index, ep_size), "ep", split_axis=0, concat_axis=0, tiled=True
        ),
    )
    moved_out = jnp.zeros_like(states).at[unpack(received[1])].set(unpack(received[0]), mode="drop")
    token_count = req_count * step_count
    core_flat = core_out.reshape(token_count, core_out.shape[-1])
    columns = jnp.dot(
        lax.all_gather(core_flat, "ep", axis=0, tiled=True),
        out_weight,
        preferred_element_type=jnp.float32,
    ).astype(jnp.bfloat16)
    attention = lax.all_to_all(columns, "ep", split_axis=0, concat_axis=1, tiled=True)
    hidden = (
        residual.reshape(token_count, model_width).astype(jnp.float32)
        + attention.astype(jnp.float32)
    ).astype(jnp.bfloat16)
    normed = rms_scale(hidden.astype(jnp.float32), moe_gain).astype(jnp.bfloat16)
    top_count = route_ids.shape[-1]
    experts = dp_size * ep_size
    capacity = (token_count * top_count + experts - 1) // experts + 1
    flat_ids = route_ids.reshape(-1)
    onehot = (flat_ids[:, None] == jnp.arange(experts, dtype=jnp.int32)[None, :]).astype(jnp.int32)
    route_rank = jnp.sum(jnp.cumsum(onehot, axis=0) * onehot, axis=1) - 1
    slot_index = flat_ids * capacity + route_rank
    outgoing = (
        jnp.zeros((experts * capacity, model_width), jnp.bfloat16)
        .at[slot_index]
        .set(jnp.repeat(normed, top_count, axis=0))
    )
    arrived = lax.all_to_all(
        lax.all_to_all(
            outgoing.reshape(dp_size, ep_size, capacity, model_width),
            "dp",
            split_axis=0,
            concat_axis=0,
            tiled=True,
        ),
        "ep",
        split_axis=1,
        concat_axis=1,
        tiled=True,
    )
    result = expert_apply(arrived.reshape(-1, model_width), gate_up[0], down_weight[0]).reshape(
        dp_size, ep_size, capacity, model_width
    )
    returned = lax.all_to_all(
        lax.all_to_all(result, "dp", split_axis=0, concat_axis=0, tiled=True),
        "ep",
        split_axis=1,
        concat_axis=1,
        tiled=True,
    )
    routed = returned.reshape(experts * capacity, model_width)[slot_index]
    weights = route_prob.reshape(token_count, top_count)
    weights = weights / jnp.sum(weights, -1, keepdims=True)
    combined = jnp.sum(
        routed.reshape(token_count, top_count, model_width).astype(jnp.float32)
        * weights[:, :, None],
        axis=1,
    )
    mixed_out = (
        (hidden.astype(jnp.float32) + combined)
        .astype(jnp.bfloat16)
        .reshape(req_count, step_count, model_width)
    )
    return (mixed_out, moved_out)


def solution(mesh):
    placed = (
        P(("dp", "ep"), None, None, None),
        P(("dp", "ep"), None, None),
        P(("dp", "ep"), None, None),
        P(("dp", "ep"), None, None),
        P(("dp", "ep"), None, None),
        P(("dp", "ep"), None, None),
        P(("dp", "ep"), None, None),
        P(("dp", "ep"), None, None),
        P(("dp", "ep"), None, None),
        P(("dp", "ep"), None, None),
        P(None, "ep"),
        P(),
        P(),
        P(("dp", "ep"), None, None),
        P(("dp", "ep"), None, None),
        P(("dp", "ep")),
    )
    return jax.shard_map(
        shards,
        mesh=mesh,
        in_specs=placed,
        out_specs=(P(("dp", "ep"), None, None), P(("dp", "ep"), None, None, None)),
        check_vma=False,
    )
```

```python
import jax
import jax.numpy as jnp
from jax import lax
from jax.sharding import PartitionSpec as P

import functools
from jax.experimental import pallas as pl
from jax.experimental.pallas import tpu as pltpu

epsilon = 1e-06
f32 = jnp.float32
bf16 = jnp.bfloat16


def split2(x):
    hi = x.astype(bf16)
    lo = (x - hi.astype(f32)).astype(bf16)
    return hi, lo


def recur_kernel(s_ref, kq_ref, v_ref, g_ref, dec_ref, beta_ref, gain_ref, so_ref, co_ref, n_ref, r_ref, u_ref):
    heads = s_ref.shape[1]
    width = s_ref.shape[-1]
    steps = v_ref.shape[1]
    span = 2 * steps
    kq = kq_ref[0].astype(f32)
    kq = kq * lax.rsqrt(jnp.sum(kq * kq, -1, keepdims=True) + epsilon)
    row = lax.broadcasted_iota(jnp.int32, kq.shape, 0)
    kq = jnp.where(row % span >= steps, kq * width ** (-0.5), kq)
    n_ref[...] = kq
    for h in range(heads):
        p = n_ref[pl.ds(h * span, span), :]
        hi = p.astype(bf16).astype(f32)
        rest = p - hi
        mid = rest.astype(bf16).astype(f32)
        lo = rest - mid
        lhs = jnp.concatenate([hi, mid, lo], axis=0).astype(bf16)
        res = jnp.dot(lhs, s_ref[0, h], preferred_element_type=f32)
        r_ref[pl.ds(h * span, span), :] = (res[0:span] + res[span:2 * span]) + res[2 * span:3 * span]
    decay = jax.nn.sigmoid(dec_ref[0])
    strength = jax.nn.sigmoid(beta_ref[0])
    gain = gain_ref[...]
    keys = [n_ref[pl.ds(t, heads, stride=span), :] for t in range(steps)]
    queries = [n_ref[pl.ds(steps + t, heads, stride=span), :] for t in range(steps)]
    u_ref[...] = jnp.zeros(u_ref.shape, f32)
    updates = []
    carried = []
    total = None
    for t in range(steps):
        a_t = decay[:, t:t + 1]
        b_t = strength[:, t:t + 1]
        total = a_t if t == 0 else total * a_t
        carried = [c * a_t for c in carried]
        memory = total * r_ref[pl.ds(t, heads, stride=span), :]
        for j in range(t):
            kk = jnp.sum(keys[j] * keys[t], -1, keepdims=True)
            memory = memory + (carried[j] * kk) * updates[j]
        values = v_ref[0, t].astype(f32)
        update = (values - memory) * b_t
        updates.append(update)
        carried.append(jnp.ones_like(a_t))
        reading = total * r_ref[pl.ds(steps + t, heads, stride=span), :]
        for j in range(t + 1):
            qk = jnp.sum(keys[j] * queries[t], -1, keepdims=True)
            coef = qk if j == t else carried[j] * qk
            reading = reading + coef * updates[j]
        scaled = reading * lax.rsqrt(jnp.mean(reading * reading, -1, keepdims=True) + epsilon)
        gate_vals = g_ref[0, t].astype(f32)
        co_ref[0, t] = (scaled * gain * (gate_vals * jax.nn.sigmoid(gate_vals))).astype(co_ref.dtype)
    for j in range(steps):
        u_ref[pl.ds(j, heads, stride=span), :] = carried[j] * updates[j]
    for h in range(heads):
        kt = n_ref[pl.ds(h * span, span), :].T
        w = u_ref[pl.ds(h * span, span), :]
        k_hi, k_lo = split2(kt)
        w_hi, w_lo = split2(w)
        delta = (
            jnp.dot(k_hi, w_hi, preferred_element_type=f32)
            + jnp.dot(k_hi, w_lo, preferred_element_type=f32)
            + jnp.dot(k_lo, w_hi, preferred_element_type=f32)
        )
        so_ref[0, h] = (total[h:h + 1, :] * s_ref[0, h].astype(f32) + delta).astype(so_ref.dtype)


def recurrence(states, query_rows, key_rows, value_rows, gate_rows, beta_logit, decay_logit, core_gain):
    batch, heads, width, _ = states.shape
    steps = query_rows.shape[1]
    key_heads = query_rows.shape[-1] // width
    repeats = heads // key_heads
    span = 2 * steps
    kq = jnp.concatenate(
        [key_rows.reshape(batch, steps, key_heads, width), query_rows.reshape(batch, steps, key_heads, width)], axis=1
    )
    kq = jnp.repeat(kq.transpose(0, 2, 1, 3), repeats, axis=1).reshape(batch, heads * span, width)
    values = value_rows.reshape(batch, steps, heads, width)
    gates = gate_rows.reshape(batch, steps, heads, width)
    decay = decay_logit.astype(f32).transpose(0, 2, 1)
    beta = beta_logit.astype(f32).transpose(0, 2, 1)
    gain = core_gain.reshape(1, width)
    state_spec = pl.BlockSpec((1, heads, width, width), lambda i: (i, 0, 0, 0))
    row_spec = pl.BlockSpec((1, steps, heads, width), lambda i: (i, 0, 0, 0))
    coef_spec = pl.BlockSpec((1, heads, steps), lambda i: (i, 0, 0))
    fresh, core = pl.pallas_call(
        recur_kernel,
        grid=(batch,),
        in_specs=[
            state_spec,
            pl.BlockSpec((1, heads * span, width), lambda i: (i, 0, 0)),
            row_spec,
            row_spec,
            coef_spec,
            coef_spec,
            pl.BlockSpec((1, width), lambda i: (0, 0)),
        ],
        out_specs=[state_spec, row_spec],
        out_shape=[
            jax.ShapeDtypeStruct(states.shape, bf16),
            jax.ShapeDtypeStruct((batch, steps, heads, width), bf16),
        ],
        scratch_shapes=[pltpu.VMEM((heads * span, width), f32)] * 3,
    )(states, kq, values, gates, decay, beta, gain)
    return fresh, core.reshape(batch, steps, heads * width)


def unit_rows(values):
    return values * lax.rsqrt(jnp.sum(values * values, -1, keepdims=True) + epsilon)


def delta_block(
    state_in, query_rows, key_rows, value_rows, gate_rows, beta_logit, decay_logit, core_gain
):
    batch_size = state_in.shape[0]
    head_count = decay_logit.shape[-1]
    head_width = state_in.shape[-1]
    key_heads = query_rows.shape[-1] // head_width
    repeats = head_count // key_heads
    memory_state = state_in.astype(jnp.float32)
    outputs = []
    for position in range(query_rows.shape[1]):
        queries = unit_rows(
            query_rows[:, position].astype(jnp.float32).reshape(batch_size, key_heads, head_width)
        )
        queries = jnp.repeat(queries, repeats, axis=1) * head_width ** (-0.5)
        key_units = unit_rows(
            key_rows[:, position].astype(jnp.float32).reshape(batch_size, key_heads, head_width)
        )
        key_units = jnp.repeat(key_units, repeats, axis=1)
        values = (
            value_rows[:, position].astype(jnp.float32).reshape(batch_size, head_count, head_width)
        )
        decays = jax.nn.sigmoid(decay_logit[:, position].astype(jnp.float32))
        strength = jax.nn.sigmoid(beta_logit[:, position].astype(jnp.float32))
        memory_state = memory_state * decays[:, :, None, None]
        memory = jnp.einsum(
            "bhkv,bhk->bhv", memory_state, key_units, precision=lax.Precision.HIGHEST
        )
        update = (values - memory) * strength[:, :, None]
        memory_state = memory_state + key_units[:, :, :, None] * update[:, :, None, :]
        reading = jnp.einsum(
            "bhkv,bhk->bhv", memory_state, queries, precision=lax.Precision.HIGHEST
        )
        scaled = reading * lax.rsqrt(jnp.mean(reading * reading, -1, keepdims=True) + epsilon)
        gate_vals = (
            gate_rows[:, position].astype(jnp.float32).reshape(batch_size, head_count, head_width)
        )
        gated_out = scaled * core_gain * jax.nn.silu(gate_vals)
        outputs.append(gated_out.reshape(batch_size, head_count * head_width).astype(jnp.bfloat16))
    return (memory_state.astype(jnp.bfloat16), jnp.stack(outputs, axis=1))


def rms_scale(values, gain):
    return values * lax.rsqrt(jnp.mean(values * values, -1, keepdims=True) + epsilon) * gain


def expert_apply(chosen_rows, gate_up, down_weight):
    hidden_units = down_weight.shape[0]
    joined = jnp.dot(chosen_rows, gate_up, preferred_element_type=jnp.float32)
    active = (jax.nn.silu(joined[:, :hidden_units]) * joined[:, hidden_units:]).astype(jnp.bfloat16)
    return jnp.dot(active, down_weight, preferred_element_type=jnp.float32).astype(jnp.bfloat16)


def pack(values, positions, lane_count):
    zeroed = jnp.zeros(values.shape, values.dtype)
    placed = zeroed.at[positions].set(values)
    return placed.reshape((lane_count, values.shape[0] // lane_count) + values.shape[1:])


def unpack(values):
    return values.reshape((values.shape[0] * values.shape[1],) + values.shape[2:])


def shards(
    states,
    query_rows,
    key_rows,
    value_rows,
    gate_rows,
    beta_logit,
    decay_logit,
    residual,
    route_ids,
    route_prob,
    out_weight,
    core_gain,
    moe_gain,
    gate_up,
    down_weight,
    new_home,
):
    req_count = states.shape[0]
    step_count = query_rows.shape[1]
    model_width = residual.shape[-1]
    ep_size = lax.axis_size("ep")
    dp_size = lax.axis_size("dp")
    target = new_home // req_count % ep_size
    new_place = new_home % req_count
    order_ids = jnp.arange(req_count, dtype=jnp.int32)
    earlier = (target[:, None] == target[None, :]) & (order_ids[None, :] < order_ids[:, None])
    lane_rank = jnp.sum(earlier.astype(jnp.int32), axis=1)
    lane_cap = req_count // ep_size
    buffer_index = target * lane_cap + lane_rank
    fresh_states, core_out = recurrence(
        states, query_rows, key_rows, value_rows, gate_rows, beta_logit, decay_logit, core_gain
    )
    received = (
        lax.all_to_all(
            pack(fresh_states, buffer_index, ep_size), "ep", split_axis=0, concat_axis=0, tiled=True
        ),
        lax.all_to_all(
            pack(new_place, buffer_index, ep_size), "ep", split_axis=0, concat_axis=0, tiled=True
        ),
    )
    moved_out = jnp.zeros_like(states).at[unpack(received[1])].set(unpack(received[0]), mode="drop")
    token_count = req_count * step_count
    core_flat = core_out.reshape(token_count, core_out.shape[-1])
    columns = jnp.dot(
        lax.all_gather(core_flat, "ep", axis=0, tiled=True),
        out_weight,
        preferred_element_type=jnp.float32,
    ).astype(jnp.bfloat16)
    attention = lax.all_to_all(columns, "ep", split_axis=0, concat_axis=1, tiled=True)
    hidden = (
        residual.reshape(token_count, model_width).astype(jnp.float32)
        + attention.astype(jnp.float32)
    ).astype(jnp.bfloat16)
    normed = rms_scale(hidden.astype(jnp.float32), moe_gain).astype(jnp.bfloat16)
    top_count = route_ids.shape[-1]
    experts = dp_size * ep_size
    capacity = (token_count * top_count + experts - 1) // experts + 1
    flat_ids = route_ids.reshape(-1)
    onehot = (flat_ids[:, None] == jnp.arange(experts, dtype=jnp.int32)[None, :]).astype(jnp.int32)
    route_rank = jnp.sum(jnp.cumsum(onehot, axis=0) * onehot, axis=1) - 1
    slot_index = flat_ids * capacity + route_rank
    outgoing = (
        jnp.zeros((experts * capacity, model_width), jnp.bfloat16)
        .at[slot_index]
        .set(jnp.repeat(normed, top_count, axis=0))
    )
    arrived = lax.all_to_all(outgoing, ("dp", "ep"), 0, 0, tiled=True)
    result = expert_apply(arrived, gate_up[0], down_weight[0])
    returned = lax.all_to_all(result, ("dp", "ep"), 0, 0, tiled=True)
    routed = returned.reshape(experts * capacity, model_width)[slot_index]
    weights = route_prob.reshape(token_count, top_count)
    weights = weights / jnp.sum(weights, -1, keepdims=True)
    combined = jnp.sum(
        routed.reshape(token_count, top_count, model_width).astype(jnp.float32)
        * weights[:, :, None],
        axis=1,
    )
    mixed_out = (
        (hidden.astype(jnp.float32) + combined)
        .astype(jnp.bfloat16)
        .reshape(req_count, step_count, model_width)
    )
    return (mixed_out, moved_out)


def solution(mesh):
    placed = (
        P(("dp", "ep"), None, None, None),
        P(("dp", "ep"), None, None),
        P(("dp", "ep"), None, None),
        P(("dp", "ep"), None, None),
        P(("dp", "ep"), None, None),
        P(("dp", "ep"), None, None),
        P(("dp", "ep"), None, None),
        P(("dp", "ep"), None, None),
        P(("dp", "ep"), None, None),
        P(("dp", "ep"), None, None),
        P(None, "ep"),
        P(),
        P(),
        P(("dp", "ep"), None, None),
        P(("dp", "ep"), None, None),
        P(("dp", "ep")),
    )
    return jax.shard_map(
        shards,
        mesh=mesh,
        in_specs=placed,
        out_specs=(P(("dp", "ep"), None, None), P(("dp", "ep"), None, None, None)),
        check_vma=False,
    )
```

```python
import jax
import jax.numpy as jnp
from jax import lax
from jax.sharding import PartitionSpec as P

import functools
from jax.experimental import pallas as pl
from jax.experimental.pallas import tpu as pltpu

epsilon = 1e-06
f32 = jnp.float32
bf16 = jnp.bfloat16


def split2(x):
    hi = x.astype(bf16)
    lo = (x - hi.astype(f32)).astype(bf16)
    return hi, lo


def recur_kernel(slot_ref, s_ref, kq_ref, v_ref, g_ref, dec_ref, beta_ref, gain_ref, so_ref, co_ref, n_ref, r_ref, u_ref):
    heads = s_ref.shape[1]
    width = s_ref.shape[-1]
    steps = v_ref.shape[1]
    span = 2 * steps
    kq = kq_ref[0].astype(f32)
    kq = kq * lax.rsqrt(jnp.sum(kq * kq, -1, keepdims=True) + epsilon)
    row = lax.broadcasted_iota(jnp.int32, kq.shape, 0)
    kq = jnp.where(row % span >= steps, kq * width ** (-0.5), kq)
    n_ref[...] = kq
    for h in range(heads):
        p = n_ref[pl.ds(h * span, span), :]
        hi = p.astype(bf16).astype(f32)
        rest = p - hi
        mid = rest.astype(bf16).astype(f32)
        lo = rest - mid
        lhs = jnp.concatenate([hi, mid, lo], axis=0).astype(bf16)
        res = jnp.dot(lhs, s_ref[0, h], preferred_element_type=f32)
        r_ref[pl.ds(h * span, span), :] = (res[0:span] + res[span:2 * span]) + res[2 * span:3 * span]
    decay = jax.nn.sigmoid(dec_ref[0])
    strength = jax.nn.sigmoid(beta_ref[0])
    gain = gain_ref[...]
    keys = [n_ref[pl.ds(t, heads, stride=span), :] for t in range(steps)]
    queries = [n_ref[pl.ds(steps + t, heads, stride=span), :] for t in range(steps)]
    u_ref[...] = jnp.zeros(u_ref.shape, f32)
    updates = []
    carried = []
    total = None
    for t in range(steps):
        a_t = decay[:, t:t + 1]
        b_t = strength[:, t:t + 1]
        total = a_t if t == 0 else total * a_t
        carried = [c * a_t for c in carried]
        memory = total * r_ref[pl.ds(t, heads, stride=span), :]
        for j in range(t):
            kk = jnp.sum(keys[j] * keys[t], -1, keepdims=True)
            memory = memory + (carried[j] * kk) * updates[j]
        values = v_ref[0, t].astype(f32)
        update = (values - memory) * b_t
        updates.append(update)
        carried.append(jnp.ones_like(a_t))
        reading = total * r_ref[pl.ds(steps + t, heads, stride=span), :]
        for j in range(t + 1):
            qk = jnp.sum(keys[j] * queries[t], -1, keepdims=True)
            coef = qk if j == t else carried[j] * qk
            reading = reading + coef * updates[j]
        scaled = reading * lax.rsqrt(jnp.mean(reading * reading, -1, keepdims=True) + epsilon)
        gate_vals = g_ref[0, t].astype(f32)
        co_ref[0, t] = (scaled * gain * (gate_vals * jax.nn.sigmoid(gate_vals))).astype(co_ref.dtype)
    for j in range(steps):
        u_ref[pl.ds(j, heads, stride=span), :] = carried[j] * updates[j]
    for h in range(heads):
        kt = n_ref[pl.ds(h * span, span), :].T
        w = u_ref[pl.ds(h * span, span), :]
        k_hi, k_lo = split2(kt)
        w_hi, w_lo = split2(w)
        delta = (
            jnp.dot(k_hi, w_hi, preferred_element_type=f32)
            + jnp.dot(k_hi, w_lo, preferred_element_type=f32)
            + jnp.dot(k_lo, w_hi, preferred_element_type=f32)
        )
        so_ref[0, h] = (total[h:h + 1, :] * s_ref[0, h].astype(f32) + delta).astype(so_ref.dtype)


def recurrence(slots, states, query_rows, key_rows, value_rows, gate_rows, beta_logit, decay_logit, core_gain):
    batch, heads, width, _ = states.shape
    steps = query_rows.shape[1]
    key_heads = query_rows.shape[-1] // width
    repeats = heads // key_heads
    span = 2 * steps
    kq = jnp.concatenate(
        [key_rows.reshape(batch, steps, key_heads, width), query_rows.reshape(batch, steps, key_heads, width)], axis=1
    )
    kq = jnp.repeat(kq.transpose(0, 2, 1, 3), repeats, axis=1).reshape(batch, heads * span, width)
    values = value_rows.reshape(batch, steps, heads, width)
    gates = gate_rows.reshape(batch, steps, heads, width)
    decay = decay_logit.astype(f32).transpose(0, 2, 1)
    beta = beta_logit.astype(f32).transpose(0, 2, 1)
    gain = core_gain.reshape(1, width)
    state_in = pl.BlockSpec((1, heads, width, width), lambda i, slot: (i, 0, 0, 0))
    state_out = pl.BlockSpec((1, heads, width, width), lambda i, slot: (slot[i], 0, 0, 0))
    row_spec = pl.BlockSpec((1, steps, heads, width), lambda i, slot: (i, 0, 0, 0))
    coef_spec = pl.BlockSpec((1, heads, steps), lambda i, slot: (i, 0, 0))
    fresh, core = pl.pallas_call(
        recur_kernel,
        grid_spec=pltpu.PrefetchScalarGridSpec(
            num_scalar_prefetch=1,
            grid=(batch,),
            in_specs=[
                state_in,
                pl.BlockSpec((1, heads * span, width), lambda i, slot: (i, 0, 0)),
                row_spec,
                row_spec,
                coef_spec,
                coef_spec,
                pl.BlockSpec((1, width), lambda i, slot: (0, 0)),
            ],
            out_specs=[state_out, row_spec],
            scratch_shapes=[pltpu.VMEM((heads * span, width), f32)] * 3,
        ),
        out_shape=[
            jax.ShapeDtypeStruct(states.shape, bf16),
            jax.ShapeDtypeStruct((batch, steps, heads, width), bf16),
        ],
    )(slots, states, kq, values, gates, decay, beta, gain)
    return fresh, core.reshape(batch, steps, heads * width)


def unit_rows(values):
    return values * lax.rsqrt(jnp.sum(values * values, -1, keepdims=True) + epsilon)


def delta_block(
    state_in, query_rows, key_rows, value_rows, gate_rows, beta_logit, decay_logit, core_gain
):
    batch_size = state_in.shape[0]
    head_count = decay_logit.shape[-1]
    head_width = state_in.shape[-1]
    key_heads = query_rows.shape[-1] // head_width
    repeats = head_count // key_heads
    memory_state = state_in.astype(jnp.float32)
    outputs = []
    for position in range(query_rows.shape[1]):
        queries = unit_rows(
            query_rows[:, position].astype(jnp.float32).reshape(batch_size, key_heads, head_width)
        )
        queries = jnp.repeat(queries, repeats, axis=1) * head_width ** (-0.5)
        key_units = unit_rows(
            key_rows[:, position].astype(jnp.float32).reshape(batch_size, key_heads, head_width)
        )
        key_units = jnp.repeat(key_units, repeats, axis=1)
        values = (
            value_rows[:, position].astype(jnp.float32).reshape(batch_size, head_count, head_width)
        )
        decays = jax.nn.sigmoid(decay_logit[:, position].astype(jnp.float32))
        strength = jax.nn.sigmoid(beta_logit[:, position].astype(jnp.float32))
        memory_state = memory_state * decays[:, :, None, None]
        memory = jnp.einsum(
            "bhkv,bhk->bhv", memory_state, key_units, precision=lax.Precision.HIGHEST
        )
        update = (values - memory) * strength[:, :, None]
        memory_state = memory_state + key_units[:, :, :, None] * update[:, :, None, :]
        reading = jnp.einsum(
            "bhkv,bhk->bhv", memory_state, queries, precision=lax.Precision.HIGHEST
        )
        scaled = reading * lax.rsqrt(jnp.mean(reading * reading, -1, keepdims=True) + epsilon)
        gate_vals = (
            gate_rows[:, position].astype(jnp.float32).reshape(batch_size, head_count, head_width)
        )
        gated_out = scaled * core_gain * jax.nn.silu(gate_vals)
        outputs.append(gated_out.reshape(batch_size, head_count * head_width).astype(jnp.bfloat16))
    return (memory_state.astype(jnp.bfloat16), jnp.stack(outputs, axis=1))


def place_kernel(place_ref, in_ref, out_ref):
    out_ref[...] = in_ref[...]


def place_rows(rows, places):
    block = (1,) + rows.shape[1:]
    tail = (0,) * (rows.ndim - 1)
    return pl.pallas_call(
        place_kernel,
        grid_spec=pltpu.PrefetchScalarGridSpec(
            num_scalar_prefetch=1,
            grid=(rows.shape[0],),
            in_specs=[pl.BlockSpec(block, lambda j, place: (j,) + tail)],
            out_specs=pl.BlockSpec(block, lambda j, place: (place[j],) + tail),
        ),
        out_shape=jax.ShapeDtypeStruct(rows.shape, rows.dtype),
    )(places, rows)


def rms_scale(values, gain):
    return values * lax.rsqrt(jnp.mean(values * values, -1, keepdims=True) + epsilon) * gain


def expert_apply(chosen_rows, gate_up, down_weight):
    hidden_units = down_weight.shape[0]
    joined = jnp.dot(chosen_rows, gate_up, preferred_element_type=jnp.float32)
    active = (jax.nn.silu(joined[:, :hidden_units]) * joined[:, hidden_units:]).astype(jnp.bfloat16)
    return jnp.dot(active, down_weight, preferred_element_type=jnp.float32).astype(jnp.bfloat16)


def pack(values, positions, lane_count):
    zeroed = jnp.zeros(values.shape, values.dtype)
    placed = zeroed.at[positions].set(values)
    return placed.reshape((lane_count, values.shape[0] // lane_count) + values.shape[1:])


def unpack(values):
    return values.reshape((values.shape[0] * values.shape[1],) + values.shape[2:])


def shards(
    states,
    query_rows,
    key_rows,
    value_rows,
    gate_rows,
    beta_logit,
    decay_logit,
    residual,
    route_ids,
    route_prob,
    out_weight,
    core_gain,
    moe_gain,
    gate_up,
    down_weight,
    new_home,
):
    req_count = states.shape[0]
    step_count = query_rows.shape[1]
    model_width = residual.shape[-1]
    ep_size = lax.axis_size("ep")
    dp_size = lax.axis_size("dp")
    target = new_home // req_count % ep_size
    new_place = new_home % req_count
    fresh_states, core_out = recurrence(
        target, states, query_rows, key_rows, value_rows, gate_rows, beta_logit, decay_logit, core_gain
    )
    packed_place = jnp.zeros_like(new_place).at[target].set(new_place)
    received = (
        lax.all_to_all(fresh_states, "ep", split_axis=0, concat_axis=0, tiled=True),
        lax.all_to_all(packed_place, "ep", split_axis=0, concat_axis=0, tiled=True),
    )
    moved_out = place_rows(received[0], received[1])
    token_count = req_count * step_count
    core_flat = core_out.reshape(token_count, core_out.shape[-1])
    columns = jnp.dot(
        lax.all_gather(core_flat, "ep", axis=0, tiled=True),
        out_weight,
        preferred_element_type=jnp.float32,
    ).astype(jnp.bfloat16)
    attention = lax.all_to_all(columns, "ep", split_axis=0, concat_axis=1, tiled=True)
    hidden = (
        residual.reshape(token_count, model_width).astype(jnp.float32)
        + attention.astype(jnp.float32)
    ).astype(jnp.bfloat16)
    normed = rms_scale(hidden.astype(jnp.float32), moe_gain).astype(jnp.bfloat16)
    top_count = route_ids.shape[-1]
    experts = dp_size * ep_size
    capacity = (token_count * top_count + experts - 1) // experts + 1
    flat_ids = route_ids.reshape(-1)
    onehot = (flat_ids[:, None] == jnp.arange(experts, dtype=jnp.int32)[None, :]).astype(jnp.int32)
    route_rank = jnp.sum(jnp.cumsum(onehot, axis=0) * onehot, axis=1) - 1
    slot_index = flat_ids * capacity + route_rank
    slot_count = experts * capacity
    match = slot_index[None, :] == jnp.arange(slot_count, dtype=jnp.int32)[:, None]
    match = match.reshape(slot_count, token_count, top_count)
    pick = jnp.any(match, axis=-1).astype(jnp.bfloat16)
    outgoing = jnp.dot(pick, normed, preferred_element_type=jnp.float32).astype(jnp.bfloat16)
    arrived = lax.all_to_all(outgoing, ("dp", "ep"), 0, 0, tiled=True)
    result = expert_apply(arrived, gate_up[0], down_weight[0])
    returned = lax.all_to_all(result, ("dp", "ep"), 0, 0, tiled=True)
    weights = route_prob.reshape(token_count, top_count)
    weights = weights / jnp.sum(weights, -1, keepdims=True)
    spread = jnp.sum(jnp.where(match, weights[None, :, :], 0.0), axis=-1).T
    high = spread.astype(jnp.bfloat16)
    rest = spread - high.astype(jnp.float32)
    middle = rest.astype(jnp.bfloat16)
    low = (rest - middle.astype(jnp.float32)).astype(jnp.bfloat16)
    combined = (
        jnp.dot(high, returned, preferred_element_type=jnp.float32)
        + jnp.dot(middle, returned, preferred_element_type=jnp.float32)
    ) + jnp.dot(low, returned, preferred_element_type=jnp.float32)
    mixed_out = (
        (hidden.astype(jnp.float32) + combined)
        .astype(jnp.bfloat16)
        .reshape(req_count, step_count, model_width)
    )
    return (mixed_out, moved_out)


def solution(mesh):
    placed = (
        P(("dp", "ep"), None, None, None),
        P(("dp", "ep"), None, None),
        P(("dp", "ep"), None, None),
        P(("dp", "ep"), None, None),
        P(("dp", "ep"), None, None),
        P(("dp", "ep"), None, None),
        P(("dp", "ep"), None, None),
        P(("dp", "ep"), None, None),
        P(("dp", "ep"), None, None),
        P(("dp", "ep"), None, None),
        P(None, "ep"),
        P(),
        P(),
        P(("dp", "ep"), None, None),
        P(("dp", "ep"), None, None),
        P(("dp", "ep")),
    )
    return jax.shard_map(
        shards,
        mesh=mesh,
        in_specs=placed,
        out_specs=(P(("dp", "ep"), None, None), P(("dp", "ep"), None, None, None)),
        check_vma=False,
    )
```

```python
import jax
import jax.numpy as jnp
from jax import lax
from jax.sharding import PartitionSpec as P

import functools
from jax.experimental import pallas as pl
from jax.experimental.pallas import tpu as pltpu

epsilon = 1e-06
f32 = jnp.float32
bf16 = jnp.bfloat16


def split2(x):
    hi = x.astype(bf16)
    lo = (x - hi.astype(f32)).astype(bf16)
    return hi, lo


def recur_kernel(slot_ref, s_ref, kq_ref, v_ref, g_ref, dec_ref, beta_ref, gain_ref, so_ref, co_ref, n_ref, r_ref, u_ref):
    heads = s_ref.shape[1]
    width = s_ref.shape[-1]
    steps = v_ref.shape[1]
    span = 2 * steps
    kq = kq_ref[0].astype(f32)
    kq = kq * lax.rsqrt(jnp.sum(kq * kq, -1, keepdims=True) + epsilon)
    row = lax.broadcasted_iota(jnp.int32, kq.shape, 0)
    kq = jnp.where(row % span >= steps, kq * width ** (-0.5), kq)
    n_ref[...] = kq
    for h in range(heads):
        p = n_ref[pl.ds(h * span, span), :]
        hi = p.astype(bf16).astype(f32)
        rest = p - hi
        mid = rest.astype(bf16).astype(f32)
        lo = rest - mid
        lhs = jnp.concatenate([hi, mid, lo], axis=0).astype(bf16)
        res = jnp.dot(lhs, s_ref[0, h], preferred_element_type=f32)
        r_ref[pl.ds(h * span, span), :] = (res[0:span] + res[span:2 * span]) + res[2 * span:3 * span]
    decay = jax.nn.sigmoid(dec_ref[0])
    strength = jax.nn.sigmoid(beta_ref[0])
    gain = gain_ref[...]
    keys = [n_ref[pl.ds(t, heads, stride=span), :] for t in range(steps)]
    queries = [n_ref[pl.ds(steps + t, heads, stride=span), :] for t in range(steps)]
    u_ref[...] = jnp.zeros(u_ref.shape, f32)
    updates = []
    carried = []
    total = None
    for t in range(steps):
        a_t = decay[:, t:t + 1]
        b_t = strength[:, t:t + 1]
        total = a_t if t == 0 else total * a_t
        carried = [c * a_t for c in carried]
        memory = total * r_ref[pl.ds(t, heads, stride=span), :]
        for j in range(t):
            kk = jnp.sum(keys[j] * keys[t], -1, keepdims=True)
            memory = memory + (carried[j] * kk) * updates[j]
        values = v_ref[0, t].astype(f32)
        update = (values - memory) * b_t
        updates.append(update)
        carried.append(jnp.ones_like(a_t))
        reading = total * r_ref[pl.ds(steps + t, heads, stride=span), :]
        for j in range(t + 1):
            qk = jnp.sum(keys[j] * queries[t], -1, keepdims=True)
            coef = qk if j == t else carried[j] * qk
            reading = reading + coef * updates[j]
        scaled = reading * lax.rsqrt(jnp.mean(reading * reading, -1, keepdims=True) + epsilon)
        gate_vals = g_ref[0, t].astype(f32)
        co_ref[0, t] = (scaled * gain * (gate_vals * jax.nn.sigmoid(gate_vals))).astype(co_ref.dtype)
    for j in range(steps):
        u_ref[pl.ds(j, heads, stride=span), :] = carried[j] * updates[j]
    for h in range(heads):
        kt = n_ref[pl.ds(h * span, span), :].T
        w = u_ref[pl.ds(h * span, span), :]
        k_hi, k_lo = split2(kt)
        w_hi, w_lo = split2(w)
        delta = (
            jnp.dot(k_hi, w_hi, preferred_element_type=f32)
            + jnp.dot(k_hi, w_lo, preferred_element_type=f32)
            + jnp.dot(k_lo, w_hi, preferred_element_type=f32)
        )
        so_ref[0, h] = (total[h:h + 1, :] * s_ref[0, h].astype(f32) + delta).astype(so_ref.dtype)


def recurrence(slots, states, query_rows, key_rows, value_rows, gate_rows, beta_logit, decay_logit, core_gain):
    batch, heads, width, _ = states.shape
    steps = query_rows.shape[1]
    key_heads = query_rows.shape[-1] // width
    repeats = heads // key_heads
    span = 2 * steps
    kq = jnp.concatenate(
        [key_rows.reshape(batch, steps, key_heads, width), query_rows.reshape(batch, steps, key_heads, width)], axis=1
    )
    kq = jnp.repeat(kq.transpose(0, 2, 1, 3), repeats, axis=1).reshape(batch, heads * span, width)
    values = value_rows.reshape(batch, steps, heads, width)
    gates = gate_rows.reshape(batch, steps, heads, width)
    decay = decay_logit.astype(f32).transpose(0, 2, 1)
    beta = beta_logit.astype(f32).transpose(0, 2, 1)
    gain = core_gain.reshape(1, width)
    state_in = pl.BlockSpec((1, heads, width, width), lambda i, slot: (i, 0, 0, 0))
    state_out = pl.BlockSpec((1, heads, width, width), lambda i, slot: (slot[i], 0, 0, 0))
    row_spec = pl.BlockSpec((1, steps, heads, width), lambda i, slot: (i, 0, 0, 0))
    coef_spec = pl.BlockSpec((1, heads, steps), lambda i, slot: (i, 0, 0))
    fresh, core = pl.pallas_call(
        recur_kernel,
        grid_spec=pltpu.PrefetchScalarGridSpec(
            num_scalar_prefetch=1,
            grid=(batch,),
            in_specs=[
                state_in,
                pl.BlockSpec((1, heads * span, width), lambda i, slot: (i, 0, 0)),
                row_spec,
                row_spec,
                coef_spec,
                coef_spec,
                pl.BlockSpec((1, width), lambda i, slot: (0, 0)),
            ],
            out_specs=[state_out, row_spec],
            scratch_shapes=[pltpu.VMEM((heads * span, width), f32)] * 3,
        ),
        out_shape=[
            jax.ShapeDtypeStruct(states.shape, bf16),
            jax.ShapeDtypeStruct((batch, steps, heads, width), bf16),
        ],
    )(slots, states, kq, values, gates, decay, beta, gain)
    return fresh, core.reshape(batch, steps, heads * width)


def unit_rows(values):
    return values * lax.rsqrt(jnp.sum(values * values, -1, keepdims=True) + epsilon)


def delta_block(
    state_in, query_rows, key_rows, value_rows, gate_rows, beta_logit, decay_logit, core_gain
):
    batch_size = state_in.shape[0]
    head_count = decay_logit.shape[-1]
    head_width = state_in.shape[-1]
    key_heads = query_rows.shape[-1] // head_width
    repeats = head_count // key_heads
    memory_state = state_in.astype(jnp.float32)
    outputs = []
    for position in range(query_rows.shape[1]):
        queries = unit_rows(
            query_rows[:, position].astype(jnp.float32).reshape(batch_size, key_heads, head_width)
        )
        queries = jnp.repeat(queries, repeats, axis=1) * head_width ** (-0.5)
        key_units = unit_rows(
            key_rows[:, position].astype(jnp.float32).reshape(batch_size, key_heads, head_width)
        )
        key_units = jnp.repeat(key_units, repeats, axis=1)
        values = (
            value_rows[:, position].astype(jnp.float32).reshape(batch_size, head_count, head_width)
        )
        decays = jax.nn.sigmoid(decay_logit[:, position].astype(jnp.float32))
        strength = jax.nn.sigmoid(beta_logit[:, position].astype(jnp.float32))
        memory_state = memory_state * decays[:, :, None, None]
        memory = jnp.einsum(
            "bhkv,bhk->bhv", memory_state, key_units, precision=lax.Precision.HIGHEST
        )
        update = (values - memory) * strength[:, :, None]
        memory_state = memory_state + key_units[:, :, :, None] * update[:, :, None, :]
        reading = jnp.einsum(
            "bhkv,bhk->bhv", memory_state, queries, precision=lax.Precision.HIGHEST
        )
        scaled = reading * lax.rsqrt(jnp.mean(reading * reading, -1, keepdims=True) + epsilon)
        gate_vals = (
            gate_rows[:, position].astype(jnp.float32).reshape(batch_size, head_count, head_width)
        )
        gated_out = scaled * core_gain * jax.nn.silu(gate_vals)
        outputs.append(gated_out.reshape(batch_size, head_count * head_width).astype(jnp.bfloat16))
    return (memory_state.astype(jnp.bfloat16), jnp.stack(outputs, axis=1))


def place_kernel(place_ref, in_ref, out_ref):
    out_ref[...] = in_ref[...]


def place_rows(rows, places):
    block = (1,) + rows.shape[1:]
    tail = (0,) * (rows.ndim - 1)
    return pl.pallas_call(
        place_kernel,
        grid_spec=pltpu.PrefetchScalarGridSpec(
            num_scalar_prefetch=1,
            grid=(rows.shape[0],),
            in_specs=[pl.BlockSpec(block, lambda j, place: (j,) + tail)],
            out_specs=pl.BlockSpec(block, lambda j, place: (place[j],) + tail),
        ),
        out_shape=jax.ShapeDtypeStruct(rows.shape, rows.dtype),
    )(places, rows)


def rms_scale(values, gain):
    return values * lax.rsqrt(jnp.mean(values * values, -1, keepdims=True) + epsilon) * gain


def expert_apply(chosen_rows, gate_up, down_weight):
    hidden_units = down_weight.shape[0]
    joined = jnp.dot(chosen_rows, gate_up, preferred_element_type=jnp.float32)
    active = (jax.nn.silu(joined[:, :hidden_units]) * joined[:, hidden_units:]).astype(jnp.bfloat16)
    return jnp.dot(active, down_weight, preferred_element_type=jnp.float32).astype(jnp.bfloat16)


def pack(values, positions, lane_count):
    zeroed = jnp.zeros(values.shape, values.dtype)
    placed = zeroed.at[positions].set(values)
    return placed.reshape((lane_count, values.shape[0] // lane_count) + values.shape[1:])


def unpack(values):
    return values.reshape((values.shape[0] * values.shape[1],) + values.shape[2:])


def shards(
    states,
    query_rows,
    key_rows,
    value_rows,
    gate_rows,
    beta_logit,
    decay_logit,
    residual,
    route_ids,
    route_prob,
    out_weight,
    core_gain,
    moe_gain,
    gate_up,
    down_weight,
    new_home,
):
    req_count = states.shape[0]
    step_count = query_rows.shape[1]
    model_width = residual.shape[-1]
    ep_size = lax.axis_size("ep")
    dp_size = lax.axis_size("dp")
    target = new_home // req_count % ep_size
    new_place = new_home % req_count
    fresh_states, core_out = recurrence(
        target, states, query_rows, key_rows, value_rows, gate_rows, beta_logit, decay_logit, core_gain
    )
    packed_place = jnp.zeros_like(new_place).at[target].set(new_place)
    received = (
        lax.all_to_all(fresh_states, "ep", split_axis=0, concat_axis=0, tiled=True),
        lax.all_to_all(packed_place, "ep", split_axis=0, concat_axis=0, tiled=True),
    )
    moved_out = place_rows(received[0], received[1])
    token_count = req_count * step_count
    core_flat = core_out.reshape(token_count, core_out.shape[-1])
    columns = jnp.dot(
        lax.all_gather(core_flat, "ep", axis=0, tiled=True),
        out_weight,
        preferred_element_type=jnp.float32,
    ).astype(jnp.bfloat16)
    attention = lax.all_to_all(columns, "ep", split_axis=0, concat_axis=1, tiled=True)
    hidden = (
        residual.reshape(token_count, model_width).astype(jnp.float32)
        + attention.astype(jnp.float32)
    ).astype(jnp.bfloat16)
    normed = rms_scale(hidden.astype(jnp.float32), moe_gain).astype(jnp.bfloat16)
    top_count = route_ids.shape[-1]
    experts = dp_size * ep_size
    capacity = 4
    flat_ids = route_ids.reshape(-1)
    onehot = (flat_ids[:, None] == jnp.arange(experts, dtype=jnp.int32)[None, :]).astype(jnp.int32)
    route_rank = jnp.sum(jnp.cumsum(onehot, axis=0) * onehot, axis=1) - 1
    slot_index = flat_ids * capacity + route_rank
    slot_count = experts * capacity
    match = slot_index[None, :] == jnp.arange(slot_count, dtype=jnp.int32)[:, None]
    match = match.reshape(experts, capacity, token_count, top_count)
    pick = jnp.any(match, axis=-1).astype(jnp.bfloat16)
    outgoing = jnp.einsum(
        "esk,kd->esd", pick, normed, preferred_element_type=jnp.float32
    ).astype(jnp.bfloat16)
    arrived = lax.all_to_all(outgoing, ("dp", "ep"), 0, 0, tiled=True)
    hidden_units = down_weight.shape[1]
    joined = jnp.einsum("esd,df->esf", arrived, gate_up[0], preferred_element_type=jnp.float32)
    active = (jax.nn.silu(joined[..., :hidden_units]) * joined[..., hidden_units:]).astype(jnp.bfloat16)
    result = jnp.einsum(
        "esf,fd->esd", active, down_weight[0], preferred_element_type=jnp.float32
    ).astype(jnp.bfloat16)
    returned = lax.all_to_all(result, ("dp", "ep"), 0, 0, tiled=True)
    weights = route_prob.reshape(token_count, top_count)
    weights = weights / jnp.sum(weights, -1, keepdims=True)
    spread = jnp.sum(jnp.where(match, weights[None, None, :, :], 0.0), axis=-1)
    high = spread.astype(jnp.bfloat16)
    rest = spread - high.astype(jnp.float32)
    middle = rest.astype(jnp.bfloat16)
    low = (rest - middle.astype(jnp.float32)).astype(jnp.bfloat16)
    combine = "esk,esd->kd"
    combined = (
        jnp.einsum(combine, high, returned, preferred_element_type=jnp.float32)
        + jnp.einsum(combine, middle, returned, preferred_element_type=jnp.float32)
    ) + jnp.einsum(combine, low, returned, preferred_element_type=jnp.float32)
    mixed_out = (
        (hidden.astype(jnp.float32) + combined)
        .astype(jnp.bfloat16)
        .reshape(req_count, step_count, model_width)
    )
    return (mixed_out, moved_out)


def solution(mesh):
    placed = (
        P(("dp", "ep"), None, None, None),
        P(("dp", "ep"), None, None),
        P(("dp", "ep"), None, None),
        P(("dp", "ep"), None, None),
        P(("dp", "ep"), None, None),
        P(("dp", "ep"), None, None),
        P(("dp", "ep"), None, None),
        P(("dp", "ep"), None, None),
        P(("dp", "ep"), None, None),
        P(("dp", "ep"), None, None),
        P(None, "ep"),
        P(),
        P(),
        P(("dp", "ep"), None, None),
        P(("dp", "ep"), None, None),
        P(("dp", "ep")),
    )
    return jax.shard_map(
        shards,
        mesh=mesh,
        in_specs=placed,
        out_specs=(P(("dp", "ep"), None, None), P(("dp", "ep"), None, None, None)),
        check_vma=False,
    )
```

```python
import jax
import jax.numpy as jnp
from jax import lax
from jax.sharding import PartitionSpec as P

import functools
from jax.experimental import pallas as pl
from jax.experimental.pallas import tpu as pltpu

epsilon = 1e-06
f32 = jnp.float32
bf16 = jnp.bfloat16


def split2(x):
    hi = x.astype(bf16)
    lo = (x - hi.astype(f32)).astype(bf16)
    return hi, lo


def recur_kernel(slot_ref, s_ref, kq_ref, v_ref, g_ref, dec_ref, beta_ref, gain_ref, so_ref, co_ref, n_ref, r_ref, u_ref):
    heads = s_ref.shape[1]
    width = s_ref.shape[-1]
    steps = v_ref.shape[1]
    span = 2 * steps
    kq = kq_ref[0].astype(f32)
    kq = kq * lax.rsqrt(jnp.sum(kq * kq, -1, keepdims=True) + epsilon)
    row = lax.broadcasted_iota(jnp.int32, kq.shape, 0)
    kq = jnp.where(row % span >= steps, kq * width ** (-0.5), kq)
    n_ref[...] = kq
    for h in range(heads):
        p = n_ref[pl.ds(h * span, span), :]
        hi = p.astype(bf16).astype(f32)
        rest = p - hi
        mid = rest.astype(bf16).astype(f32)
        lo = rest - mid
        lhs = jnp.concatenate([hi, mid, lo], axis=0).astype(bf16)
        res = jnp.dot(lhs, s_ref[0, h], preferred_element_type=f32)
        r_ref[pl.ds(h * span, span), :] = (res[0:span] + res[span:2 * span]) + res[2 * span:3 * span]
    decay = jax.nn.sigmoid(dec_ref[0])
    strength = jax.nn.sigmoid(beta_ref[0])
    gain = gain_ref[...]
    keys = [n_ref[pl.ds(t, heads, stride=span), :] for t in range(steps)]
    queries = [n_ref[pl.ds(steps + t, heads, stride=span), :] for t in range(steps)]
    u_ref[...] = jnp.zeros(u_ref.shape, f32)
    updates = []
    carried = []
    total = None
    for t in range(steps):
        a_t = decay[:, t:t + 1]
        b_t = strength[:, t:t + 1]
        total = a_t if t == 0 else total * a_t
        carried = [c * a_t for c in carried]
        memory = total * r_ref[pl.ds(t, heads, stride=span), :]
        for j in range(t):
            kk = jnp.sum(keys[j] * keys[t], -1, keepdims=True)
            memory = memory + (carried[j] * kk) * updates[j]
        values = v_ref[0, t].astype(f32)
        update = (values - memory) * b_t
        updates.append(update)
        carried.append(jnp.ones_like(a_t))
        reading = total * r_ref[pl.ds(steps + t, heads, stride=span), :]
        for j in range(t + 1):
            qk = jnp.sum(keys[j] * queries[t], -1, keepdims=True)
            coef = qk if j == t else carried[j] * qk
            reading = reading + coef * updates[j]
        scaled = reading * lax.rsqrt(jnp.mean(reading * reading, -1, keepdims=True) + epsilon)
        gate_vals = g_ref[0, t].astype(f32)
        co_ref[0, t] = (scaled * gain * (gate_vals * jax.nn.sigmoid(gate_vals))).astype(co_ref.dtype)
    for j in range(steps):
        u_ref[pl.ds(j, heads, stride=span), :] = carried[j] * updates[j]
    for h in range(heads):
        kt = n_ref[pl.ds(h * span, span), :].T
        w = u_ref[pl.ds(h * span, span), :]
        k_hi, k_lo = split2(kt)
        w_hi, w_lo = split2(w)
        delta = (
            jnp.dot(k_hi, w_hi, preferred_element_type=f32)
            + jnp.dot(k_hi, w_lo, preferred_element_type=f32)
            + jnp.dot(k_lo, w_hi, preferred_element_type=f32)
        )
        so_ref[0, h] = (total[h:h + 1, :] * s_ref[0, h].astype(f32) + delta).astype(so_ref.dtype)


def recurrence(slots, states, query_rows, key_rows, value_rows, gate_rows, beta_logit, decay_logit, core_gain):
    batch, heads, width, _ = states.shape
    steps = query_rows.shape[1]
    key_heads = query_rows.shape[-1] // width
    repeats = heads // key_heads
    span = 2 * steps
    kq = jnp.concatenate(
        [key_rows.reshape(batch, steps, key_heads, width), query_rows.reshape(batch, steps, key_heads, width)], axis=1
    )
    kq = jnp.repeat(kq.transpose(0, 2, 1, 3), repeats, axis=1).reshape(batch, heads * span, width)
    values = value_rows.reshape(batch, steps, heads, width)
    gates = gate_rows.reshape(batch, steps, heads, width)
    decay = decay_logit.astype(f32).transpose(0, 2, 1)
    beta = beta_logit.astype(f32).transpose(0, 2, 1)
    gain = core_gain.reshape(1, width)
    state_in = pl.BlockSpec((1, heads, width, width), lambda i, slot: (i, 0, 0, 0))
    state_out = pl.BlockSpec((1, heads, width, width), lambda i, slot: (slot[i], 0, 0, 0))
    row_spec = pl.BlockSpec((1, steps, heads, width), lambda i, slot: (i, 0, 0, 0))
    coef_spec = pl.BlockSpec((1, heads, steps), lambda i, slot: (i, 0, 0))
    fresh, core = pl.pallas_call(
        recur_kernel,
        grid_spec=pltpu.PrefetchScalarGridSpec(
            num_scalar_prefetch=1,
            grid=(batch,),
            in_specs=[
                state_in,
                pl.BlockSpec((1, heads * span, width), lambda i, slot: (i, 0, 0)),
                row_spec,
                row_spec,
                coef_spec,
                coef_spec,
                pl.BlockSpec((1, width), lambda i, slot: (0, 0)),
            ],
            out_specs=[state_out, row_spec],
            scratch_shapes=[pltpu.VMEM((heads * span, width), f32)] * 3,
        ),
        out_shape=[
            jax.ShapeDtypeStruct(states.shape, bf16),
            jax.ShapeDtypeStruct((batch, steps, heads, width), bf16),
        ],
    )(slots, states, kq, values, gates, decay, beta, gain)
    return fresh, core.reshape(batch, steps, heads * width)


def unit_rows(values):
    return values * lax.rsqrt(jnp.sum(values * values, -1, keepdims=True) + epsilon)


def delta_block(
    state_in, query_rows, key_rows, value_rows, gate_rows, beta_logit, decay_logit, core_gain
):
    batch_size = state_in.shape[0]
    head_count = decay_logit.shape[-1]
    head_width = state_in.shape[-1]
    key_heads = query_rows.shape[-1] // head_width
    repeats = head_count // key_heads
    memory_state = state_in.astype(jnp.float32)
    outputs = []
    for position in range(query_rows.shape[1]):
        queries = unit_rows(
            query_rows[:, position].astype(jnp.float32).reshape(batch_size, key_heads, head_width)
        )
        queries = jnp.repeat(queries, repeats, axis=1) * head_width ** (-0.5)
        key_units = unit_rows(
            key_rows[:, position].astype(jnp.float32).reshape(batch_size, key_heads, head_width)
        )
        key_units = jnp.repeat(key_units, repeats, axis=1)
        values = (
            value_rows[:, position].astype(jnp.float32).reshape(batch_size, head_count, head_width)
        )
        decays = jax.nn.sigmoid(decay_logit[:, position].astype(jnp.float32))
        strength = jax.nn.sigmoid(beta_logit[:, position].astype(jnp.float32))
        memory_state = memory_state * decays[:, :, None, None]
        memory = jnp.einsum(
            "bhkv,bhk->bhv", memory_state, key_units, precision=lax.Precision.HIGHEST
        )
        update = (values - memory) * strength[:, :, None]
        memory_state = memory_state + key_units[:, :, :, None] * update[:, :, None, :]
        reading = jnp.einsum(
            "bhkv,bhk->bhv", memory_state, queries, precision=lax.Precision.HIGHEST
        )
        scaled = reading * lax.rsqrt(jnp.mean(reading * reading, -1, keepdims=True) + epsilon)
        gate_vals = (
            gate_rows[:, position].astype(jnp.float32).reshape(batch_size, head_count, head_width)
        )
        gated_out = scaled * core_gain * jax.nn.silu(gate_vals)
        outputs.append(gated_out.reshape(batch_size, head_count * head_width).astype(jnp.bfloat16))
    return (memory_state.astype(jnp.bfloat16), jnp.stack(outputs, axis=1))


def place_kernel(place_ref, in_ref, out_ref):
    out_ref[...] = in_ref[...]


def place_rows(rows, places):
    block = (1,) + rows.shape[1:]
    tail = (0,) * (rows.ndim - 1)
    return pl.pallas_call(
        place_kernel,
        grid_spec=pltpu.PrefetchScalarGridSpec(
            num_scalar_prefetch=1,
            grid=(rows.shape[0],),
            in_specs=[pl.BlockSpec(block, lambda j, place: (j,) + tail)],
            out_specs=pl.BlockSpec(block, lambda j, place: (place[j],) + tail),
        ),
        out_shape=jax.ShapeDtypeStruct(rows.shape, rows.dtype),
    )(places, rows)


def rms_scale(values, gain):
    return values * lax.rsqrt(jnp.mean(values * values, -1, keepdims=True) + epsilon) * gain


def expert_apply(chosen_rows, gate_up, down_weight):
    hidden_units = down_weight.shape[0]
    joined = jnp.dot(chosen_rows, gate_up, preferred_element_type=jnp.float32)
    active = (jax.nn.silu(joined[:, :hidden_units]) * joined[:, hidden_units:]).astype(jnp.bfloat16)
    return jnp.dot(active, down_weight, preferred_element_type=jnp.float32).astype(jnp.bfloat16)


def pack(values, positions, lane_count):
    zeroed = jnp.zeros(values.shape, values.dtype)
    placed = zeroed.at[positions].set(values)
    return placed.reshape((lane_count, values.shape[0] // lane_count) + values.shape[1:])


def unpack(values):
    return values.reshape((values.shape[0] * values.shape[1],) + values.shape[2:])


def shards(
    states,
    query_rows,
    key_rows,
    value_rows,
    gate_rows,
    beta_logit,
    decay_logit,
    residual,
    route_ids,
    route_prob,
    out_weight,
    core_gain,
    moe_gain,
    gate_up,
    down_weight,
    new_home,
):
    req_count = states.shape[0]
    step_count = query_rows.shape[1]
    model_width = residual.shape[-1]
    ep_size = lax.axis_size("ep")
    dp_size = lax.axis_size("dp")
    target = new_home // req_count % ep_size
    new_place = new_home % req_count
    fresh_states, core_out = recurrence(
        target, states, query_rows, key_rows, value_rows, gate_rows, beta_logit, decay_logit, core_gain
    )
    packed_place = jnp.zeros_like(new_place).at[target].set(new_place)
    received = (
        lax.all_to_all(fresh_states, "ep", split_axis=0, concat_axis=0, tiled=True),
        lax.all_to_all(packed_place, "ep", split_axis=0, concat_axis=0, tiled=True),
    )
    moved_out = place_rows(received[0], received[1])
    token_count = req_count * step_count
    core_flat = core_out.reshape(token_count, core_out.shape[-1])
    columns = jnp.dot(
        lax.all_gather(core_flat, "ep", axis=0, tiled=True),
        out_weight,
        preferred_element_type=jnp.float32,
    ).astype(jnp.bfloat16)
    attention = lax.all_to_all(columns, "ep", split_axis=0, concat_axis=1, tiled=True)
    hidden = (
        residual.reshape(token_count, model_width).astype(jnp.float32)
        + attention.astype(jnp.float32)
    ).astype(jnp.bfloat16)
    normed = rms_scale(hidden.astype(jnp.float32), moe_gain).astype(jnp.bfloat16)
    top_count = route_ids.shape[-1]
    experts = dp_size * ep_size
    capacity = (token_count * top_count + experts - 1) // experts + 1
    flat_ids = route_ids.reshape(-1)
    onehot = (flat_ids[:, None] == jnp.arange(experts, dtype=jnp.int32)[None, :]).astype(jnp.int32)
    route_rank = jnp.sum(jnp.cumsum(onehot, axis=0) * onehot, axis=1) - 1
    slot_index = flat_ids * capacity + route_rank
    slot_count = experts * capacity
    match = slot_index[None, :] == jnp.arange(slot_count, dtype=jnp.int32)[:, None]
    match = match.reshape(experts, capacity, token_count, top_count)
    pick = jnp.any(match, axis=-1).astype(jnp.bfloat16)
    lane_count = 128
    chunks = model_width // lane_count
    normed_tiles = normed.reshape(token_count, chunks, lane_count)
    outgoing = jnp.einsum(
        "esk,kcl->escl", pick, normed_tiles, preferred_element_type=jnp.float32
    ).astype(jnp.bfloat16)
    outgoing = outgoing.reshape(experts, capacity * chunks, lane_count)
    arrived = lax.all_to_all(outgoing, ("dp", "ep"), 0, 0, tiled=True)
    arrived = arrived.reshape(experts, capacity, chunks, lane_count)
    hidden_units = down_weight.shape[1]
    gate_tiles = gate_up[0].reshape(chunks, lane_count, gate_up.shape[-1])
    joined = jnp.einsum("escl,clf->esf", arrived, gate_tiles, preferred_element_type=jnp.float32)
    active = (jax.nn.silu(joined[..., :hidden_units]) * joined[..., hidden_units:]).astype(jnp.bfloat16)
    down_tiles = down_weight[0].reshape(hidden_units, chunks, lane_count)
    result = jnp.einsum(
        "esf,fcl->escl", active, down_tiles, preferred_element_type=jnp.float32
    ).astype(jnp.bfloat16)
    result = result.reshape(experts, capacity * chunks, lane_count)
    returned = lax.all_to_all(result, ("dp", "ep"), 0, 0, tiled=True)
    returned = returned.reshape(experts, capacity, chunks, lane_count)
    weights = route_prob.reshape(token_count, top_count)
    weights = weights / jnp.sum(weights, -1, keepdims=True)
    spread = jnp.sum(jnp.where(match, weights[None, None, :, :], 0.0), axis=-1)
    high = spread.astype(jnp.bfloat16)
    rest = spread - high.astype(jnp.float32)
    middle = rest.astype(jnp.bfloat16)
    low = (rest - middle.astype(jnp.float32)).astype(jnp.bfloat16)
    combine = "esk,escl->kcl"
    combined = (
        jnp.einsum(combine, high, returned, preferred_element_type=jnp.float32)
        + jnp.einsum(combine, middle, returned, preferred_element_type=jnp.float32)
    ) + jnp.einsum(combine, low, returned, preferred_element_type=jnp.float32)
    combined = combined.reshape(token_count, model_width)
    mixed_out = (
        (hidden.astype(jnp.float32) + combined)
        .astype(jnp.bfloat16)
        .reshape(req_count, step_count, model_width)
    )
    return (mixed_out, moved_out)


def solution(mesh):
    placed = (
        P(("dp", "ep"), None, None, None),
        P(("dp", "ep"), None, None),
        P(("dp", "ep"), None, None),
        P(("dp", "ep"), None, None),
        P(("dp", "ep"), None, None),
        P(("dp", "ep"), None, None),
        P(("dp", "ep"), None, None),
        P(("dp", "ep"), None, None),
        P(("dp", "ep"), None, None),
        P(("dp", "ep"), None, None),
        P(None, "ep"),
        P(),
        P(),
        P(("dp", "ep"), None, None),
        P(("dp", "ep"), None, None),
        P(("dp", "ep")),
    )
    return jax.shard_map(
        shards,
        mesh=mesh,
        in_specs=placed,
        out_specs=(P(("dp", "ep"), None, None), P(("dp", "ep"), None, None, None)),
        check_vma=False,
    )
```

```python
import jax
import jax.numpy as jnp
from jax import lax
from jax.sharding import PartitionSpec as P

import functools
from jax.experimental import pallas as pl
from jax.experimental.pallas import tpu as pltpu

epsilon = 1e-06
f32 = jnp.float32
bf16 = jnp.bfloat16


def split2(x):
    hi = x.astype(bf16)
    lo = (x - hi.astype(f32)).astype(bf16)
    return hi, lo


def recur_kernel(slot_ref, s_ref, kq_ref, v_ref, g_ref, dec_ref, beta_ref, gain_ref, so_ref, co_ref, n_ref, r_ref, u_ref):
    heads = s_ref.shape[1]
    width = s_ref.shape[-1]
    steps = v_ref.shape[1]
    span = 2 * steps
    kq = kq_ref[0].astype(f32)
    kq = kq * lax.rsqrt(jnp.sum(kq * kq, -1, keepdims=True) + epsilon)
    row = lax.broadcasted_iota(jnp.int32, kq.shape, 0)
    kq = jnp.where(row % span >= steps, kq * width ** (-0.5), kq)
    n_ref[...] = kq
    for h in range(heads):
        p = n_ref[pl.ds(h * span, span), :]
        hi = p.astype(bf16).astype(f32)
        rest = p - hi
        mid = rest.astype(bf16).astype(f32)
        lo = rest - mid
        lhs = jnp.concatenate([hi, mid, lo], axis=0).astype(bf16)
        res = jnp.dot(lhs, s_ref[0, h], preferred_element_type=f32)
        r_ref[pl.ds(h * span, span), :] = (res[0:span] + res[span:2 * span]) + res[2 * span:3 * span]
    decay = jax.nn.sigmoid(dec_ref[0])
    strength = jax.nn.sigmoid(beta_ref[0])
    gain = gain_ref[...]
    keys = [n_ref[pl.ds(t, heads, stride=span), :] for t in range(steps)]
    queries = [n_ref[pl.ds(steps + t, heads, stride=span), :] for t in range(steps)]
    u_ref[...] = jnp.zeros(u_ref.shape, f32)
    updates = []
    carried = []
    total = None
    for t in range(steps):
        a_t = decay[:, t:t + 1]
        b_t = strength[:, t:t + 1]
        total = a_t if t == 0 else total * a_t
        carried = [c * a_t for c in carried]
        memory = total * r_ref[pl.ds(t, heads, stride=span), :]
        for j in range(t):
            kk = jnp.sum(keys[j] * keys[t], -1, keepdims=True)
            memory = memory + (carried[j] * kk) * updates[j]
        values = v_ref[0, t].astype(f32)
        update = (values - memory) * b_t
        updates.append(update)
        carried.append(jnp.ones_like(a_t))
        reading = total * r_ref[pl.ds(steps + t, heads, stride=span), :]
        for j in range(t + 1):
            qk = jnp.sum(keys[j] * queries[t], -1, keepdims=True)
            coef = qk if j == t else carried[j] * qk
            reading = reading + coef * updates[j]
        scaled = reading * lax.rsqrt(jnp.mean(reading * reading, -1, keepdims=True) + epsilon)
        gate_vals = g_ref[0, t].astype(f32)
        co_ref[0, t] = (scaled * gain * (gate_vals * jax.nn.sigmoid(gate_vals))).astype(co_ref.dtype)
    for j in range(steps):
        u_ref[pl.ds(j, heads, stride=span), :] = carried[j] * updates[j]
    for h in range(heads):
        kt = n_ref[pl.ds(h * span, span), :].T
        w = u_ref[pl.ds(h * span, span), :]
        k_hi, k_lo = split2(kt)
        w_hi, w_lo = split2(w)
        delta = (
            jnp.dot(k_hi, w_hi, preferred_element_type=f32)
            + jnp.dot(k_hi, w_lo, preferred_element_type=f32)
            + jnp.dot(k_lo, w_hi, preferred_element_type=f32)
        )
        so_ref[0, h] = (total[h:h + 1, :] * s_ref[0, h].astype(f32) + delta).astype(so_ref.dtype)


def recurrence(slots, states, query_rows, key_rows, value_rows, gate_rows, beta_logit, decay_logit, core_gain):
    batch, heads, width, _ = states.shape
    steps = query_rows.shape[1]
    key_heads = query_rows.shape[-1] // width
    repeats = heads // key_heads
    span = 2 * steps
    kq = jnp.concatenate(
        [key_rows.reshape(batch, steps, key_heads, width), query_rows.reshape(batch, steps, key_heads, width)], axis=1
    )
    kq = jnp.repeat(kq.transpose(0, 2, 1, 3), repeats, axis=1).reshape(batch, heads * span, width)
    values = value_rows.reshape(batch, steps, heads, width)
    gates = gate_rows.reshape(batch, steps, heads, width)
    decay = decay_logit.astype(f32).transpose(0, 2, 1)
    beta = beta_logit.astype(f32).transpose(0, 2, 1)
    gain = core_gain.reshape(1, width)
    state_in = pl.BlockSpec((1, heads, width, width), lambda i, slot: (i, 0, 0, 0))
    state_out = pl.BlockSpec((1, heads, width, width), lambda i, slot: (slot[i], 0, 0, 0))
    row_spec = pl.BlockSpec((1, steps, heads, width), lambda i, slot: (i, 0, 0, 0))
    coef_spec = pl.BlockSpec((1, heads, steps), lambda i, slot: (i, 0, 0))
    fresh, core = pl.pallas_call(
        recur_kernel,
        grid_spec=pltpu.PrefetchScalarGridSpec(
            num_scalar_prefetch=1,
            grid=(batch,),
            in_specs=[
                state_in,
                pl.BlockSpec((1, heads * span, width), lambda i, slot: (i, 0, 0)),
                row_spec,
                row_spec,
                coef_spec,
                coef_spec,
                pl.BlockSpec((1, width), lambda i, slot: (0, 0)),
            ],
            out_specs=[state_out, row_spec],
            scratch_shapes=[pltpu.VMEM((heads * span, width), f32)] * 3,
        ),
        out_shape=[
            jax.ShapeDtypeStruct(states.shape, bf16),
            jax.ShapeDtypeStruct((batch, steps, heads, width), bf16),
        ],
    )(slots, states, kq, values, gates, decay, beta, gain)
    return fresh, core.reshape(batch, steps, heads * width)


def unit_rows(values):
    return values * lax.rsqrt(jnp.sum(values * values, -1, keepdims=True) + epsilon)


def delta_block(
    state_in, query_rows, key_rows, value_rows, gate_rows, beta_logit, decay_logit, core_gain
):
    batch_size = state_in.shape[0]
    head_count = decay_logit.shape[-1]
    head_width = state_in.shape[-1]
    key_heads = query_rows.shape[-1] // head_width
    repeats = head_count // key_heads
    memory_state = state_in.astype(jnp.float32)
    outputs = []
    for position in range(query_rows.shape[1]):
        queries = unit_rows(
            query_rows[:, position].astype(jnp.float32).reshape(batch_size, key_heads, head_width)
        )
        queries = jnp.repeat(queries, repeats, axis=1) * head_width ** (-0.5)
        key_units = unit_rows(
            key_rows[:, position].astype(jnp.float32).reshape(batch_size, key_heads, head_width)
        )
        key_units = jnp.repeat(key_units, repeats, axis=1)
        values = (
            value_rows[:, position].astype(jnp.float32).reshape(batch_size, head_count, head_width)
        )
        decays = jax.nn.sigmoid(decay_logit[:, position].astype(jnp.float32))
        strength = jax.nn.sigmoid(beta_logit[:, position].astype(jnp.float32))
        memory_state = memory_state * decays[:, :, None, None]
        memory = jnp.einsum(
            "bhkv,bhk->bhv", memory_state, key_units, precision=lax.Precision.HIGHEST
        )
        update = (values - memory) * strength[:, :, None]
        memory_state = memory_state + key_units[:, :, :, None] * update[:, :, None, :]
        reading = jnp.einsum(
            "bhkv,bhk->bhv", memory_state, queries, precision=lax.Precision.HIGHEST
        )
        scaled = reading * lax.rsqrt(jnp.mean(reading * reading, -1, keepdims=True) + epsilon)
        gate_vals = (
            gate_rows[:, position].astype(jnp.float32).reshape(batch_size, head_count, head_width)
        )
        gated_out = scaled * core_gain * jax.nn.silu(gate_vals)
        outputs.append(gated_out.reshape(batch_size, head_count * head_width).astype(jnp.bfloat16))
    return (memory_state.astype(jnp.bfloat16), jnp.stack(outputs, axis=1))


def migrate_kernel(src_hbm, dst_hbm, send_sem, recv_sem, local_sem):
    lanes = src_hbm.shape[0]
    group = lax.axis_index("dp")
    me = lax.axis_index("ep")
    mesh_ids = pl.DeviceIdType.MESH
    barrier = pltpu.get_barrier_semaphore()
    for i in range(1, lanes):
        pl.semaphore_signal(barrier, 1, device_id=(group, lax.rem(me + i, lanes)), device_id_type=mesh_ids)
    pl.semaphore_wait(barrier, lanes - 1)
    own = pltpu.make_async_copy(src_hbm.at[me], dst_hbm.at[me], local_sem)
    own.start()
    copies = []
    for i in range(1, lanes):
        peer = lax.rem(me + i, lanes)
        copy = pltpu.make_async_remote_copy(
            src_hbm.at[peer],
            dst_hbm.at[me],
            send_sem.at[i - 1],
            recv_sem.at[i - 1],
            device_id=(group, peer),
            device_id_type=mesh_ids,
        )
        copy.start()
        copies.append(copy)
    own.wait()
    for copy in copies:
        copy.wait()


def migrate(rows):
    lanes = rows.shape[0]
    any_spec = pl.BlockSpec(memory_space=pl.ANY)
    return pl.pallas_call(
        migrate_kernel,
        in_specs=[any_spec],
        out_specs=any_spec,
        out_shape=jax.ShapeDtypeStruct(rows.shape, rows.dtype),
        scratch_shapes=[
            pltpu.SemaphoreType.DMA((lanes - 1,)),
            pltpu.SemaphoreType.DMA((lanes - 1,)),
            pltpu.SemaphoreType.DMA,
        ],
        compiler_params=pltpu.CompilerParams(collective_id=0, has_side_effects=True),
        cost_estimate=pl.CostEstimate(flops=0, transcendentals=0, bytes_accessed=2 * rows.size * rows.dtype.itemsize),
    )(rows)


def place_kernel(place_ref, in_ref, out_ref):
    out_ref[...] = in_ref[...]


def place_rows(rows, places):
    block = (1,) + rows.shape[1:]
    tail = (0,) * (rows.ndim - 1)
    return pl.pallas_call(
        place_kernel,
        grid_spec=pltpu.PrefetchScalarGridSpec(
            num_scalar_prefetch=1,
            grid=(rows.shape[0],),
            in_specs=[pl.BlockSpec(block, lambda j, place: (j,) + tail)],
            out_specs=pl.BlockSpec(block, lambda j, place: (place[j],) + tail),
        ),
        out_shape=jax.ShapeDtypeStruct(rows.shape, rows.dtype),
    )(places, rows)


def rms_scale(values, gain):
    return values * lax.rsqrt(jnp.mean(values * values, -1, keepdims=True) + epsilon) * gain


def expert_apply(chosen_rows, gate_up, down_weight):
    hidden_units = down_weight.shape[0]
    joined = jnp.dot(chosen_rows, gate_up, preferred_element_type=jnp.float32)
    active = (jax.nn.silu(joined[:, :hidden_units]) * joined[:, hidden_units:]).astype(jnp.bfloat16)
    return jnp.dot(active, down_weight, preferred_element_type=jnp.float32).astype(jnp.bfloat16)


def pack(values, positions, lane_count):
    zeroed = jnp.zeros(values.shape, values.dtype)
    placed = zeroed.at[positions].set(values)
    return placed.reshape((lane_count, values.shape[0] // lane_count) + values.shape[1:])


def unpack(values):
    return values.reshape((values.shape[0] * values.shape[1],) + values.shape[2:])


def shards(
    states,
    query_rows,
    key_rows,
    value_rows,
    gate_rows,
    beta_logit,
    decay_logit,
    residual,
    route_ids,
    route_prob,
    out_weight,
    core_gain,
    moe_gain,
    gate_up,
    down_weight,
    new_home,
):
    req_count = states.shape[0]
    step_count = query_rows.shape[1]
    model_width = residual.shape[-1]
    ep_size = lax.axis_size("ep")
    dp_size = lax.axis_size("dp")
    target = new_home // req_count % ep_size
    new_place = new_home % req_count
    fresh_states, core_out = recurrence(
        target, states, query_rows, key_rows, value_rows, gate_rows, beta_logit, decay_logit, core_gain
    )
    packed_place = jnp.zeros_like(new_place).at[target].set(new_place)
    received = (
        migrate(fresh_states),
        lax.all_to_all(packed_place, "ep", split_axis=0, concat_axis=0, tiled=True),
    )
    moved_out = place_rows(received[0], received[1])
    token_count = req_count * step_count
    core_flat = core_out.reshape(token_count, core_out.shape[-1])
    columns = jnp.dot(
        lax.all_gather(core_flat, "ep", axis=0, tiled=True),
        out_weight,
        preferred_element_type=jnp.float32,
    ).astype(jnp.bfloat16)
    attention = lax.all_to_all(columns, "ep", split_axis=0, concat_axis=1, tiled=True)
    hidden = (
        residual.reshape(token_count, model_width).astype(jnp.float32)
        + attention.astype(jnp.float32)
    ).astype(jnp.bfloat16)
    normed = rms_scale(hidden.astype(jnp.float32), moe_gain).astype(jnp.bfloat16)
    top_count = route_ids.shape[-1]
    experts = dp_size * ep_size
    capacity = (token_count * top_count + experts - 1) // experts + 1
    flat_ids = route_ids.reshape(-1)
    onehot = (flat_ids[:, None] == jnp.arange(experts, dtype=jnp.int32)[None, :]).astype(jnp.int32)
    route_rank = jnp.sum(jnp.cumsum(onehot, axis=0) * onehot, axis=1) - 1
    slot_index = flat_ids * capacity + route_rank
    slot_count = experts * capacity
    match = slot_index[None, :] == jnp.arange(slot_count, dtype=jnp.int32)[:, None]
    match = match.reshape(experts, capacity, token_count, top_count)
    pick = jnp.any(match, axis=-1).astype(jnp.bfloat16)
    lane_count = 128
    chunks = model_width // lane_count
    normed_tiles = normed.reshape(token_count, chunks, lane_count)
    outgoing = jnp.einsum(
        "esk,kcl->escl", pick, normed_tiles, preferred_element_type=jnp.float32
    ).astype(jnp.bfloat16)
    outgoing = outgoing.reshape(experts, capacity * chunks, lane_count)
    arrived = lax.all_to_all(outgoing, ("dp", "ep"), 0, 0, tiled=True)
    arrived = arrived.reshape(experts, capacity, chunks, lane_count)
    hidden_units = down_weight.shape[1]
    gate_tiles = gate_up[0].reshape(chunks, lane_count, gate_up.shape[-1])
    joined = jnp.einsum("escl,clf->esf", arrived, gate_tiles, preferred_element_type=jnp.float32)
    active = (jax.nn.silu(joined[..., :hidden_units]) * joined[..., hidden_units:]).astype(jnp.bfloat16)
    down_tiles = down_weight[0].reshape(hidden_units, chunks, lane_count)
    result = jnp.einsum(
        "esf,fcl->escl", active, down_tiles, preferred_element_type=jnp.float32
    ).astype(jnp.bfloat16)
    result = result.reshape(experts, capacity * chunks, lane_count)
    returned = lax.all_to_all(result, ("dp", "ep"), 0, 0, tiled=True)
    returned = returned.reshape(experts, capacity, chunks, lane_count)
    weights = route_prob.reshape(token_count, top_count)
    weights = weights / jnp.sum(weights, -1, keepdims=True)
    spread = jnp.sum(jnp.where(match, weights[None, None, :, :], 0.0), axis=-1)
    high = spread.astype(jnp.bfloat16)
    rest = spread - high.astype(jnp.float32)
    middle = rest.astype(jnp.bfloat16)
    low = (rest - middle.astype(jnp.float32)).astype(jnp.bfloat16)
    combine = "esk,escl->kcl"
    combined = (
        jnp.einsum(combine, high, returned, preferred_element_type=jnp.float32)
        + jnp.einsum(combine, middle, returned, preferred_element_type=jnp.float32)
    ) + jnp.einsum(combine, low, returned, preferred_element_type=jnp.float32)
    combined = combined.reshape(token_count, model_width)
    mixed_out = (
        (hidden.astype(jnp.float32) + combined)
        .astype(jnp.bfloat16)
        .reshape(req_count, step_count, model_width)
    )
    return (mixed_out, moved_out)


def solution(mesh):
    placed = (
        P(("dp", "ep"), None, None, None),
        P(("dp", "ep"), None, None),
        P(("dp", "ep"), None, None),
        P(("dp", "ep"), None, None),
        P(("dp", "ep"), None, None),
        P(("dp", "ep"), None, None),
        P(("dp", "ep"), None, None),
        P(("dp", "ep"), None, None),
        P(("dp", "ep"), None, None),
        P(("dp", "ep"), None, None),
        P(None, "ep"),
        P(),
        P(),
        P(("dp", "ep"), None, None),
        P(("dp", "ep"), None, None),
        P(("dp", "ep")),
    )
    return jax.shard_map(
        shards,
        mesh=mesh,
        in_specs=placed,
        out_specs=(P(("dp", "ep"), None, None), P(("dp", "ep"), None, None, None)),
        check_vma=False,
    )
```

```python
import jax
import jax.numpy as jnp
from jax import lax
from jax.sharding import PartitionSpec as P

import functools
from jax.experimental import pallas as pl
from jax.experimental.pallas import tpu as pltpu

epsilon = 1e-06
f32 = jnp.float32
bf16 = jnp.bfloat16


def split2(x):
    hi = x.astype(bf16)
    lo = (x - hi.astype(f32)).astype(bf16)
    return hi, lo


def recur_kernel(slot_ref, s_ref, kq_ref, v_ref, g_ref, dec_ref, beta_ref, gain_ref, so_ref, co_ref, n_ref, r_ref, u_ref):
    heads = s_ref.shape[1]
    width = s_ref.shape[-1]
    steps = v_ref.shape[1]
    span = 2 * steps
    kq = kq_ref[0].astype(f32)
    kq = kq * lax.rsqrt(jnp.sum(kq * kq, -1, keepdims=True) + epsilon)
    row = lax.broadcasted_iota(jnp.int32, kq.shape, 0)
    kq = jnp.where(row % span >= steps, kq * width ** (-0.5), kq)
    n_ref[...] = kq
    for h in range(heads):
        p = n_ref[pl.ds(h * span, span), :]
        hi = p.astype(bf16).astype(f32)
        rest = p - hi
        mid = rest.astype(bf16).astype(f32)
        lo = rest - mid
        lhs = jnp.concatenate([hi, mid, lo], axis=0).astype(bf16)
        res = jnp.dot(lhs, s_ref[0, h], preferred_element_type=f32)
        r_ref[pl.ds(h * span, span), :] = (res[0:span] + res[span:2 * span]) + res[2 * span:3 * span]
    decay = jax.nn.sigmoid(dec_ref[0])
    strength = jax.nn.sigmoid(beta_ref[0])
    gain = gain_ref[...]
    keys = [n_ref[pl.ds(t, heads, stride=span), :] for t in range(steps)]
    queries = [n_ref[pl.ds(steps + t, heads, stride=span), :] for t in range(steps)]
    u_ref[...] = jnp.zeros(u_ref.shape, f32)
    updates = []
    carried = []
    total = None
    for t in range(steps):
        a_t = decay[:, t:t + 1]
        b_t = strength[:, t:t + 1]
        total = a_t if t == 0 else total * a_t
        carried = [c * a_t for c in carried]
        memory = total * r_ref[pl.ds(t, heads, stride=span), :]
        for j in range(t):
            kk = jnp.sum(keys[j] * keys[t], -1, keepdims=True)
            memory = memory + (carried[j] * kk) * updates[j]
        values = v_ref[0, t].astype(f32)
        update = (values - memory) * b_t
        updates.append(update)
        carried.append(jnp.ones_like(a_t))
        reading = total * r_ref[pl.ds(steps + t, heads, stride=span), :]
        for j in range(t + 1):
            qk = jnp.sum(keys[j] * queries[t], -1, keepdims=True)
            coef = qk if j == t else carried[j] * qk
            reading = reading + coef * updates[j]
        scaled = reading * lax.rsqrt(jnp.mean(reading * reading, -1, keepdims=True) + epsilon)
        gate_vals = g_ref[0, t].astype(f32)
        co_ref[0, t] = (scaled * gain * (gate_vals * jax.nn.sigmoid(gate_vals))).astype(co_ref.dtype)
    for j in range(steps):
        u_ref[pl.ds(j, heads, stride=span), :] = carried[j] * updates[j]
    for h in range(heads):
        kt = n_ref[pl.ds(h * span, span), :].T
        w = u_ref[pl.ds(h * span, span), :]
        k_hi, k_lo = split2(kt)
        w_hi, w_lo = split2(w)
        delta = (
            jnp.dot(k_hi, w_hi, preferred_element_type=f32)
            + jnp.dot(k_hi, w_lo, preferred_element_type=f32)
            + jnp.dot(k_lo, w_hi, preferred_element_type=f32)
        )
        so_ref[0, h] = (total[h:h + 1, :] * s_ref[0, h].astype(f32) + delta).astype(so_ref.dtype)


def recurrence(slots, states, query_rows, key_rows, value_rows, gate_rows, beta_logit, decay_logit, core_gain):
    batch, heads, width, _ = states.shape
    steps = query_rows.shape[1]
    key_heads = query_rows.shape[-1] // width
    repeats = heads // key_heads
    span = 2 * steps
    kq = jnp.concatenate(
        [key_rows.reshape(batch, steps, key_heads, width), query_rows.reshape(batch, steps, key_heads, width)], axis=1
    )
    kq = jnp.repeat(kq.transpose(0, 2, 1, 3), repeats, axis=1).reshape(batch, heads * span, width)
    values = value_rows.reshape(batch, steps, heads, width)
    gates = gate_rows.reshape(batch, steps, heads, width)
    decay = decay_logit.astype(f32).transpose(0, 2, 1)
    beta = beta_logit.astype(f32).transpose(0, 2, 1)
    gain = core_gain.reshape(1, width)
    state_in = pl.BlockSpec((1, heads, width, width), lambda i, slot: (i, 0, 0, 0))
    state_out = pl.BlockSpec((1, heads, width, width), lambda i, slot: (slot[i], 0, 0, 0))
    row_spec = pl.BlockSpec((1, steps, heads, width), lambda i, slot: (i, 0, 0, 0))
    coef_spec = pl.BlockSpec((1, heads, steps), lambda i, slot: (i, 0, 0))
    fresh, core = pl.pallas_call(
        recur_kernel,
        grid_spec=pltpu.PrefetchScalarGridSpec(
            num_scalar_prefetch=1,
            grid=(batch,),
            in_specs=[
                state_in,
                pl.BlockSpec((1, heads * span, width), lambda i, slot: (i, 0, 0)),
                row_spec,
                row_spec,
                coef_spec,
                coef_spec,
                pl.BlockSpec((1, width), lambda i, slot: (0, 0)),
            ],
            out_specs=[state_out, row_spec],
            scratch_shapes=[pltpu.VMEM((heads * span, width), f32)] * 3,
        ),
        out_shape=[
            jax.ShapeDtypeStruct(states.shape, bf16),
            jax.ShapeDtypeStruct((batch, steps, heads, width), bf16),
        ],
    )(slots, states, kq, values, gates, decay, beta, gain)
    return fresh, core.reshape(batch, steps, heads * width)


def unit_rows(values):
    return values * lax.rsqrt(jnp.sum(values * values, -1, keepdims=True) + epsilon)


def delta_block(
    state_in, query_rows, key_rows, value_rows, gate_rows, beta_logit, decay_logit, core_gain
):
    batch_size = state_in.shape[0]
    head_count = decay_logit.shape[-1]
    head_width = state_in.shape[-1]
    key_heads = query_rows.shape[-1] // head_width
    repeats = head_count // key_heads
    memory_state = state_in.astype(jnp.float32)
    outputs = []
    for position in range(query_rows.shape[1]):
        queries = unit_rows(
            query_rows[:, position].astype(jnp.float32).reshape(batch_size, key_heads, head_width)
        )
        queries = jnp.repeat(queries, repeats, axis=1) * head_width ** (-0.5)
        key_units = unit_rows(
            key_rows[:, position].astype(jnp.float32).reshape(batch_size, key_heads, head_width)
        )
        key_units = jnp.repeat(key_units, repeats, axis=1)
        values = (
            value_rows[:, position].astype(jnp.float32).reshape(batch_size, head_count, head_width)
        )
        decays = jax.nn.sigmoid(decay_logit[:, position].astype(jnp.float32))
        strength = jax.nn.sigmoid(beta_logit[:, position].astype(jnp.float32))
        memory_state = memory_state * decays[:, :, None, None]
        memory = jnp.einsum(
            "bhkv,bhk->bhv", memory_state, key_units, precision=lax.Precision.HIGHEST
        )
        update = (values - memory) * strength[:, :, None]
        memory_state = memory_state + key_units[:, :, :, None] * update[:, :, None, :]
        reading = jnp.einsum(
            "bhkv,bhk->bhv", memory_state, queries, precision=lax.Precision.HIGHEST
        )
        scaled = reading * lax.rsqrt(jnp.mean(reading * reading, -1, keepdims=True) + epsilon)
        gate_vals = (
            gate_rows[:, position].astype(jnp.float32).reshape(batch_size, head_count, head_width)
        )
        gated_out = scaled * core_gain * jax.nn.silu(gate_vals)
        outputs.append(gated_out.reshape(batch_size, head_count * head_width).astype(jnp.bfloat16))
    return (memory_state.astype(jnp.bfloat16), jnp.stack(outputs, axis=1))


def migrate_kernel(src_hbm, dst_hbm, send_sem, recv_sem, local_sem):
    lanes = src_hbm.shape[0]
    group = lax.axis_index("dp")
    me = lax.axis_index("ep")
    mesh_ids = pl.DeviceIdType.MESH
    barrier = pltpu.get_barrier_semaphore()
    for i in range(1, lanes):
        pl.semaphore_signal(barrier, 1, device_id=(group, lax.rem(me + i, lanes)), device_id_type=mesh_ids)
    pl.semaphore_wait(barrier, lanes - 1)
    own = pltpu.make_async_copy(src_hbm.at[me], dst_hbm.at[me], local_sem)
    own.start()
    copies = []
    for i in range(1, lanes):
        peer = lax.rem(me + i, lanes)
        copy = pltpu.make_async_remote_copy(
            src_hbm.at[peer],
            dst_hbm.at[me],
            send_sem.at[i - 1],
            recv_sem.at[i - 1],
            device_id=(group, peer),
            device_id_type=mesh_ids,
        )
        copy.start()
        copies.append(copy)
    own.wait()
    for copy in copies:
        copy.wait()


def migrate(rows):
    lanes = rows.shape[0]
    any_spec = pl.BlockSpec(memory_space=pl.ANY)
    return pl.pallas_call(
        migrate_kernel,
        in_specs=[any_spec],
        out_specs=any_spec,
        out_shape=jax.ShapeDtypeStruct(rows.shape, rows.dtype),
        scratch_shapes=[
            pltpu.SemaphoreType.DMA((lanes - 1,)),
            pltpu.SemaphoreType.DMA((lanes - 1,)),
            pltpu.SemaphoreType.DMA,
        ],
        compiler_params=pltpu.CompilerParams(collective_id=0, has_side_effects=True),
        cost_estimate=pl.CostEstimate(flops=0, transcendentals=0, bytes_accessed=2 * rows.size * rows.dtype.itemsize),
    )(rows)


def project_kernel(rows_ref, weight_ref, out_ref, gathered, product, send_a, recv_a, send_b, recv_b, local_sem):
    lanes = gathered.shape[0]
    count = rows_ref.shape[0]
    block = weight_ref.shape[1]
    group = lax.axis_index("dp")
    me = lax.axis_index("ep")
    mesh_ids = pl.DeviceIdType.MESH
    barrier = pltpu.get_barrier_semaphore()
    for i in range(1, lanes):
        pl.semaphore_signal(barrier, 1, device_id=(group, lax.rem(me + i, lanes)), device_id_type=mesh_ids)
    pl.semaphore_wait(barrier, lanes - 1)
    own = pltpu.make_async_copy(rows_ref, gathered.at[me], local_sem)
    own.start()
    sends = []
    for i in range(1, lanes):
        copy = pltpu.make_async_remote_copy(
            rows_ref, gathered.at[me], send_a.at[i - 1], recv_a.at[i - 1],
            device_id=(group, lax.rem(me + i, lanes)), device_id_type=mesh_ids,
        )
        copy.start()
        sends.append(copy)
    own.wait()
    for copy in sends:
        copy.wait()
    for j in range(lanes):
        product[j] = jnp.dot(gathered[j], weight_ref[...], preferred_element_type=jnp.float32).astype(product.dtype)
    columns = pl.ds(pl.multiple_of(me * block, block), block)
    back = pltpu.make_async_copy(product.at[me], out_ref.at[:, columns], local_sem)
    back.start()
    replies = []
    for i in range(1, lanes):
        peer = lax.rem(me + i, lanes)
        copy = pltpu.make_async_remote_copy(
            product.at[peer], out_ref.at[:, columns], send_b.at[i - 1], recv_b.at[i - 1],
            device_id=(group, peer), device_id_type=mesh_ids,
        )
        copy.start()
        replies.append(copy)
    back.wait()
    for copy in replies:
        copy.wait()


def project(rows, weight):
    lanes = lax.axis_size("ep")
    count, width = rows.shape
    block = weight.shape[1]
    vmem = pl.BlockSpec(memory_space=pltpu.VMEM)
    return pl.pallas_call(
        project_kernel,
        in_specs=[vmem, vmem],
        out_specs=vmem,
        out_shape=jax.ShapeDtypeStruct((count, lanes * block), rows.dtype),
        scratch_shapes=[
            pltpu.VMEM((lanes, count, width), rows.dtype),
            pltpu.VMEM((lanes, count, block), rows.dtype),
            pltpu.SemaphoreType.DMA((lanes - 1,)),
            pltpu.SemaphoreType.DMA((lanes - 1,)),
            pltpu.SemaphoreType.DMA((lanes - 1,)),
            pltpu.SemaphoreType.DMA((lanes - 1,)),
            pltpu.SemaphoreType.DMA,
        ],
        compiler_params=pltpu.CompilerParams(collective_id=1, has_side_effects=True),
    )(rows, weight)


def place_kernel(place_ref, in_ref, out_ref):
    out_ref[...] = in_ref[...]


def place_rows(rows, places):
    block = (1,) + rows.shape[1:]
    tail = (0,) * (rows.ndim - 1)
    return pl.pallas_call(
        place_kernel,
        grid_spec=pltpu.PrefetchScalarGridSpec(
            num_scalar_prefetch=1,
            grid=(rows.shape[0],),
            in_specs=[pl.BlockSpec(block, lambda j, place: (j,) + tail)],
            out_specs=pl.BlockSpec(block, lambda j, place: (place[j],) + tail),
        ),
        out_shape=jax.ShapeDtypeStruct(rows.shape, rows.dtype),
    )(places, rows)


def rms_scale(values, gain):
    return values * lax.rsqrt(jnp.mean(values * values, -1, keepdims=True) + epsilon) * gain


def expert_apply(chosen_rows, gate_up, down_weight):
    hidden_units = down_weight.shape[0]
    joined = jnp.dot(chosen_rows, gate_up, preferred_element_type=jnp.float32)
    active = (jax.nn.silu(joined[:, :hidden_units]) * joined[:, hidden_units:]).astype(jnp.bfloat16)
    return jnp.dot(active, down_weight, preferred_element_type=jnp.float32).astype(jnp.bfloat16)


def pack(values, positions, lane_count):
    zeroed = jnp.zeros(values.shape, values.dtype)
    placed = zeroed.at[positions].set(values)
    return placed.reshape((lane_count, values.shape[0] // lane_count) + values.shape[1:])


def unpack(values):
    return values.reshape((values.shape[0] * values.shape[1],) + values.shape[2:])


def shards(
    states,
    query_rows,
    key_rows,
    value_rows,
    gate_rows,
    beta_logit,
    decay_logit,
    residual,
    route_ids,
    route_prob,
    out_weight,
    core_gain,
    moe_gain,
    gate_up,
    down_weight,
    new_home,
):
    req_count = states.shape[0]
    step_count = query_rows.shape[1]
    model_width = residual.shape[-1]
    ep_size = lax.axis_size("ep")
    dp_size = lax.axis_size("dp")
    target = new_home // req_count % ep_size
    new_place = new_home % req_count
    fresh_states, core_out = recurrence(
        target, states, query_rows, key_rows, value_rows, gate_rows, beta_logit, decay_logit, core_gain
    )
    packed_place = jnp.zeros_like(new_place).at[target].set(new_place)
    received = (
        migrate(fresh_states),
        lax.all_to_all(packed_place, "ep", split_axis=0, concat_axis=0, tiled=True),
    )
    moved_out = place_rows(received[0], received[1])
    token_count = req_count * step_count
    core_flat = core_out.reshape(token_count, core_out.shape[-1])
    attention = project(core_flat, out_weight)
    hidden = (
        residual.reshape(token_count, model_width).astype(jnp.float32)
        + attention.astype(jnp.float32)
    ).astype(jnp.bfloat16)
    normed = rms_scale(hidden.astype(jnp.float32), moe_gain).astype(jnp.bfloat16)
    top_count = route_ids.shape[-1]
    experts = dp_size * ep_size
    capacity = (token_count * top_count + experts - 1) // experts + 1
    flat_ids = route_ids.reshape(-1)
    onehot = (flat_ids[:, None] == jnp.arange(experts, dtype=jnp.int32)[None, :]).astype(jnp.int32)
    route_rank = jnp.sum(jnp.cumsum(onehot, axis=0) * onehot, axis=1) - 1
    slot_index = flat_ids * capacity + route_rank
    slot_count = experts * capacity
    match = slot_index[None, :] == jnp.arange(slot_count, dtype=jnp.int32)[:, None]
    match = match.reshape(experts, capacity, token_count, top_count)
    pick = jnp.any(match, axis=-1).astype(jnp.bfloat16)
    lane_count = 128
    chunks = model_width // lane_count
    normed_tiles = normed.reshape(token_count, chunks, lane_count)
    outgoing = jnp.einsum(
        "esk,kcl->escl", pick, normed_tiles, preferred_element_type=jnp.float32
    ).astype(jnp.bfloat16)
    outgoing = outgoing.reshape(experts, capacity * chunks, lane_count)
    arrived = lax.all_to_all(outgoing, ("dp", "ep"), 0, 0, tiled=True)
    arrived = arrived.reshape(experts, capacity, chunks, lane_count)
    hidden_units = down_weight.shape[1]
    gate_tiles = gate_up[0].reshape(chunks, lane_count, gate_up.shape[-1])
    joined = jnp.einsum("escl,clf->esf", arrived, gate_tiles, preferred_element_type=jnp.float32)
    active = (jax.nn.silu(joined[..., :hidden_units]) * joined[..., hidden_units:]).astype(jnp.bfloat16)
    down_tiles = down_weight[0].reshape(hidden_units, chunks, lane_count)
    result = jnp.einsum(
        "esf,fcl->escl", active, down_tiles, preferred_element_type=jnp.float32
    ).astype(jnp.bfloat16)
    result = result.reshape(experts, capacity * chunks, lane_count)
    returned = lax.all_to_all(result, ("dp", "ep"), 0, 0, tiled=True)
    returned = returned.reshape(experts, capacity, chunks, lane_count)
    weights = route_prob.reshape(token_count, top_count)
    weights = weights / jnp.sum(weights, -1, keepdims=True)
    spread = jnp.sum(jnp.where(match, weights[None, None, :, :], 0.0), axis=-1)
    high = spread.astype(jnp.bfloat16)
    rest = spread - high.astype(jnp.float32)
    middle = rest.astype(jnp.bfloat16)
    low = (rest - middle.astype(jnp.float32)).astype(jnp.bfloat16)
    combine = "esk,escl->kcl"
    combined = (
        jnp.einsum(combine, high, returned, preferred_element_type=jnp.float32)
        + jnp.einsum(combine, middle, returned, preferred_element_type=jnp.float32)
    ) + jnp.einsum(combine, low, returned, preferred_element_type=jnp.float32)
    combined = combined.reshape(token_count, model_width)
    mixed_out = (
        (hidden.astype(jnp.float32) + combined)
        .astype(jnp.bfloat16)
        .reshape(req_count, step_count, model_width)
    )
    return (mixed_out, moved_out)


def solution(mesh):
    placed = (
        P(("dp", "ep"), None, None, None),
        P(("dp", "ep"), None, None),
        P(("dp", "ep"), None, None),
        P(("dp", "ep"), None, None),
        P(("dp", "ep"), None, None),
        P(("dp", "ep"), None, None),
        P(("dp", "ep"), None, None),
        P(("dp", "ep"), None, None),
        P(("dp", "ep"), None, None),
        P(("dp", "ep"), None, None),
        P(None, "ep"),
        P(),
        P(),
        P(("dp", "ep"), None, None),
        P(("dp", "ep"), None, None),
        P(("dp", "ep")),
    )
    return jax.shard_map(
        shards,
        mesh=mesh,
        in_specs=placed,
        out_specs=(P(("dp", "ep"), None, None), P(("dp", "ep"), None, None, None)),
        check_vma=False,
    )
```

```python
import jax
import jax.numpy as jnp
from jax import lax
from jax.sharding import PartitionSpec as P

import functools
from jax.experimental import pallas as pl
from jax.experimental.pallas import tpu as pltpu

epsilon = 1e-06
f32 = jnp.float32
bf16 = jnp.bfloat16


def split2(x):
    hi = x.astype(bf16)
    lo = (x - hi.astype(f32)).astype(bf16)
    return hi, lo


def recur_kernel(slot_ref, s_ref, kq_ref, v_ref, g_ref, dec_ref, beta_ref, gain_ref, so_ref, co_ref, n_ref, r_ref, u_ref):
    heads = s_ref.shape[1]
    width = s_ref.shape[-1]
    steps = v_ref.shape[1]
    span = 2 * steps
    kq = kq_ref[0].astype(f32)
    kq = kq * lax.rsqrt(jnp.sum(kq * kq, -1, keepdims=True) + epsilon)
    row = lax.broadcasted_iota(jnp.int32, kq.shape, 0)
    kq = jnp.where(row % span >= steps, kq * width ** (-0.5), kq)
    n_ref[...] = kq
    for h in range(heads):
        p = n_ref[pl.ds(h * span, span), :]
        hi = p.astype(bf16).astype(f32)
        rest = p - hi
        mid = rest.astype(bf16).astype(f32)
        lo = rest - mid
        lhs = jnp.concatenate([hi, mid, lo], axis=0).astype(bf16)
        res = jnp.dot(lhs, s_ref[0, h], preferred_element_type=f32)
        r_ref[pl.ds(h * span, span), :] = (res[0:span] + res[span:2 * span]) + res[2 * span:3 * span]
    decay = jax.nn.sigmoid(dec_ref[0])
    strength = jax.nn.sigmoid(beta_ref[0])
    gain = gain_ref[...]
    keys = [n_ref[pl.ds(t, heads, stride=span), :] for t in range(steps)]
    queries = [n_ref[pl.ds(steps + t, heads, stride=span), :] for t in range(steps)]
    u_ref[...] = jnp.zeros(u_ref.shape, f32)
    updates = []
    carried = []
    total = None
    for t in range(steps):
        a_t = decay[:, t:t + 1]
        b_t = strength[:, t:t + 1]
        total = a_t if t == 0 else total * a_t
        carried = [c * a_t for c in carried]
        memory = total * r_ref[pl.ds(t, heads, stride=span), :]
        for j in range(t):
            kk = jnp.sum(keys[j] * keys[t], -1, keepdims=True)
            memory = memory + (carried[j] * kk) * updates[j]
        values = v_ref[0, t].astype(f32)
        update = (values - memory) * b_t
        updates.append(update)
        carried.append(jnp.ones_like(a_t))
        reading = total * r_ref[pl.ds(steps + t, heads, stride=span), :]
        for j in range(t + 1):
            qk = jnp.sum(keys[j] * queries[t], -1, keepdims=True)
            coef = qk if j == t else carried[j] * qk
            reading = reading + coef * updates[j]
        scaled = reading * lax.rsqrt(jnp.mean(reading * reading, -1, keepdims=True) + epsilon)
        gate_vals = g_ref[0, t].astype(f32)
        co_ref[0, t] = (scaled * gain * (gate_vals * jax.nn.sigmoid(gate_vals))).astype(co_ref.dtype)
    for j in range(steps):
        u_ref[pl.ds(j, heads, stride=span), :] = carried[j] * updates[j]
    for h in range(heads):
        kt = n_ref[pl.ds(h * span, span), :].T
        w = u_ref[pl.ds(h * span, span), :]
        k_hi, k_lo = split2(kt)
        w_hi, w_lo = split2(w)
        delta = (
            jnp.dot(k_hi, w_hi, preferred_element_type=f32)
            + jnp.dot(k_hi, w_lo, preferred_element_type=f32)
            + jnp.dot(k_lo, w_hi, preferred_element_type=f32)
        )
        so_ref[0, h] = (total[h:h + 1, :] * s_ref[0, h].astype(f32) + delta).astype(so_ref.dtype)


def recurrence(slots, states, query_rows, key_rows, value_rows, gate_rows, beta_logit, decay_logit, core_gain):
    batch, heads, width, _ = states.shape
    steps = query_rows.shape[1]
    key_heads = query_rows.shape[-1] // width
    repeats = heads // key_heads
    span = 2 * steps
    kq = jnp.concatenate(
        [key_rows.reshape(batch, steps, key_heads, width), query_rows.reshape(batch, steps, key_heads, width)], axis=1
    )
    kq = jnp.repeat(kq.transpose(0, 2, 1, 3), repeats, axis=1).reshape(batch, heads * span, width)
    values = value_rows.reshape(batch, steps, heads, width)
    gates = gate_rows.reshape(batch, steps, heads, width)
    decay = decay_logit.astype(f32).transpose(0, 2, 1)
    beta = beta_logit.astype(f32).transpose(0, 2, 1)
    gain = core_gain.reshape(1, width)
    state_in = pl.BlockSpec((1, heads, width, width), lambda i, slot: (i, 0, 0, 0))
    state_out = pl.BlockSpec((1, heads, width, width), lambda i, slot: (slot[i], 0, 0, 0))
    row_spec = pl.BlockSpec((1, steps, heads, width), lambda i, slot: (i, 0, 0, 0))
    coef_spec = pl.BlockSpec((1, heads, steps), lambda i, slot: (i, 0, 0))
    fresh, core = pl.pallas_call(
        recur_kernel,
        grid_spec=pltpu.PrefetchScalarGridSpec(
            num_scalar_prefetch=1,
            grid=(batch,),
            in_specs=[
                state_in,
                pl.BlockSpec((1, heads * span, width), lambda i, slot: (i, 0, 0)),
                row_spec,
                row_spec,
                coef_spec,
                coef_spec,
                pl.BlockSpec((1, width), lambda i, slot: (0, 0)),
            ],
            out_specs=[state_out, row_spec],
            scratch_shapes=[pltpu.VMEM((heads * span, width), f32)] * 3,
        ),
        out_shape=[
            jax.ShapeDtypeStruct(states.shape, bf16),
            jax.ShapeDtypeStruct((batch, steps, heads, width), bf16),
        ],
    )(slots, states, kq, values, gates, decay, beta, gain)
    return fresh, core.reshape(batch, steps, heads * width)


def unit_rows(values):
    return values * lax.rsqrt(jnp.sum(values * values, -1, keepdims=True) + epsilon)


def delta_block(
    state_in, query_rows, key_rows, value_rows, gate_rows, beta_logit, decay_logit, core_gain
):
    batch_size = state_in.shape[0]
    head_count = decay_logit.shape[-1]
    head_width = state_in.shape[-1]
    key_heads = query_rows.shape[-1] // head_width
    repeats = head_count // key_heads
    memory_state = state_in.astype(jnp.float32)
    outputs = []
    for position in range(query_rows.shape[1]):
        queries = unit_rows(
            query_rows[:, position].astype(jnp.float32).reshape(batch_size, key_heads, head_width)
        )
        queries = jnp.repeat(queries, repeats, axis=1) * head_width ** (-0.5)
        key_units = unit_rows(
            key_rows[:, position].astype(jnp.float32).reshape(batch_size, key_heads, head_width)
        )
        key_units = jnp.repeat(key_units, repeats, axis=1)
        values = (
            value_rows[:, position].astype(jnp.float32).reshape(batch_size, head_count, head_width)
        )
        decays = jax.nn.sigmoid(decay_logit[:, position].astype(jnp.float32))
        strength = jax.nn.sigmoid(beta_logit[:, position].astype(jnp.float32))
        memory_state = memory_state * decays[:, :, None, None]
        memory = jnp.einsum(
            "bhkv,bhk->bhv", memory_state, key_units, precision=lax.Precision.HIGHEST
        )
        update = (values - memory) * strength[:, :, None]
        memory_state = memory_state + key_units[:, :, :, None] * update[:, :, None, :]
        reading = jnp.einsum(
            "bhkv,bhk->bhv", memory_state, queries, precision=lax.Precision.HIGHEST
        )
        scaled = reading * lax.rsqrt(jnp.mean(reading * reading, -1, keepdims=True) + epsilon)
        gate_vals = (
            gate_rows[:, position].astype(jnp.float32).reshape(batch_size, head_count, head_width)
        )
        gated_out = scaled * core_gain * jax.nn.silu(gate_vals)
        outputs.append(gated_out.reshape(batch_size, head_count * head_width).astype(jnp.bfloat16))
    return (memory_state.astype(jnp.bfloat16), jnp.stack(outputs, axis=1))


def migrate_kernel(src_hbm, dst_hbm, send_sem, recv_sem, local_sem):
    lanes = src_hbm.shape[0]
    group = lax.axis_index("dp")
    me = lax.axis_index("ep")
    mesh_ids = pl.DeviceIdType.MESH
    barrier = pltpu.get_barrier_semaphore()
    for i in range(1, lanes):
        pl.semaphore_signal(barrier, 1, device_id=(group, lax.rem(me + i, lanes)), device_id_type=mesh_ids)
    pl.semaphore_wait(barrier, lanes - 1)
    own = pltpu.make_async_copy(src_hbm.at[me], dst_hbm.at[me], local_sem)
    own.start()
    copies = []
    for i in range(1, lanes):
        peer = lax.rem(me + i, lanes)
        copy = pltpu.make_async_remote_copy(
            src_hbm.at[peer],
            dst_hbm.at[me],
            send_sem.at[i - 1],
            recv_sem.at[i - 1],
            device_id=(group, peer),
            device_id_type=mesh_ids,
        )
        copy.start()
        copies.append(copy)
    own.wait()
    for copy in copies:
        copy.wait()


def migrate(rows):
    lanes = rows.shape[0]
    any_spec = pl.BlockSpec(memory_space=pl.ANY)
    return pl.pallas_call(
        migrate_kernel,
        in_specs=[any_spec],
        out_specs=any_spec,
        out_shape=jax.ShapeDtypeStruct(rows.shape, rows.dtype),
        scratch_shapes=[
            pltpu.SemaphoreType.DMA((lanes - 1,)),
            pltpu.SemaphoreType.DMA((lanes - 1,)),
            pltpu.SemaphoreType.DMA,
        ],
        compiler_params=pltpu.CompilerParams(collective_id=0, has_side_effects=True),
        cost_estimate=pl.CostEstimate(flops=0, transcendentals=0, bytes_accessed=2 * rows.size * rows.dtype.itemsize),
    )(rows)


def project_kernel(rows_ref, weight_ref, out_ref, gathered, product, send_a, recv_a, send_b, recv_b, local_sem):
    lanes = gathered.shape[0]
    count = rows_ref.shape[0]
    block = weight_ref.shape[1]
    group = lax.axis_index("dp")
    me = lax.axis_index("ep")
    mesh_ids = pl.DeviceIdType.MESH
    barrier = pltpu.get_barrier_semaphore()
    for i in range(1, lanes):
        pl.semaphore_signal(barrier, 1, device_id=(group, lax.rem(me + i, lanes)), device_id_type=mesh_ids)
    pl.semaphore_wait(barrier, lanes - 1)
    own = pltpu.make_async_copy(rows_ref, gathered.at[me], local_sem)
    own.start()
    sends = []
    for i in range(1, lanes):
        copy = pltpu.make_async_remote_copy(
            rows_ref, gathered.at[me], send_a.at[i - 1], recv_a.at[i - 1],
            device_id=(group, lax.rem(me + i, lanes)), device_id_type=mesh_ids,
        )
        copy.start()
        sends.append(copy)
    own.wait()
    for copy in sends:
        copy.wait()
    width = gathered.shape[-1]
    stacked = gathered[...].reshape(lanes * count, width)
    product[...] = (
        jnp.dot(stacked, weight_ref[...], preferred_element_type=jnp.float32)
        .astype(product.dtype)
        .reshape(lanes, count, block)
    )
    columns = pl.ds(pl.multiple_of(me * block, block), block)
    back = pltpu.make_async_copy(product.at[me], out_ref.at[:, columns], local_sem)
    back.start()
    replies = []
    for i in range(1, lanes):
        peer = lax.rem(me + i, lanes)
        copy = pltpu.make_async_remote_copy(
            product.at[peer], out_ref.at[:, columns], send_b.at[i - 1], recv_b.at[i - 1],
            device_id=(group, peer), device_id_type=mesh_ids,
        )
        copy.start()
        replies.append(copy)
    back.wait()
    for copy in replies:
        copy.wait()


def project(rows, weight):
    lanes = lax.axis_size("ep")
    count, width = rows.shape
    block = weight.shape[1]
    vmem = pl.BlockSpec(memory_space=pltpu.VMEM)
    return pl.pallas_call(
        project_kernel,
        in_specs=[vmem, vmem],
        out_specs=vmem,
        out_shape=jax.ShapeDtypeStruct((count, lanes * block), rows.dtype),
        scratch_shapes=[
            pltpu.VMEM((lanes, count, width), rows.dtype),
            pltpu.VMEM((lanes, count, block), rows.dtype),
            pltpu.SemaphoreType.DMA((lanes - 1,)),
            pltpu.SemaphoreType.DMA((lanes - 1,)),
            pltpu.SemaphoreType.DMA((lanes - 1,)),
            pltpu.SemaphoreType.DMA((lanes - 1,)),
            pltpu.SemaphoreType.DMA,
        ],
        compiler_params=pltpu.CompilerParams(collective_id=1, has_side_effects=True),
    )(rows, weight)


def place_kernel(place_ref, in_ref, out_ref):
    out_ref[...] = in_ref[...]


def place_rows(rows, places):
    block = (1,) + rows.shape[1:]
    tail = (0,) * (rows.ndim - 1)
    return pl.pallas_call(
        place_kernel,
        grid_spec=pltpu.PrefetchScalarGridSpec(
            num_scalar_prefetch=1,
            grid=(rows.shape[0],),
            in_specs=[pl.BlockSpec(block, lambda j, place: (j,) + tail)],
            out_specs=pl.BlockSpec(block, lambda j, place: (place[j],) + tail),
        ),
        out_shape=jax.ShapeDtypeStruct(rows.shape, rows.dtype),
    )(places, rows)


def rms_scale(values, gain):
    return values * lax.rsqrt(jnp.mean(values * values, -1, keepdims=True) + epsilon) * gain


def expert_apply(chosen_rows, gate_up, down_weight):
    hidden_units = down_weight.shape[0]
    joined = jnp.dot(chosen_rows, gate_up, preferred_element_type=jnp.float32)
    active = (jax.nn.silu(joined[:, :hidden_units]) * joined[:, hidden_units:]).astype(jnp.bfloat16)
    return jnp.dot(active, down_weight, preferred_element_type=jnp.float32).astype(jnp.bfloat16)


def pack(values, positions, lane_count):
    zeroed = jnp.zeros(values.shape, values.dtype)
    placed = zeroed.at[positions].set(values)
    return placed.reshape((lane_count, values.shape[0] // lane_count) + values.shape[1:])


def unpack(values):
    return values.reshape((values.shape[0] * values.shape[1],) + values.shape[2:])


def shards(
    states,
    query_rows,
    key_rows,
    value_rows,
    gate_rows,
    beta_logit,
    decay_logit,
    residual,
    route_ids,
    route_prob,
    out_weight,
    core_gain,
    moe_gain,
    gate_up,
    down_weight,
    new_home,
):
    req_count = states.shape[0]
    step_count = query_rows.shape[1]
    model_width = residual.shape[-1]
    ep_size = lax.axis_size("ep")
    dp_size = lax.axis_size("dp")
    target = new_home // req_count % ep_size
    new_place = new_home % req_count
    fresh_states, core_out = recurrence(
        target, states, query_rows, key_rows, value_rows, gate_rows, beta_logit, decay_logit, core_gain
    )
    packed_place = jnp.zeros_like(new_place).at[target].set(new_place)
    received = (
        migrate(fresh_states),
        lax.all_to_all(packed_place, "ep", split_axis=0, concat_axis=0, tiled=True),
    )
    moved_out = place_rows(received[0], received[1])
    token_count = req_count * step_count
    core_flat = core_out.reshape(token_count, core_out.shape[-1])
    attention = project(core_flat, out_weight)
    hidden = (
        residual.reshape(token_count, model_width).astype(jnp.float32)
        + attention.astype(jnp.float32)
    ).astype(jnp.bfloat16)
    normed = rms_scale(hidden.astype(jnp.float32), moe_gain).astype(jnp.bfloat16)
    top_count = route_ids.shape[-1]
    experts = dp_size * ep_size
    capacity = (token_count * top_count + experts - 1) // experts + 1
    flat_ids = route_ids.reshape(-1)
    onehot = (flat_ids[:, None] == jnp.arange(experts, dtype=jnp.int32)[None, :]).astype(jnp.int32)
    route_rank = jnp.sum(jnp.cumsum(onehot, axis=0) * onehot, axis=1) - 1
    slot_index = flat_ids * capacity + route_rank
    slot_count = experts * capacity
    match = slot_index[None, :] == jnp.arange(slot_count, dtype=jnp.int32)[:, None]
    match = match.reshape(experts, capacity, token_count, top_count)
    pick = jnp.any(match, axis=-1).astype(jnp.bfloat16)
    lane_count = 128
    chunks = model_width // lane_count
    normed_tiles = normed.reshape(token_count, chunks, lane_count)
    outgoing = jnp.einsum(
        "esk,kcl->escl", pick, normed_tiles, preferred_element_type=jnp.float32
    ).astype(jnp.bfloat16)
    outgoing = outgoing.reshape(experts, capacity * chunks, lane_count)
    arrived = lax.all_to_all(outgoing, ("dp", "ep"), 0, 0, tiled=True)
    arrived = arrived.reshape(experts, capacity, chunks, lane_count)
    hidden_units = down_weight.shape[1]
    gate_tiles = gate_up[0].reshape(chunks, lane_count, gate_up.shape[-1])
    joined = jnp.einsum("escl,clf->esf", arrived, gate_tiles, preferred_element_type=jnp.float32)
    active = (jax.nn.silu(joined[..., :hidden_units]) * joined[..., hidden_units:]).astype(jnp.bfloat16)
    down_tiles = down_weight[0].reshape(hidden_units, chunks, lane_count)
    result = jnp.einsum(
        "esf,fcl->escl", active, down_tiles, preferred_element_type=jnp.float32
    ).astype(jnp.bfloat16)
    result = result.reshape(experts, capacity * chunks, lane_count)
    returned = lax.all_to_all(result, ("dp", "ep"), 0, 0, tiled=True)
    returned = returned.reshape(experts, capacity, chunks, lane_count)
    weights = route_prob.reshape(token_count, top_count)
    weights = weights / jnp.sum(weights, -1, keepdims=True)
    spread = jnp.sum(jnp.where(match, weights[None, None, :, :], 0.0), axis=-1)
    high = spread.astype(jnp.bfloat16)
    rest = spread - high.astype(jnp.float32)
    middle = rest.astype(jnp.bfloat16)
    low = (rest - middle.astype(jnp.float32)).astype(jnp.bfloat16)
    parts = jnp.concatenate([high, middle, low], axis=-1)
    combined = jnp.einsum("esk,escl->kcl", parts, returned, preferred_element_type=jnp.float32)
    combined = combined.reshape(3, token_count, chunks, lane_count).sum(axis=0)
    combined = combined.reshape(token_count, model_width)
    mixed_out = (
        (hidden.astype(jnp.float32) + combined)
        .astype(jnp.bfloat16)
        .reshape(req_count, step_count, model_width)
    )
    return (mixed_out, moved_out)


def solution(mesh):
    placed = (
        P(("dp", "ep"), None, None, None),
        P(("dp", "ep"), None, None),
        P(("dp", "ep"), None, None),
        P(("dp", "ep"), None, None),
        P(("dp", "ep"), None, None),
        P(("dp", "ep"), None, None),
        P(("dp", "ep"), None, None),
        P(("dp", "ep"), None, None),
        P(("dp", "ep"), None, None),
        P(("dp", "ep"), None, None),
        P(None, "ep"),
        P(),
        P(),
        P(("dp", "ep"), None, None),
        P(("dp", "ep"), None, None),
        P(("dp", "ep")),
    )
    return jax.shard_map(
        shards,
        mesh=mesh,
        in_specs=placed,
        out_specs=(P(("dp", "ep"), None, None), P(("dp", "ep"), None, None, None)),
        check_vma=False,
    )
```

```python
import jax
import jax.numpy as jnp
from jax import lax
from jax.sharding import PartitionSpec as P

import functools
from jax.experimental import pallas as pl
from jax.experimental.pallas import tpu as pltpu

epsilon = 1e-06
f32 = jnp.float32
bf16 = jnp.bfloat16


def split2(x):
    hi = x.astype(bf16)
    lo = (x - hi.astype(f32)).astype(bf16)
    return hi, lo


def recur_kernel(slot_ref, s_ref, kq_ref, v_ref, g_ref, dec_ref, beta_ref, gain_ref, so_ref, co_ref, n_ref, r_ref, u_ref):
    heads = s_ref.shape[1]
    width = s_ref.shape[-1]
    steps = v_ref.shape[1]
    span = 2 * steps
    kq = kq_ref[0].astype(f32)
    kq = kq * lax.rsqrt(jnp.sum(kq * kq, -1, keepdims=True) + epsilon)
    row = lax.broadcasted_iota(jnp.int32, kq.shape, 0)
    kq = jnp.where(row % span >= steps, kq * width ** (-0.5), kq)
    n_ref[...] = kq
    for h in range(heads):
        p = n_ref[pl.ds(h * span, span), :]
        hi = p.astype(bf16).astype(f32)
        rest = p - hi
        mid = rest.astype(bf16).astype(f32)
        lo = rest - mid
        lhs = jnp.concatenate([hi, mid, lo], axis=0).astype(bf16)
        res = jnp.dot(lhs, s_ref[0, h], preferred_element_type=f32)
        r_ref[pl.ds(h * span, span), :] = (res[0:span] + res[span:2 * span]) + res[2 * span:3 * span]
    decay = jax.nn.sigmoid(dec_ref[0])
    strength = jax.nn.sigmoid(beta_ref[0])
    gain = gain_ref[...]
    keys = [n_ref[pl.ds(t, heads, stride=span), :] for t in range(steps)]
    queries = [n_ref[pl.ds(steps + t, heads, stride=span), :] for t in range(steps)]
    u_ref[...] = jnp.zeros(u_ref.shape, f32)
    updates = []
    carried = []
    total = None
    for t in range(steps):
        a_t = decay[:, t:t + 1]
        b_t = strength[:, t:t + 1]
        total = a_t if t == 0 else total * a_t
        carried = [c * a_t for c in carried]
        memory = total * r_ref[pl.ds(t, heads, stride=span), :]
        for j in range(t):
            kk = jnp.sum(keys[j] * keys[t], -1, keepdims=True)
            memory = memory + (carried[j] * kk) * updates[j]
        values = v_ref[0, t].astype(f32)
        update = (values - memory) * b_t
        updates.append(update)
        carried.append(jnp.ones_like(a_t))
        reading = total * r_ref[pl.ds(steps + t, heads, stride=span), :]
        for j in range(t + 1):
            qk = jnp.sum(keys[j] * queries[t], -1, keepdims=True)
            coef = qk if j == t else carried[j] * qk
            reading = reading + coef * updates[j]
        scaled = reading * lax.rsqrt(jnp.mean(reading * reading, -1, keepdims=True) + epsilon)
        gate_vals = g_ref[0, t].astype(f32)
        co_ref[0, t] = (scaled * gain * (gate_vals * jax.nn.sigmoid(gate_vals))).astype(co_ref.dtype)
    for j in range(steps):
        u_ref[pl.ds(j, heads, stride=span), :] = carried[j] * updates[j]
    for h in range(heads):
        kt = n_ref[pl.ds(h * span, span), :].T
        w = u_ref[pl.ds(h * span, span), :]
        k_hi, k_lo = split2(kt)
        w_hi, w_lo = split2(w)
        delta = (
            jnp.dot(k_hi, w_hi, preferred_element_type=f32)
            + jnp.dot(k_hi, w_lo, preferred_element_type=f32)
            + jnp.dot(k_lo, w_hi, preferred_element_type=f32)
        )
        so_ref[0, h] = (total[h:h + 1, :] * s_ref[0, h].astype(f32) + delta).astype(so_ref.dtype)


def recurrence(slots, states, query_rows, key_rows, value_rows, gate_rows, beta_logit, decay_logit, core_gain):
    batch, heads, width, _ = states.shape
    steps = query_rows.shape[1]
    key_heads = query_rows.shape[-1] // width
    repeats = heads // key_heads
    span = 2 * steps
    kq = jnp.concatenate(
        [key_rows.reshape(batch, steps, key_heads, width), query_rows.reshape(batch, steps, key_heads, width)], axis=1
    )
    kq = jnp.repeat(kq.transpose(0, 2, 1, 3), repeats, axis=1).reshape(batch, heads * span, width)
    values = value_rows.reshape(batch, steps, heads, width)
    gates = gate_rows.reshape(batch, steps, heads, width)
    decay = decay_logit.astype(f32).transpose(0, 2, 1)
    beta = beta_logit.astype(f32).transpose(0, 2, 1)
    gain = core_gain.reshape(1, width)
    state_in = pl.BlockSpec((1, heads, width, width), lambda i, slot: (i, 0, 0, 0))
    state_out = pl.BlockSpec((1, heads, width, width), lambda i, slot: (slot[i], 0, 0, 0))
    row_spec = pl.BlockSpec((1, steps, heads, width), lambda i, slot: (i, 0, 0, 0))
    coef_spec = pl.BlockSpec((1, heads, steps), lambda i, slot: (i, 0, 0))
    fresh, core = pl.pallas_call(
        recur_kernel,
        grid_spec=pltpu.PrefetchScalarGridSpec(
            num_scalar_prefetch=1,
            grid=(batch,),
            in_specs=[
                state_in,
                pl.BlockSpec((1, heads * span, width), lambda i, slot: (i, 0, 0)),
                row_spec,
                row_spec,
                coef_spec,
                coef_spec,
                pl.BlockSpec((1, width), lambda i, slot: (0, 0)),
            ],
            out_specs=[state_out, row_spec],
            scratch_shapes=[pltpu.VMEM((heads * span, width), f32)] * 3,
        ),
        out_shape=[
            jax.ShapeDtypeStruct(states.shape, bf16),
            jax.ShapeDtypeStruct((batch, steps, heads, width), bf16),
        ],
    )(slots, states, kq, values, gates, decay, beta, gain)
    return fresh, core.reshape(batch, steps, heads * width)


def unit_rows(values):
    return values * lax.rsqrt(jnp.sum(values * values, -1, keepdims=True) + epsilon)


def delta_block(
    state_in, query_rows, key_rows, value_rows, gate_rows, beta_logit, decay_logit, core_gain
):
    batch_size = state_in.shape[0]
    head_count = decay_logit.shape[-1]
    head_width = state_in.shape[-1]
    key_heads = query_rows.shape[-1] // head_width
    repeats = head_count // key_heads
    memory_state = state_in.astype(jnp.float32)
    outputs = []
    for position in range(query_rows.shape[1]):
        queries = unit_rows(
            query_rows[:, position].astype(jnp.float32).reshape(batch_size, key_heads, head_width)
        )
        queries = jnp.repeat(queries, repeats, axis=1) * head_width ** (-0.5)
        key_units = unit_rows(
            key_rows[:, position].astype(jnp.float32).reshape(batch_size, key_heads, head_width)
        )
        key_units = jnp.repeat(key_units, repeats, axis=1)
        values = (
            value_rows[:, position].astype(jnp.float32).reshape(batch_size, head_count, head_width)
        )
        decays = jax.nn.sigmoid(decay_logit[:, position].astype(jnp.float32))
        strength = jax.nn.sigmoid(beta_logit[:, position].astype(jnp.float32))
        memory_state = memory_state * decays[:, :, None, None]
        memory = jnp.einsum(
            "bhkv,bhk->bhv", memory_state, key_units, precision=lax.Precision.HIGHEST
        )
        update = (values - memory) * strength[:, :, None]
        memory_state = memory_state + key_units[:, :, :, None] * update[:, :, None, :]
        reading = jnp.einsum(
            "bhkv,bhk->bhv", memory_state, queries, precision=lax.Precision.HIGHEST
        )
        scaled = reading * lax.rsqrt(jnp.mean(reading * reading, -1, keepdims=True) + epsilon)
        gate_vals = (
            gate_rows[:, position].astype(jnp.float32).reshape(batch_size, head_count, head_width)
        )
        gated_out = scaled * core_gain * jax.nn.silu(gate_vals)
        outputs.append(gated_out.reshape(batch_size, head_count * head_width).astype(jnp.bfloat16))
    return (memory_state.astype(jnp.bfloat16), jnp.stack(outputs, axis=1))


def migrate_kernel(src_hbm, tag_hbm, dst_hbm, tag_out, send_sem, recv_sem, tag_send, tag_recv, local_sem):
    lanes = src_hbm.shape[0]
    group = lax.axis_index("dp")
    me = lax.axis_index("ep")
    mesh_ids = pl.DeviceIdType.MESH
    barrier = pltpu.get_barrier_semaphore()
    for i in range(1, lanes):
        pl.semaphore_signal(barrier, 1, device_id=(group, lax.rem(me + i, lanes)), device_id_type=mesh_ids)
    pl.semaphore_wait(barrier, lanes - 1)
    own = pltpu.make_async_copy(src_hbm.at[me], dst_hbm.at[me], local_sem.at[0])
    own.start()
    own_tag = pltpu.make_async_copy(tag_hbm.at[me], tag_out.at[me], local_sem.at[1])
    own_tag.start()
    copies = []
    for i in range(1, lanes):
        peer = lax.rem(me + i, lanes)
        for source, target, sent, landed in ((tag_hbm, tag_out, tag_send, tag_recv), (src_hbm, dst_hbm, send_sem, recv_sem)):
            copy = pltpu.make_async_remote_copy(
                source.at[peer],
                target.at[me],
                sent.at[i - 1],
                landed.at[i - 1],
                device_id=(group, peer),
                device_id_type=mesh_ids,
            )
            copy.start()
            copies.append(copy)
    own.wait()
    own_tag.wait()
    for copy in copies:
        copy.wait()


def migrate(rows, tags):
    lanes = rows.shape[0]
    any_spec = pl.BlockSpec(memory_space=pl.ANY)
    return pl.pallas_call(
        migrate_kernel,
        in_specs=[any_spec, any_spec],
        out_specs=[any_spec, any_spec],
        out_shape=[
            jax.ShapeDtypeStruct(rows.shape, rows.dtype),
            jax.ShapeDtypeStruct(tags.shape, tags.dtype),
        ],
        scratch_shapes=[
            pltpu.SemaphoreType.DMA((lanes - 1,)),
            pltpu.SemaphoreType.DMA((lanes - 1,)),
            pltpu.SemaphoreType.DMA((lanes - 1,)),
            pltpu.SemaphoreType.DMA((lanes - 1,)),
            pltpu.SemaphoreType.DMA((2,)),
        ],
        compiler_params=pltpu.CompilerParams(collective_id=0, has_side_effects=True),
        cost_estimate=pl.CostEstimate(flops=0, transcendentals=0, bytes_accessed=2 * rows.size * rows.dtype.itemsize),
    )(rows, tags)

def project_kernel(rows_ref, weight_ref, out_ref, gathered, product, send_a, recv_a, send_b, recv_b, local_sem):
    lanes = gathered.shape[0]
    count = rows_ref.shape[0]
    block = weight_ref.shape[1]
    group = lax.axis_index("dp")
    me = lax.axis_index("ep")
    mesh_ids = pl.DeviceIdType.MESH
    barrier = pltpu.get_barrier_semaphore()
    for i in range(1, lanes):
        pl.semaphore_signal(barrier, 1, device_id=(group, lax.rem(me + i, lanes)), device_id_type=mesh_ids)
    pl.semaphore_wait(barrier, lanes - 1)
    own = pltpu.make_async_copy(rows_ref, gathered.at[me], local_sem)
    own.start()
    sends = []
    for i in range(1, lanes):
        copy = pltpu.make_async_remote_copy(
            rows_ref, gathered.at[me], send_a.at[i - 1], recv_a.at[i - 1],
            device_id=(group, lax.rem(me + i, lanes)), device_id_type=mesh_ids,
        )
        copy.start()
        sends.append(copy)
    own.wait()
    for copy in sends:
        copy.wait()
    width = gathered.shape[-1]
    stacked = gathered[...].reshape(lanes * count, width)
    product[...] = (
        jnp.dot(stacked, weight_ref[...], preferred_element_type=jnp.float32)
        .astype(product.dtype)
        .reshape(lanes, count, block)
    )
    columns = pl.ds(pl.multiple_of(me * block, block), block)
    back = pltpu.make_async_copy(product.at[me], out_ref.at[:, columns], local_sem)
    back.start()
    replies = []
    for i in range(1, lanes):
        peer = lax.rem(me + i, lanes)
        copy = pltpu.make_async_remote_copy(
            product.at[peer], out_ref.at[:, columns], send_b.at[i - 1], recv_b.at[i - 1],
            device_id=(group, peer), device_id_type=mesh_ids,
        )
        copy.start()
        replies.append(copy)
    back.wait()
    for copy in replies:
        copy.wait()


def project(rows, weight):
    lanes = lax.axis_size("ep")
    count, width = rows.shape
    block = weight.shape[1]
    vmem = pl.BlockSpec(memory_space=pltpu.VMEM)
    return pl.pallas_call(
        project_kernel,
        in_specs=[vmem, vmem],
        out_specs=vmem,
        out_shape=jax.ShapeDtypeStruct((count, lanes * block), rows.dtype),
        scratch_shapes=[
            pltpu.VMEM((lanes, count, width), rows.dtype),
            pltpu.VMEM((lanes, count, block), rows.dtype),
            pltpu.SemaphoreType.DMA((lanes - 1,)),
            pltpu.SemaphoreType.DMA((lanes - 1,)),
            pltpu.SemaphoreType.DMA((lanes - 1,)),
            pltpu.SemaphoreType.DMA((lanes - 1,)),
            pltpu.SemaphoreType.DMA,
        ],
        compiler_params=pltpu.CompilerParams(collective_id=1, has_side_effects=True),
    )(rows, weight)


def place_kernel(place_ref, in_ref, out_ref):
    out_ref[...] = in_ref[...]


def place_rows(rows, places):
    block = (1,) + rows.shape[1:]
    tail = (0,) * (rows.ndim - 1)
    return pl.pallas_call(
        place_kernel,
        grid_spec=pltpu.PrefetchScalarGridSpec(
            num_scalar_prefetch=1,
            grid=(rows.shape[0],),
            in_specs=[pl.BlockSpec(block, lambda j, place: (j,) + tail)],
            out_specs=pl.BlockSpec(block, lambda j, place: (place[j],) + tail),
        ),
        out_shape=jax.ShapeDtypeStruct(rows.shape, rows.dtype),
    )(places, rows)


def rms_scale(values, gain):
    return values * lax.rsqrt(jnp.mean(values * values, -1, keepdims=True) + epsilon) * gain


def expert_apply(chosen_rows, gate_up, down_weight):
    hidden_units = down_weight.shape[0]
    joined = jnp.dot(chosen_rows, gate_up, preferred_element_type=jnp.float32)
    active = (jax.nn.silu(joined[:, :hidden_units]) * joined[:, hidden_units:]).astype(jnp.bfloat16)
    return jnp.dot(active, down_weight, preferred_element_type=jnp.float32).astype(jnp.bfloat16)


def pack(values, positions, lane_count):
    zeroed = jnp.zeros(values.shape, values.dtype)
    placed = zeroed.at[positions].set(values)
    return placed.reshape((lane_count, values.shape[0] // lane_count) + values.shape[1:])


def unpack(values):
    return values.reshape((values.shape[0] * values.shape[1],) + values.shape[2:])


def shards(
    states,
    query_rows,
    key_rows,
    value_rows,
    gate_rows,
    beta_logit,
    decay_logit,
    residual,
    route_ids,
    route_prob,
    out_weight,
    core_gain,
    moe_gain,
    gate_up,
    down_weight,
    new_home,
):
    req_count = states.shape[0]
    step_count = query_rows.shape[1]
    model_width = residual.shape[-1]
    ep_size = lax.axis_size("ep")
    dp_size = lax.axis_size("dp")
    target = new_home // req_count % ep_size
    new_place = new_home % req_count
    fresh_states, core_out = recurrence(
        target, states, query_rows, key_rows, value_rows, gate_rows, beta_logit, decay_logit, core_gain
    )
    packed_place = jnp.zeros_like(new_place).at[target].set(new_place)
    tags = jnp.broadcast_to(packed_place[:, None, None], (ep_size, 8, 128))
    moved_rows, moved_tags = migrate(fresh_states, tags)
    moved_out = place_rows(moved_rows, moved_tags[:, 0, 0])
    token_count = req_count * step_count
    core_flat = core_out.reshape(token_count, core_out.shape[-1])
    attention = project(core_flat, out_weight)
    hidden = (
        residual.reshape(token_count, model_width).astype(jnp.float32)
        + attention.astype(jnp.float32)
    ).astype(jnp.bfloat16)
    normed = rms_scale(hidden.astype(jnp.float32), moe_gain).astype(jnp.bfloat16)
    top_count = route_ids.shape[-1]
    experts = dp_size * ep_size
    capacity = (token_count * top_count + experts - 1) // experts + 1
    flat_ids = route_ids.reshape(-1)
    onehot = (flat_ids[:, None] == jnp.arange(experts, dtype=jnp.int32)[None, :]).astype(jnp.int32)
    route_rank = jnp.sum(jnp.cumsum(onehot, axis=0) * onehot, axis=1) - 1
    slot_index = flat_ids * capacity + route_rank
    slot_count = experts * capacity
    match = slot_index[None, :] == jnp.arange(slot_count, dtype=jnp.int32)[:, None]
    match = match.reshape(experts, capacity, token_count, top_count)
    pick = jnp.any(match, axis=-1).astype(jnp.bfloat16)
    lane_count = 128
    chunks = model_width // lane_count
    normed_tiles = normed.reshape(token_count, chunks, lane_count)
    outgoing = jnp.einsum(
        "esk,kcl->escl", pick, normed_tiles, preferred_element_type=jnp.float32
    ).astype(jnp.bfloat16)
    outgoing = outgoing.reshape(experts, capacity * chunks, lane_count)
    arrived = lax.all_to_all(outgoing, ("dp", "ep"), 0, 0, tiled=True)
    arrived = arrived.reshape(experts, capacity, chunks, lane_count)
    hidden_units = down_weight.shape[1]
    gate_tiles = gate_up[0].reshape(chunks, lane_count, gate_up.shape[-1])
    joined = jnp.einsum("escl,clf->esf", arrived, gate_tiles, preferred_element_type=jnp.float32)
    active = (jax.nn.silu(joined[..., :hidden_units]) * joined[..., hidden_units:]).astype(jnp.bfloat16)
    down_tiles = down_weight[0].reshape(hidden_units, chunks, lane_count)
    result = jnp.einsum(
        "esf,fcl->escl", active, down_tiles, preferred_element_type=jnp.float32
    ).astype(jnp.bfloat16)
    result = result.reshape(experts, capacity * chunks, lane_count)
    returned = lax.all_to_all(result, ("dp", "ep"), 0, 0, tiled=True)
    returned = returned.reshape(experts, capacity, chunks, lane_count)
    weights = route_prob.reshape(token_count, top_count)
    weights = weights / jnp.sum(weights, -1, keepdims=True)
    spread = jnp.sum(jnp.where(match, weights[None, None, :, :], 0.0), axis=-1)
    high = spread.astype(jnp.bfloat16)
    rest = spread - high.astype(jnp.float32)
    middle = rest.astype(jnp.bfloat16)
    low = (rest - middle.astype(jnp.float32)).astype(jnp.bfloat16)
    parts = jnp.concatenate([high, middle, low], axis=-1)
    combined = jnp.einsum("esk,escl->kcl", parts, returned, preferred_element_type=jnp.float32)
    combined = combined.reshape(3, token_count, chunks, lane_count).sum(axis=0)
    combined = combined.reshape(token_count, model_width)
    mixed_out = (
        (hidden.astype(jnp.float32) + combined)
        .astype(jnp.bfloat16)
        .reshape(req_count, step_count, model_width)
    )
    return (mixed_out, moved_out)


def solution(mesh):
    placed = (
        P(("dp", "ep"), None, None, None),
        P(("dp", "ep"), None, None),
        P(("dp", "ep"), None, None),
        P(("dp", "ep"), None, None),
        P(("dp", "ep"), None, None),
        P(("dp", "ep"), None, None),
        P(("dp", "ep"), None, None),
        P(("dp", "ep"), None, None),
        P(("dp", "ep"), None, None),
        P(("dp", "ep"), None, None),
        P(None, "ep"),
        P(),
        P(),
        P(("dp", "ep"), None, None),
        P(("dp", "ep"), None, None),
        P(("dp", "ep")),
    )
    return jax.shard_map(
        shards,
        mesh=mesh,
        in_specs=placed,
        out_specs=(P(("dp", "ep"), None, None), P(("dp", "ep"), None, None, None)),
        check_vma=False,
    )
```

```python
import jax
import jax.numpy as jnp
from jax import lax
from jax.sharding import PartitionSpec as P

import functools
from jax.experimental import pallas as pl
from jax.experimental.pallas import tpu as pltpu

epsilon = 1e-06
f32 = jnp.float32
bf16 = jnp.bfloat16


def split2(x):
    hi = x.astype(bf16)
    lo = (x - hi.astype(f32)).astype(bf16)
    return hi, lo


def recur_kernel(slot_ref, s_ref, kq_ref, v_ref, g_ref, dec_ref, beta_ref, gain_ref, so_ref, co_ref, n_ref, r_ref, u_ref):
    heads = s_ref.shape[1]
    width = s_ref.shape[-1]
    steps = v_ref.shape[1]
    span = 2 * steps
    kq = kq_ref[0].astype(f32)
    kq = kq * lax.rsqrt(jnp.sum(kq * kq, -1, keepdims=True) + epsilon)
    row = lax.broadcasted_iota(jnp.int32, kq.shape, 0)
    kq = jnp.where(row % span >= steps, kq * width ** (-0.5), kq)
    n_ref[...] = kq
    for h in range(heads):
        p = n_ref[pl.ds(h * span, span), :]
        hi = p.astype(bf16).astype(f32)
        rest = p - hi
        mid = rest.astype(bf16).astype(f32)
        lo = rest - mid
        lhs = jnp.concatenate([hi, mid, lo], axis=0).astype(bf16)
        res = jnp.dot(lhs, s_ref[0, h], preferred_element_type=f32)
        r_ref[pl.ds(h * span, span), :] = (res[0:span] + res[span:2 * span]) + res[2 * span:3 * span]
    decay = jax.nn.sigmoid(dec_ref[0])
    strength = jax.nn.sigmoid(beta_ref[0])
    gain = gain_ref[...]
    keys = [n_ref[pl.ds(t, heads, stride=span), :] for t in range(steps)]
    queries = [n_ref[pl.ds(steps + t, heads, stride=span), :] for t in range(steps)]
    u_ref[...] = jnp.zeros(u_ref.shape, f32)
    updates = []
    carried = []
    total = None
    for t in range(steps):
        a_t = decay[:, t:t + 1]
        b_t = strength[:, t:t + 1]
        total = a_t if t == 0 else total * a_t
        carried = [c * a_t for c in carried]
        memory = total * r_ref[pl.ds(t, heads, stride=span), :]
        for j in range(t):
            kk = jnp.sum(keys[j] * keys[t], -1, keepdims=True)
            memory = memory + (carried[j] * kk) * updates[j]
        values = v_ref[0, t].astype(f32)
        update = (values - memory) * b_t
        updates.append(update)
        carried.append(jnp.ones_like(a_t))
        reading = total * r_ref[pl.ds(steps + t, heads, stride=span), :]
        for j in range(t + 1):
            qk = jnp.sum(keys[j] * queries[t], -1, keepdims=True)
            coef = qk if j == t else carried[j] * qk
            reading = reading + coef * updates[j]
        scaled = reading * lax.rsqrt(jnp.mean(reading * reading, -1, keepdims=True) + epsilon)
        gate_vals = g_ref[0, t].astype(f32)
        co_ref[0, t] = (scaled * gain * (gate_vals * jax.nn.sigmoid(gate_vals))).astype(co_ref.dtype)
    for j in range(steps):
        u_ref[pl.ds(j, heads, stride=span), :] = carried[j] * updates[j]
    for h in range(heads):
        kt = n_ref[pl.ds(h * span, span), :].T
        w = u_ref[pl.ds(h * span, span), :]
        k_hi, k_lo = split2(kt)
        w_hi, w_lo = split2(w)
        delta = (
            jnp.dot(k_hi, w_hi, preferred_element_type=f32)
            + jnp.dot(k_hi, w_lo, preferred_element_type=f32)
            + jnp.dot(k_lo, w_hi, preferred_element_type=f32)
        )
        so_ref[0, h] = (total[h:h + 1, :] * s_ref[0, h].astype(f32) + delta).astype(so_ref.dtype)


def recurrence(slots, states, query_rows, key_rows, value_rows, gate_rows, beta_logit, decay_logit, core_gain):
    batch, heads, width, _ = states.shape
    steps = query_rows.shape[1]
    key_heads = query_rows.shape[-1] // width
    repeats = heads // key_heads
    span = 2 * steps
    kq = jnp.concatenate(
        [key_rows.reshape(batch, steps, key_heads, width), query_rows.reshape(batch, steps, key_heads, width)], axis=1
    )
    kq = jnp.repeat(kq.transpose(0, 2, 1, 3), repeats, axis=1).reshape(batch, heads * span, width)
    values = value_rows.reshape(batch, steps, heads, width)
    gates = gate_rows.reshape(batch, steps, heads, width)
    decay = decay_logit.astype(f32).transpose(0, 2, 1)
    beta = beta_logit.astype(f32).transpose(0, 2, 1)
    gain = core_gain.reshape(1, width)
    state_in = pl.BlockSpec((1, heads, width, width), lambda i, slot: (i, 0, 0, 0))
    state_out = pl.BlockSpec((1, heads, width, width), lambda i, slot: (slot[i], 0, 0, 0))
    row_spec = pl.BlockSpec((1, steps, heads, width), lambda i, slot: (i, 0, 0, 0))
    coef_spec = pl.BlockSpec((1, heads, steps), lambda i, slot: (i, 0, 0))
    fresh, core = pl.pallas_call(
        recur_kernel,
        grid_spec=pltpu.PrefetchScalarGridSpec(
            num_scalar_prefetch=1,
            grid=(batch,),
            in_specs=[
                state_in,
                pl.BlockSpec((1, heads * span, width), lambda i, slot: (i, 0, 0)),
                row_spec,
                row_spec,
                coef_spec,
                coef_spec,
                pl.BlockSpec((1, width), lambda i, slot: (0, 0)),
            ],
            out_specs=[state_out, row_spec],
            scratch_shapes=[pltpu.VMEM((heads * span, width), f32)] * 3,
        ),
        out_shape=[
            jax.ShapeDtypeStruct(states.shape, bf16),
            jax.ShapeDtypeStruct((batch, steps, heads, width), bf16),
        ],
    )(slots, states, kq, values, gates, decay, beta, gain)
    return fresh, core.reshape(batch, steps, heads * width)


def unit_rows(values):
    return values * lax.rsqrt(jnp.sum(values * values, -1, keepdims=True) + epsilon)


def delta_block(
    state_in, query_rows, key_rows, value_rows, gate_rows, beta_logit, decay_logit, core_gain
):
    batch_size = state_in.shape[0]
    head_count = decay_logit.shape[-1]
    head_width = state_in.shape[-1]
    key_heads = query_rows.shape[-1] // head_width
    repeats = head_count // key_heads
    memory_state = state_in.astype(jnp.float32)
    outputs = []
    for position in range(query_rows.shape[1]):
        queries = unit_rows(
            query_rows[:, position].astype(jnp.float32).reshape(batch_size, key_heads, head_width)
        )
        queries = jnp.repeat(queries, repeats, axis=1) * head_width ** (-0.5)
        key_units = unit_rows(
            key_rows[:, position].astype(jnp.float32).reshape(batch_size, key_heads, head_width)
        )
        key_units = jnp.repeat(key_units, repeats, axis=1)
        values = (
            value_rows[:, position].astype(jnp.float32).reshape(batch_size, head_count, head_width)
        )
        decays = jax.nn.sigmoid(decay_logit[:, position].astype(jnp.float32))
        strength = jax.nn.sigmoid(beta_logit[:, position].astype(jnp.float32))
        memory_state = memory_state * decays[:, :, None, None]
        memory = jnp.einsum(
            "bhkv,bhk->bhv", memory_state, key_units, precision=lax.Precision.HIGHEST
        )
        update = (values - memory) * strength[:, :, None]
        memory_state = memory_state + key_units[:, :, :, None] * update[:, :, None, :]
        reading = jnp.einsum(
            "bhkv,bhk->bhv", memory_state, queries, precision=lax.Precision.HIGHEST
        )
        scaled = reading * lax.rsqrt(jnp.mean(reading * reading, -1, keepdims=True) + epsilon)
        gate_vals = (
            gate_rows[:, position].astype(jnp.float32).reshape(batch_size, head_count, head_width)
        )
        gated_out = scaled * core_gain * jax.nn.silu(gate_vals)
        outputs.append(gated_out.reshape(batch_size, head_count * head_width).astype(jnp.bfloat16))
    return (memory_state.astype(jnp.bfloat16), jnp.stack(outputs, axis=1))


def migrate_kernel(src_hbm, tag_hbm, dst_hbm, tag_out, send_sem, recv_sem, tag_send, tag_recv, local_sem):
    lanes = src_hbm.shape[0]
    group = lax.axis_index("dp")
    me = lax.axis_index("ep")
    mesh_ids = pl.DeviceIdType.MESH
    barrier = pltpu.get_barrier_semaphore()
    for i in range(1, lanes):
        pl.semaphore_signal(barrier, 1, device_id=(group, lax.rem(me + i, lanes)), device_id_type=mesh_ids)
    pl.semaphore_wait(barrier, lanes - 1)
    own = pltpu.make_async_copy(src_hbm.at[me], dst_hbm.at[me], local_sem.at[0])
    own.start()
    own_tag = pltpu.make_async_copy(tag_hbm.at[me], tag_out.at[me], local_sem.at[1])
    own_tag.start()
    copies = []
    for i in range(1, lanes):
        peer = lax.rem(me + i, lanes)
        for source, target, sent, landed in ((tag_hbm, tag_out, tag_send, tag_recv), (src_hbm, dst_hbm, send_sem, recv_sem)):
            copy = pltpu.make_async_remote_copy(
                source.at[peer],
                target.at[me],
                sent.at[i - 1],
                landed.at[i - 1],
                device_id=(group, peer),
                device_id_type=mesh_ids,
            )
            copy.start()
            copies.append(copy)
    own.wait()
    own_tag.wait()
    for copy in copies:
        copy.wait()


def migrate(rows, tags):
    lanes = rows.shape[0]
    any_spec = pl.BlockSpec(memory_space=pl.ANY)
    return pl.pallas_call(
        migrate_kernel,
        in_specs=[any_spec, any_spec],
        out_specs=[any_spec, any_spec],
        out_shape=[
            jax.ShapeDtypeStruct(rows.shape, rows.dtype),
            jax.ShapeDtypeStruct(tags.shape, tags.dtype),
        ],
        scratch_shapes=[
            pltpu.SemaphoreType.DMA((lanes - 1,)),
            pltpu.SemaphoreType.DMA((lanes - 1,)),
            pltpu.SemaphoreType.DMA((lanes - 1,)),
            pltpu.SemaphoreType.DMA((lanes - 1,)),
            pltpu.SemaphoreType.DMA((2,)),
        ],
        compiler_params=pltpu.CompilerParams(collective_id=0, has_side_effects=True),
        cost_estimate=pl.CostEstimate(flops=0, transcendentals=0, bytes_accessed=2 * rows.size * rows.dtype.itemsize),
    )(rows, tags)

def project_kernel(rows_ref, weight_ref, out_ref, gathered, product, send_a, recv_a, send_b, recv_b, local_sem):
    lanes = gathered.shape[0]
    count = rows_ref.shape[0]
    block = weight_ref.shape[1]
    group = lax.axis_index("dp")
    me = lax.axis_index("ep")
    mesh_ids = pl.DeviceIdType.MESH
    barrier = pltpu.get_barrier_semaphore()
    for i in range(1, lanes):
        pl.semaphore_signal(barrier, 1, device_id=(group, lax.rem(me + i, lanes)), device_id_type=mesh_ids)
    pl.semaphore_wait(barrier, lanes - 1)
    own = pltpu.make_async_copy(rows_ref, gathered.at[me], local_sem)
    own.start()
    sends = []
    for i in range(1, lanes):
        copy = pltpu.make_async_remote_copy(
            rows_ref, gathered.at[me], send_a.at[i - 1], recv_a.at[i - 1],
            device_id=(group, lax.rem(me + i, lanes)), device_id_type=mesh_ids,
        )
        copy.start()
        sends.append(copy)
    own.wait()
    for copy in sends:
        copy.wait()
    width = gathered.shape[-1]
    stacked = gathered[...].reshape(lanes * count, width)
    product[...] = (
        jnp.dot(stacked, weight_ref[...], preferred_element_type=jnp.float32)
        .astype(product.dtype)
        .reshape(lanes, count, block)
    )
    columns = pl.ds(pl.multiple_of(me * block, block), block)
    back = pltpu.make_async_copy(product.at[me], out_ref.at[:, columns], local_sem)
    back.start()
    replies = []
    for i in range(1, lanes):
        peer = lax.rem(me + i, lanes)
        copy = pltpu.make_async_remote_copy(
            product.at[peer], out_ref.at[:, columns], send_b.at[i - 1], recv_b.at[i - 1],
            device_id=(group, peer), device_id_type=mesh_ids,
        )
        copy.start()
        replies.append(copy)
    back.wait()
    for copy in replies:
        copy.wait()


def project(rows, weight):
    lanes = lax.axis_size("ep")
    count, width = rows.shape
    block = weight.shape[1]
    vmem = pl.BlockSpec(memory_space=pltpu.VMEM)
    return pl.pallas_call(
        project_kernel,
        in_specs=[vmem, vmem],
        out_specs=vmem,
        out_shape=jax.ShapeDtypeStruct((count, lanes * block), rows.dtype),
        scratch_shapes=[
            pltpu.VMEM((lanes, count, width), rows.dtype),
            pltpu.VMEM((lanes, count, block), rows.dtype),
            pltpu.SemaphoreType.DMA((lanes - 1,)),
            pltpu.SemaphoreType.DMA((lanes - 1,)),
            pltpu.SemaphoreType.DMA((lanes - 1,)),
            pltpu.SemaphoreType.DMA((lanes - 1,)),
            pltpu.SemaphoreType.DMA,
        ],
        compiler_params=pltpu.CompilerParams(collective_id=1, has_side_effects=True),
    )(rows, weight)


def place_kernel(place_ref, in_hbm, out_hbm, held, in_sem, out_sem):
    count = in_hbm.shape[0]
    loads = []
    for j in range(count):
        load = pltpu.make_async_copy(in_hbm.at[j], held.at[j], in_sem.at[j])
        load.start()
        loads.append(load)
    stores = []
    for j in range(count):
        loads[j].wait()
        store = pltpu.make_async_copy(held.at[j], out_hbm.at[place_ref[j]], out_sem.at[j])
        store.start()
        stores.append(store)
    for store in stores:
        store.wait()


def place_rows(rows, places):
    count = rows.shape[0]
    any_spec = pl.BlockSpec(memory_space=pl.ANY)
    return pl.pallas_call(
        place_kernel,
        in_specs=[pl.BlockSpec(memory_space=pltpu.SMEM), any_spec],
        out_specs=any_spec,
        out_shape=jax.ShapeDtypeStruct(rows.shape, rows.dtype),
        scratch_shapes=[
            pltpu.VMEM(rows.shape, rows.dtype),
            pltpu.SemaphoreType.DMA((count,)),
            pltpu.SemaphoreType.DMA((count,)),
        ],
        compiler_params=pltpu.CompilerParams(vmem_limit_bytes=48 * 1024 * 1024),
    )(places, rows)

def rms_scale(values, gain):
    return values * lax.rsqrt(jnp.mean(values * values, -1, keepdims=True) + epsilon) * gain


def expert_apply(chosen_rows, gate_up, down_weight):
    hidden_units = down_weight.shape[0]
    joined = jnp.dot(chosen_rows, gate_up, preferred_element_type=jnp.float32)
    active = (jax.nn.silu(joined[:, :hidden_units]) * joined[:, hidden_units:]).astype(jnp.bfloat16)
    return jnp.dot(active, down_weight, preferred_element_type=jnp.float32).astype(jnp.bfloat16)


def pack(values, positions, lane_count):
    zeroed = jnp.zeros(values.shape, values.dtype)
    placed = zeroed.at[positions].set(values)
    return placed.reshape((lane_count, values.shape[0] // lane_count) + values.shape[1:])


def unpack(values):
    return values.reshape((values.shape[0] * values.shape[1],) + values.shape[2:])


def shards(
    states,
    query_rows,
    key_rows,
    value_rows,
    gate_rows,
    beta_logit,
    decay_logit,
    residual,
    route_ids,
    route_prob,
    out_weight,
    core_gain,
    moe_gain,
    gate_up,
    down_weight,
    new_home,
):
    req_count = states.shape[0]
    step_count = query_rows.shape[1]
    model_width = residual.shape[-1]
    ep_size = lax.axis_size("ep")
    dp_size = lax.axis_size("dp")
    target = new_home // req_count % ep_size
    new_place = new_home % req_count
    fresh_states, core_out = recurrence(
        target, states, query_rows, key_rows, value_rows, gate_rows, beta_logit, decay_logit, core_gain
    )
    packed_place = jnp.zeros_like(new_place).at[target].set(new_place)
    tags = jnp.broadcast_to(packed_place[:, None, None], (ep_size, 8, 128))
    moved_rows, moved_tags = migrate(fresh_states, tags)
    moved_out = place_rows(moved_rows, moved_tags[:, 0, 0])
    token_count = req_count * step_count
    core_flat = core_out.reshape(token_count, core_out.shape[-1])
    attention = project(core_flat, out_weight)
    hidden = (
        residual.reshape(token_count, model_width).astype(jnp.float32)
        + attention.astype(jnp.float32)
    ).astype(jnp.bfloat16)
    normed = rms_scale(hidden.astype(jnp.float32), moe_gain).astype(jnp.bfloat16)
    top_count = route_ids.shape[-1]
    experts = dp_size * ep_size
    capacity = (token_count * top_count + experts - 1) // experts + 1
    flat_ids = route_ids.reshape(-1)
    onehot = (flat_ids[:, None] == jnp.arange(experts, dtype=jnp.int32)[None, :]).astype(jnp.int32)
    route_rank = jnp.sum(jnp.cumsum(onehot, axis=0) * onehot, axis=1) - 1
    slot_index = flat_ids * capacity + route_rank
    slot_count = experts * capacity
    match = slot_index[None, :] == jnp.arange(slot_count, dtype=jnp.int32)[:, None]
    match = match.reshape(experts, capacity, token_count, top_count)
    pick = jnp.any(match, axis=-1).astype(jnp.bfloat16)
    lane_count = 128
    chunks = model_width // lane_count
    normed_tiles = normed.reshape(token_count, chunks, lane_count)
    outgoing = jnp.einsum(
        "esk,kcl->escl", pick, normed_tiles, preferred_element_type=jnp.float32
    ).astype(jnp.bfloat16)
    outgoing = outgoing.reshape(experts, capacity * chunks, lane_count)
    arrived = lax.all_to_all(outgoing, ("dp", "ep"), 0, 0, tiled=True)
    arrived = arrived.reshape(experts, capacity, chunks, lane_count)
    hidden_units = down_weight.shape[1]
    gate_tiles = gate_up[0].reshape(chunks, lane_count, gate_up.shape[-1])
    joined = jnp.einsum("escl,clf->esf", arrived, gate_tiles, preferred_element_type=jnp.float32)
    active = (jax.nn.silu(joined[..., :hidden_units]) * joined[..., hidden_units:]).astype(jnp.bfloat16)
    down_tiles = down_weight[0].reshape(hidden_units, chunks, lane_count)
    result = jnp.einsum(
        "esf,fcl->escl", active, down_tiles, preferred_element_type=jnp.float32
    ).astype(jnp.bfloat16)
    result = result.reshape(experts, capacity * chunks, lane_count)
    returned = lax.all_to_all(result, ("dp", "ep"), 0, 0, tiled=True)
    returned = returned.reshape(experts, capacity, chunks, lane_count)
    weights = route_prob.reshape(token_count, top_count)
    weights = weights / jnp.sum(weights, -1, keepdims=True)
    spread = jnp.sum(jnp.where(match, weights[None, None, :, :], 0.0), axis=-1)
    high = spread.astype(jnp.bfloat16)
    rest = spread - high.astype(jnp.float32)
    middle = rest.astype(jnp.bfloat16)
    low = (rest - middle.astype(jnp.float32)).astype(jnp.bfloat16)
    parts = jnp.concatenate([high, middle, low], axis=-1)
    combined = jnp.einsum("esk,escl->kcl", parts, returned, preferred_element_type=jnp.float32)
    combined = combined.reshape(3, token_count, chunks, lane_count).sum(axis=0)
    combined = combined.reshape(token_count, model_width)
    mixed_out = (
        (hidden.astype(jnp.float32) + combined)
        .astype(jnp.bfloat16)
        .reshape(req_count, step_count, model_width)
    )
    return (mixed_out, moved_out)


def solution(mesh):
    placed = (
        P(("dp", "ep"), None, None, None),
        P(("dp", "ep"), None, None),
        P(("dp", "ep"), None, None),
        P(("dp", "ep"), None, None),
        P(("dp", "ep"), None, None),
        P(("dp", "ep"), None, None),
        P(("dp", "ep"), None, None),
        P(("dp", "ep"), None, None),
        P(("dp", "ep"), None, None),
        P(("dp", "ep"), None, None),
        P(None, "ep"),
        P(),
        P(),
        P(("dp", "ep"), None, None),
        P(("dp", "ep"), None, None),
        P(("dp", "ep")),
    )
    return jax.shard_map(
        shards,
        mesh=mesh,
        in_specs=placed,
        out_specs=(P(("dp", "ep"), None, None), P(("dp", "ep"), None, None, None)),
        check_vma=False,
    )
```

```python
import jax
import jax.numpy as jnp
from jax import lax
from jax.sharding import PartitionSpec as P

import functools
from jax.experimental import pallas as pl
from jax.experimental.pallas import tpu as pltpu

epsilon = 1e-06
f32 = jnp.float32
bf16 = jnp.bfloat16


def split2(x):
    hi = x.astype(bf16)
    lo = (x - hi.astype(f32)).astype(bf16)
    return hi, lo


def recur_kernel(slot_ref, s_ref, kq_ref, v_ref, g_ref, dec_ref, beta_ref, gain_ref, so_ref, co_ref, n_ref, r_ref, u_ref, c_ref):
    heads = s_ref.shape[1]
    width = s_ref.shape[-1]
    steps = v_ref.shape[1]
    span = 2 * steps
    kq = kq_ref[0].astype(f32)
    kq = kq * lax.rsqrt(jnp.sum(kq * kq, -1, keepdims=True) + epsilon)
    row = lax.broadcasted_iota(jnp.int32, kq.shape, 0)
    kq = jnp.where(row % span >= steps, kq * width ** (-0.5), kq)
    n_ref[...] = kq
    for h in range(heads):
        p = n_ref[pl.ds(h * span, span), :]
        hi = p.astype(bf16).astype(f32)
        rest = p - hi
        mid = rest.astype(bf16).astype(f32)
        lo = rest - mid
        lhs = jnp.concatenate([hi, mid, lo], axis=0).astype(bf16)
        res = jnp.dot(lhs, s_ref[0, h], preferred_element_type=f32)
        r_ref[pl.ds(h * span, span), :] = (res[0:span] + res[span:2 * span]) + res[2 * span:3 * span]
    decay = jax.nn.sigmoid(dec_ref[0])
    strength = jax.nn.sigmoid(beta_ref[0])
    gain = gain_ref[...]
    keys = [n_ref[pl.ds(t, heads, stride=span), :] for t in range(steps)]
    queries = [n_ref[pl.ds(steps + t, heads, stride=span), :] for t in range(steps)]
    u_ref[...] = jnp.zeros(u_ref.shape, f32)
    updates = []
    carried = []
    total = None
    for t in range(steps):
        a_t = decay[:, t:t + 1]
        b_t = strength[:, t:t + 1]
        total = a_t if t == 0 else total * a_t
        carried = [c * a_t for c in carried]
        memory = total * r_ref[pl.ds(t, heads, stride=span), :]
        for j in range(t):
            kk = jnp.sum(keys[j] * keys[t], -1, keepdims=True)
            memory = memory + (carried[j] * kk) * updates[j]
        values = v_ref[0, t].astype(f32)
        update = (values - memory) * b_t
        updates.append(update)
        carried.append(jnp.ones_like(a_t))
        reading = total * r_ref[pl.ds(steps + t, heads, stride=span), :]
        for j in range(t + 1):
            qk = jnp.sum(keys[j] * queries[t], -1, keepdims=True)
            coef = qk if j == t else carried[j] * qk
            reading = reading + coef * updates[j]
        scaled = reading * lax.rsqrt(jnp.mean(reading * reading, -1, keepdims=True) + epsilon)
        gate_vals = g_ref[0, t].astype(f32)
        c_ref[pl.ds(t * heads, heads), :] = scaled * gain * (gate_vals * jax.nn.sigmoid(gate_vals))
    for j in range(steps):
        u_ref[pl.ds(j, heads, stride=span), :] = carried[j] * updates[j]
    for h in range(heads):
        co_ref[0, :, pl.ds(h * width, width)] = c_ref[pl.ds(h, steps, stride=heads), :].astype(co_ref.dtype)
    for h in range(heads):
        kt = n_ref[pl.ds(h * span, span), :].T
        w = u_ref[pl.ds(h * span, span), :]
        k_hi, k_lo = split2(kt)
        w_hi, w_lo = split2(w)
        delta = (
            jnp.dot(k_hi, w_hi, preferred_element_type=f32)
            + jnp.dot(k_hi, w_lo, preferred_element_type=f32)
            + jnp.dot(k_lo, w_hi, preferred_element_type=f32)
        )
        so_ref[0, h] = (total[h:h + 1, :] * s_ref[0, h].astype(f32) + delta).astype(so_ref.dtype)


def recurrence(slots, states, query_rows, key_rows, value_rows, gate_rows, beta_logit, decay_logit, core_gain):
    batch, heads, width, _ = states.shape
    steps = query_rows.shape[1]
    key_heads = query_rows.shape[-1] // width
    repeats = heads // key_heads
    span = 2 * steps
    kq = jnp.concatenate(
        [key_rows.reshape(batch, steps, key_heads, width), query_rows.reshape(batch, steps, key_heads, width)], axis=1
    )
    kq = jnp.repeat(kq.transpose(0, 2, 1, 3), repeats, axis=1).reshape(batch, heads * span, width)
    values = value_rows.reshape(batch, steps, heads, width)
    gates = gate_rows.reshape(batch, steps, heads, width)
    decay = decay_logit.astype(f32).transpose(0, 2, 1)
    beta = beta_logit.astype(f32).transpose(0, 2, 1)
    gain = core_gain.reshape(1, width)
    state_in = pl.BlockSpec((1, heads, width, width), lambda i, slot: (i, 0, 0, 0))
    state_out = pl.BlockSpec((1, heads, width, width), lambda i, slot: (slot[i], 0, 0, 0))
    row_spec = pl.BlockSpec((1, steps, heads, width), lambda i, slot: (i, 0, 0, 0))
    coef_spec = pl.BlockSpec((1, heads, steps), lambda i, slot: (i, 0, 0))
    fresh, core = pl.pallas_call(
        recur_kernel,
        grid_spec=pltpu.PrefetchScalarGridSpec(
            num_scalar_prefetch=1,
            grid=(batch,),
            in_specs=[
                state_in,
                pl.BlockSpec((1, heads * span, width), lambda i, slot: (i, 0, 0)),
                row_spec,
                row_spec,
                coef_spec,
                coef_spec,
                pl.BlockSpec((1, width), lambda i, slot: (0, 0)),
            ],
            out_specs=[state_out, pl.BlockSpec((1, steps, heads * width), lambda i, slot: (i, 0, 0))],
            scratch_shapes=[pltpu.VMEM((heads * span, width), f32)] * 3 + [pltpu.VMEM((steps * heads, width), f32)],
        ),
        out_shape=[
            jax.ShapeDtypeStruct(states.shape, bf16),
            jax.ShapeDtypeStruct((batch, steps, heads * width), bf16),
        ],
    )(slots, states, kq, values, gates, decay, beta, gain)
    return fresh, core


def unit_rows(values):
    return values * lax.rsqrt(jnp.sum(values * values, -1, keepdims=True) + epsilon)


def delta_block(
    state_in, query_rows, key_rows, value_rows, gate_rows, beta_logit, decay_logit, core_gain
):
    batch_size = state_in.shape[0]
    head_count = decay_logit.shape[-1]
    head_width = state_in.shape[-1]
    key_heads = query_rows.shape[-1] // head_width
    repeats = head_count // key_heads
    memory_state = state_in.astype(jnp.float32)
    outputs = []
    for position in range(query_rows.shape[1]):
        queries = unit_rows(
            query_rows[:, position].astype(jnp.float32).reshape(batch_size, key_heads, head_width)
        )
        queries = jnp.repeat(queries, repeats, axis=1) * head_width ** (-0.5)
        key_units = unit_rows(
            key_rows[:, position].astype(jnp.float32).reshape(batch_size, key_heads, head_width)
        )
        key_units = jnp.repeat(key_units, repeats, axis=1)
        values = (
            value_rows[:, position].astype(jnp.float32).reshape(batch_size, head_count, head_width)
        )
        decays = jax.nn.sigmoid(decay_logit[:, position].astype(jnp.float32))
        strength = jax.nn.sigmoid(beta_logit[:, position].astype(jnp.float32))
        memory_state = memory_state * decays[:, :, None, None]
        memory = jnp.einsum(
            "bhkv,bhk->bhv", memory_state, key_units, precision=lax.Precision.HIGHEST
        )
        update = (values - memory) * strength[:, :, None]
        memory_state = memory_state + key_units[:, :, :, None] * update[:, :, None, :]
        reading = jnp.einsum(
            "bhkv,bhk->bhv", memory_state, queries, precision=lax.Precision.HIGHEST
        )
        scaled = reading * lax.rsqrt(jnp.mean(reading * reading, -1, keepdims=True) + epsilon)
        gate_vals = (
            gate_rows[:, position].astype(jnp.float32).reshape(batch_size, head_count, head_width)
        )
        gated_out = scaled * core_gain * jax.nn.silu(gate_vals)
        outputs.append(gated_out.reshape(batch_size, head_count * head_width).astype(jnp.bfloat16))
    return (memory_state.astype(jnp.bfloat16), jnp.stack(outputs, axis=1))


def migrate_kernel(src_hbm, tag_hbm, dst_hbm, tag_out, send_sem, recv_sem, tag_send, tag_recv, local_sem):
    lanes = src_hbm.shape[0]
    group = lax.axis_index("dp")
    me = lax.axis_index("ep")
    mesh_ids = pl.DeviceIdType.MESH
    barrier = pltpu.get_barrier_semaphore()
    for i in range(1, lanes):
        pl.semaphore_signal(barrier, 1, device_id=(group, lax.rem(me + i, lanes)), device_id_type=mesh_ids)
    pl.semaphore_wait(barrier, lanes - 1)
    own = pltpu.make_async_copy(src_hbm.at[me], dst_hbm.at[me], local_sem.at[0])
    own.start()
    own_tag = pltpu.make_async_copy(tag_hbm.at[me], tag_out.at[me], local_sem.at[1])
    own_tag.start()
    copies = []
    for i in range(1, lanes):
        peer = lax.rem(me + i, lanes)
        for source, target, sent, landed in ((tag_hbm, tag_out, tag_send, tag_recv), (src_hbm, dst_hbm, send_sem, recv_sem)):
            copy = pltpu.make_async_remote_copy(
                source.at[peer],
                target.at[me],
                sent.at[i - 1],
                landed.at[i - 1],
                device_id=(group, peer),
                device_id_type=mesh_ids,
            )
            copy.start()
            copies.append(copy)
    own.wait()
    own_tag.wait()
    for copy in copies:
        copy.wait()


def migrate(rows, tags):
    lanes = rows.shape[0]
    any_spec = pl.BlockSpec(memory_space=pl.ANY)
    return pl.pallas_call(
        migrate_kernel,
        in_specs=[any_spec, any_spec],
        out_specs=[any_spec, any_spec],
        out_shape=[
            jax.ShapeDtypeStruct(rows.shape, rows.dtype),
            jax.ShapeDtypeStruct(tags.shape, tags.dtype),
        ],
        scratch_shapes=[
            pltpu.SemaphoreType.DMA((lanes - 1,)),
            pltpu.SemaphoreType.DMA((lanes - 1,)),
            pltpu.SemaphoreType.DMA((lanes - 1,)),
            pltpu.SemaphoreType.DMA((lanes - 1,)),
            pltpu.SemaphoreType.DMA((2,)),
        ],
        compiler_params=pltpu.CompilerParams(collective_id=0, has_side_effects=True),
        cost_estimate=pl.CostEstimate(flops=0, transcendentals=0, bytes_accessed=2 * rows.size * rows.dtype.itemsize),
    )(rows, tags)

def project_kernel(rows_ref, weight_ref, out_ref, gathered, product, send_a, recv_a, send_b, recv_b, local_sem):
    lanes = gathered.shape[0]
    count = rows_ref.shape[0]
    block = weight_ref.shape[1]
    group = lax.axis_index("dp")
    me = lax.axis_index("ep")
    mesh_ids = pl.DeviceIdType.MESH
    barrier = pltpu.get_barrier_semaphore()
    for i in range(1, lanes):
        pl.semaphore_signal(barrier, 1, device_id=(group, lax.rem(me + i, lanes)), device_id_type=mesh_ids)
    pl.semaphore_wait(barrier, lanes - 1)
    own = pltpu.make_async_copy(rows_ref, gathered.at[me], local_sem)
    own.start()
    sends = []
    for i in range(1, lanes):
        copy = pltpu.make_async_remote_copy(
            rows_ref, gathered.at[me], send_a.at[i - 1], recv_a.at[i - 1],
            device_id=(group, lax.rem(me + i, lanes)), device_id_type=mesh_ids,
        )
        copy.start()
        sends.append(copy)
    own.wait()
    for copy in sends:
        copy.wait()
    width = gathered.shape[-1]
    stacked = gathered[...].reshape(lanes * count, width)
    product[...] = (
        jnp.dot(stacked, weight_ref[...], preferred_element_type=jnp.float32)
        .astype(product.dtype)
        .reshape(lanes, count, block)
    )
    columns = pl.ds(pl.multiple_of(me * block, block), block)
    back = pltpu.make_async_copy(product.at[me], out_ref.at[:, columns], local_sem)
    back.start()
    replies = []
    for i in range(1, lanes):
        peer = lax.rem(me + i, lanes)
        copy = pltpu.make_async_remote_copy(
            product.at[peer], out_ref.at[:, columns], send_b.at[i - 1], recv_b.at[i - 1],
            device_id=(group, peer), device_id_type=mesh_ids,
        )
        copy.start()
        replies.append(copy)
    back.wait()
    for copy in replies:
        copy.wait()


def project(rows, weight):
    lanes = lax.axis_size("ep")
    count, width = rows.shape
    block = weight.shape[1]
    vmem = pl.BlockSpec(memory_space=pltpu.VMEM)
    return pl.pallas_call(
        project_kernel,
        in_specs=[vmem, vmem],
        out_specs=vmem,
        out_shape=jax.ShapeDtypeStruct((count, lanes * block), rows.dtype),
        scratch_shapes=[
            pltpu.VMEM((lanes, count, width), rows.dtype),
            pltpu.VMEM((lanes, count, block), rows.dtype),
            pltpu.SemaphoreType.DMA((lanes - 1,)),
            pltpu.SemaphoreType.DMA((lanes - 1,)),
            pltpu.SemaphoreType.DMA((lanes - 1,)),
            pltpu.SemaphoreType.DMA((lanes - 1,)),
            pltpu.SemaphoreType.DMA,
        ],
        compiler_params=pltpu.CompilerParams(collective_id=1, has_side_effects=True),
    )(rows, weight)


def place_kernel(place_ref, in_hbm, out_hbm, held, in_sem, out_sem):
    count = in_hbm.shape[0]
    loads = []
    for j in range(count):
        load = pltpu.make_async_copy(in_hbm.at[j], held.at[j], in_sem.at[j])
        load.start()
        loads.append(load)
    stores = []
    for j in range(count):
        loads[j].wait()
        store = pltpu.make_async_copy(held.at[j], out_hbm.at[place_ref[j]], out_sem.at[j])
        store.start()
        stores.append(store)
    for store in stores:
        store.wait()


def place_rows(rows, places):
    count = rows.shape[0]
    any_spec = pl.BlockSpec(memory_space=pl.ANY)
    return pl.pallas_call(
        place_kernel,
        in_specs=[pl.BlockSpec(memory_space=pltpu.SMEM), any_spec],
        out_specs=any_spec,
        out_shape=jax.ShapeDtypeStruct(rows.shape, rows.dtype),
        scratch_shapes=[
            pltpu.VMEM(rows.shape, rows.dtype),
            pltpu.SemaphoreType.DMA((count,)),
            pltpu.SemaphoreType.DMA((count,)),
        ],
        compiler_params=pltpu.CompilerParams(vmem_limit_bytes=48 * 1024 * 1024),
    )(places, rows)

def rms_scale(values, gain):
    return values * lax.rsqrt(jnp.mean(values * values, -1, keepdims=True) + epsilon) * gain


def expert_apply(chosen_rows, gate_up, down_weight):
    hidden_units = down_weight.shape[0]
    joined = jnp.dot(chosen_rows, gate_up, preferred_element_type=jnp.float32)
    active = (jax.nn.silu(joined[:, :hidden_units]) * joined[:, hidden_units:]).astype(jnp.bfloat16)
    return jnp.dot(active, down_weight, preferred_element_type=jnp.float32).astype(jnp.bfloat16)


def pack(values, positions, lane_count):
    zeroed = jnp.zeros(values.shape, values.dtype)
    placed = zeroed.at[positions].set(values)
    return placed.reshape((lane_count, values.shape[0] // lane_count) + values.shape[1:])


def unpack(values):
    return values.reshape((values.shape[0] * values.shape[1],) + values.shape[2:])


def shards(
    states,
    query_rows,
    key_rows,
    value_rows,
    gate_rows,
    beta_logit,
    decay_logit,
    residual,
    route_ids,
    route_prob,
    out_weight,
    core_gain,
    moe_gain,
    gate_up,
    down_weight,
    new_home,
):
    req_count = states.shape[0]
    step_count = query_rows.shape[1]
    model_width = residual.shape[-1]
    ep_size = lax.axis_size("ep")
    dp_size = lax.axis_size("dp")
    target = new_home // req_count % ep_size
    new_place = new_home % req_count
    fresh_states, core_out = recurrence(
        target, states, query_rows, key_rows, value_rows, gate_rows, beta_logit, decay_logit, core_gain
    )
    packed_place = jnp.zeros_like(new_place).at[target].set(new_place)
    tags = jnp.broadcast_to(packed_place[:, None, None], (ep_size, 8, 128))
    moved_rows, moved_tags = migrate(fresh_states, tags)
    moved_out = place_rows(moved_rows, moved_tags[:, 0, 0])
    token_count = req_count * step_count
    core_flat = core_out.reshape(token_count, core_out.shape[-1])
    attention = project(core_flat, out_weight)
    hidden = (
        residual.reshape(token_count, model_width).astype(jnp.float32)
        + attention.astype(jnp.float32)
    ).astype(jnp.bfloat16)
    normed = rms_scale(hidden.astype(jnp.float32), moe_gain).astype(jnp.bfloat16)
    top_count = route_ids.shape[-1]
    experts = dp_size * ep_size
    capacity = (token_count * top_count + experts - 1) // experts + 1
    flat_ids = route_ids.reshape(-1)
    onehot = (flat_ids[:, None] == jnp.arange(experts, dtype=jnp.int32)[None, :]).astype(jnp.int32)
    route_rank = jnp.sum(jnp.cumsum(onehot, axis=0) * onehot, axis=1) - 1
    slot_index = flat_ids * capacity + route_rank
    slot_count = experts * capacity
    match = slot_index[None, :] == jnp.arange(slot_count, dtype=jnp.int32)[:, None]
    match = match.reshape(experts, capacity, token_count, top_count)
    pick = jnp.any(match, axis=-1).astype(jnp.bfloat16)
    lane_count = 128
    chunks = model_width // lane_count
    normed_tiles = normed.reshape(token_count, chunks, lane_count)
    outgoing = jnp.einsum(
        "esk,kcl->escl", pick, normed_tiles, preferred_element_type=jnp.float32
    ).astype(jnp.bfloat16)
    outgoing = outgoing.reshape(experts, capacity * chunks, lane_count)
    arrived = lax.all_to_all(outgoing, ("dp", "ep"), 0, 0, tiled=True)
    arrived = arrived.reshape(experts, capacity, chunks, lane_count)
    hidden_units = down_weight.shape[1]
    gate_tiles = gate_up[0].reshape(chunks, lane_count, gate_up.shape[-1])
    joined = jnp.einsum("escl,clf->esf", arrived, gate_tiles, preferred_element_type=jnp.float32)
    active = (jax.nn.silu(joined[..., :hidden_units]) * joined[..., hidden_units:]).astype(jnp.bfloat16)
    down_tiles = down_weight[0].reshape(hidden_units, chunks, lane_count)
    result = jnp.einsum(
        "esf,fcl->escl", active, down_tiles, preferred_element_type=jnp.float32
    ).astype(jnp.bfloat16)
    result = result.reshape(experts, capacity * chunks, lane_count)
    returned = lax.all_to_all(result, ("dp", "ep"), 0, 0, tiled=True)
    returned = returned.reshape(experts, capacity, chunks, lane_count)
    weights = route_prob.reshape(token_count, top_count)
    weights = weights / jnp.sum(weights, -1, keepdims=True)
    spread = jnp.sum(jnp.where(match, weights[None, None, :, :], 0.0), axis=-1)
    high = spread.astype(jnp.bfloat16)
    rest = spread - high.astype(jnp.float32)
    middle = rest.astype(jnp.bfloat16)
    low = (rest - middle.astype(jnp.float32)).astype(jnp.bfloat16)
    parts = jnp.concatenate([high, middle, low], axis=-1)
    combined = jnp.einsum("esk,escl->kcl", parts, returned, preferred_element_type=jnp.float32)
    combined = combined.reshape(3, token_count, chunks, lane_count).sum(axis=0)
    combined = combined.reshape(token_count, model_width)
    mixed_out = (
        (hidden.astype(jnp.float32) + combined)
        .astype(jnp.bfloat16)
        .reshape(req_count, step_count, model_width)
    )
    return (mixed_out, moved_out)


def solution(mesh):
    placed = (
        P(("dp", "ep"), None, None, None),
        P(("dp", "ep"), None, None),
        P(("dp", "ep"), None, None),
        P(("dp", "ep"), None, None),
        P(("dp", "ep"), None, None),
        P(("dp", "ep"), None, None),
        P(("dp", "ep"), None, None),
        P(("dp", "ep"), None, None),
        P(("dp", "ep"), None, None),
        P(("dp", "ep"), None, None),
        P(None, "ep"),
        P(),
        P(),
        P(("dp", "ep"), None, None),
        P(("dp", "ep"), None, None),
        P(("dp", "ep")),
    )
    return jax.shard_map(
        shards,
        mesh=mesh,
        in_specs=placed,
        out_specs=(P(("dp", "ep"), None, None), P(("dp", "ep"), None, None, None)),
        check_vma=False,
    )
```

```python
import jax
import jax.numpy as jnp
from jax import lax
from jax.sharding import PartitionSpec as P

import functools
from jax.experimental import pallas as pl
from jax.experimental.pallas import tpu as pltpu

epsilon = 1e-06
f32 = jnp.float32
bf16 = jnp.bfloat16


def split2(x):
    hi = x.astype(bf16)
    lo = (x - hi.astype(f32)).astype(bf16)
    return hi, lo


def recur_kernel(slot_ref, s_ref, kq_ref, v_ref, g_ref, dec_ref, beta_ref, gain_ref, so_ref, co_ref, n_ref, r_ref, u_ref, c_ref):
    heads = s_ref.shape[1]
    width = s_ref.shape[-1]
    steps = v_ref.shape[1]
    span = 2 * steps
    kq = kq_ref[0].astype(f32)
    kq = kq * lax.rsqrt(jnp.sum(kq * kq, -1, keepdims=True) + epsilon)
    row = lax.broadcasted_iota(jnp.int32, kq.shape, 0)
    kq = jnp.where(row % span >= steps, kq * width ** (-0.5), kq)
    n_ref[...] = kq
    for h in range(heads):
        p = n_ref[pl.ds(h * span, span), :]
        hi = p.astype(bf16).astype(f32)
        rest = p - hi
        mid = rest.astype(bf16).astype(f32)
        lo = rest - mid
        lhs = jnp.concatenate([hi, mid, lo], axis=0).astype(bf16)
        res = jnp.dot(lhs, s_ref[0, h], preferred_element_type=f32)
        r_ref[pl.ds(h * span, span), :] = (res[0:span] + res[span:2 * span]) + res[2 * span:3 * span]
    decay = jax.nn.sigmoid(dec_ref[0])
    strength = jax.nn.sigmoid(beta_ref[0])
    gain = gain_ref[...]
    keys = [n_ref[pl.ds(t, heads, stride=span), :] for t in range(steps)]
    queries = [n_ref[pl.ds(steps + t, heads, stride=span), :] for t in range(steps)]
    u_ref[...] = jnp.zeros(u_ref.shape, f32)
    updates = []
    carried = []
    total = None
    for t in range(steps):
        a_t = decay[:, t:t + 1]
        b_t = strength[:, t:t + 1]
        total = a_t if t == 0 else total * a_t
        carried = [c * a_t for c in carried]
        memory = total * r_ref[pl.ds(t, heads, stride=span), :]
        for j in range(t):
            kk = jnp.sum(keys[j] * keys[t], -1, keepdims=True)
            memory = memory + (carried[j] * kk) * updates[j]
        values = v_ref[0, t].astype(f32)
        update = (values - memory) * b_t
        updates.append(update)
        carried.append(jnp.ones_like(a_t))
        reading = total * r_ref[pl.ds(steps + t, heads, stride=span), :]
        for j in range(t + 1):
            qk = jnp.sum(keys[j] * queries[t], -1, keepdims=True)
            coef = qk if j == t else carried[j] * qk
            reading = reading + coef * updates[j]
        scaled = reading * lax.rsqrt(jnp.mean(reading * reading, -1, keepdims=True) + epsilon)
        gate_vals = g_ref[0, t].astype(f32)
        c_ref[pl.ds(t * heads, heads), :] = scaled * gain * (gate_vals * jax.nn.sigmoid(gate_vals))
    for j in range(steps):
        u_ref[pl.ds(j, heads, stride=span), :] = carried[j] * updates[j]
    for h in range(heads):
        co_ref[0, :, pl.ds(h * width, width)] = c_ref[pl.ds(h, steps, stride=heads), :].astype(co_ref.dtype)
    for h in range(heads):
        kt = n_ref[pl.ds(h * span, span), :].T
        w = u_ref[pl.ds(h * span, span), :]
        k_hi, k_lo = split2(kt)
        w_hi, w_lo = split2(w)
        delta = (
            jnp.dot(k_hi, w_hi, preferred_element_type=f32)
            + jnp.dot(k_hi, w_lo, preferred_element_type=f32)
            + jnp.dot(k_lo, w_hi, preferred_element_type=f32)
        )
        so_ref[0, h] = (total[h:h + 1, :] * s_ref[0, h].astype(f32) + delta).astype(so_ref.dtype)


def recurrence(slots, states, query_rows, key_rows, value_rows, gate_rows, beta_logit, decay_logit, core_gain):
    batch, heads, width, _ = states.shape
    steps = query_rows.shape[1]
    key_heads = query_rows.shape[-1] // width
    repeats = heads // key_heads
    span = 2 * steps
    kq = jnp.concatenate(
        [key_rows.reshape(batch, steps, key_heads, width), query_rows.reshape(batch, steps, key_heads, width)], axis=1
    )
    kq = jnp.repeat(kq.transpose(0, 2, 1, 3), repeats, axis=1).reshape(batch, heads * span, width)
    values = value_rows.reshape(batch, steps, heads, width)
    gates = gate_rows.reshape(batch, steps, heads, width)
    decay = decay_logit.astype(f32).transpose(0, 2, 1)
    beta = beta_logit.astype(f32).transpose(0, 2, 1)
    gain = core_gain.reshape(1, width)
    state_in = pl.BlockSpec((1, heads, width, width), lambda i, slot: (i, 0, 0, 0))
    state_out = pl.BlockSpec((1, heads, width, width), lambda i, slot: (slot[i], 0, 0, 0))
    row_spec = pl.BlockSpec((1, steps, heads, width), lambda i, slot: (i, 0, 0, 0))
    coef_spec = pl.BlockSpec((1, heads, steps), lambda i, slot: (i, 0, 0))
    fresh, core = pl.pallas_call(
        recur_kernel,
        grid_spec=pltpu.PrefetchScalarGridSpec(
            num_scalar_prefetch=1,
            grid=(batch,),
            in_specs=[
                state_in,
                pl.BlockSpec((1, heads * span, width), lambda i, slot: (i, 0, 0)),
                row_spec,
                row_spec,
                coef_spec,
                coef_spec,
                pl.BlockSpec((1, width), lambda i, slot: (0, 0)),
            ],
            out_specs=[state_out, pl.BlockSpec((1, steps, heads * width), lambda i, slot: (i, 0, 0))],
            scratch_shapes=[pltpu.VMEM((heads * span, width), f32)] * 3 + [pltpu.VMEM((steps * heads, width), f32)],
        ),
        out_shape=[
            jax.ShapeDtypeStruct(states.shape, bf16),
            jax.ShapeDtypeStruct((batch, steps, heads * width), bf16),
        ],
    )(slots, states, kq, values, gates, decay, beta, gain)
    return fresh, core


def unit_rows(values):
    return values * lax.rsqrt(jnp.sum(values * values, -1, keepdims=True) + epsilon)


def delta_block(
    state_in, query_rows, key_rows, value_rows, gate_rows, beta_logit, decay_logit, core_gain
):
    batch_size = state_in.shape[0]
    head_count = decay_logit.shape[-1]
    head_width = state_in.shape[-1]
    key_heads = query_rows.shape[-1] // head_width
    repeats = head_count // key_heads
    memory_state = state_in.astype(jnp.float32)
    outputs = []
    for position in range(query_rows.shape[1]):
        queries = unit_rows(
            query_rows[:, position].astype(jnp.float32).reshape(batch_size, key_heads, head_width)
        )
        queries = jnp.repeat(queries, repeats, axis=1) * head_width ** (-0.5)
        key_units = unit_rows(
            key_rows[:, position].astype(jnp.float32).reshape(batch_size, key_heads, head_width)
        )
        key_units = jnp.repeat(key_units, repeats, axis=1)
        values = (
            value_rows[:, position].astype(jnp.float32).reshape(batch_size, head_count, head_width)
        )
        decays = jax.nn.sigmoid(decay_logit[:, position].astype(jnp.float32))
        strength = jax.nn.sigmoid(beta_logit[:, position].astype(jnp.float32))
        memory_state = memory_state * decays[:, :, None, None]
        memory = jnp.einsum(
            "bhkv,bhk->bhv", memory_state, key_units, precision=lax.Precision.HIGHEST
        )
        update = (values - memory) * strength[:, :, None]
        memory_state = memory_state + key_units[:, :, :, None] * update[:, :, None, :]
        reading = jnp.einsum(
            "bhkv,bhk->bhv", memory_state, queries, precision=lax.Precision.HIGHEST
        )
        scaled = reading * lax.rsqrt(jnp.mean(reading * reading, -1, keepdims=True) + epsilon)
        gate_vals = (
            gate_rows[:, position].astype(jnp.float32).reshape(batch_size, head_count, head_width)
        )
        gated_out = scaled * core_gain * jax.nn.silu(gate_vals)
        outputs.append(gated_out.reshape(batch_size, head_count * head_width).astype(jnp.bfloat16))
    return (memory_state.astype(jnp.bfloat16), jnp.stack(outputs, axis=1))


def migrate_kernel(src_hbm, tag_hbm, dst_hbm, tag_out, send_sem, recv_sem, tag_send, tag_recv, local_sem):
    lanes = src_hbm.shape[0]
    group = lax.axis_index("dp")
    me = lax.axis_index("ep")
    mesh_ids = pl.DeviceIdType.MESH
    barrier = pltpu.get_barrier_semaphore()
    for i in range(1, lanes):
        pl.semaphore_signal(barrier, 1, device_id=(group, lax.rem(me + i, lanes)), device_id_type=mesh_ids)
    pl.semaphore_wait(barrier, lanes - 1)
    own = pltpu.make_async_copy(src_hbm.at[me], dst_hbm.at[me], local_sem.at[0])
    own.start()
    own_tag = pltpu.make_async_copy(tag_hbm.at[me], tag_out.at[me], local_sem.at[1])
    own_tag.start()
    copies = []
    for i in range(1, lanes):
        peer = lax.rem(me + i, lanes)
        for source, target, sent, landed in ((tag_hbm, tag_out, tag_send, tag_recv), (src_hbm, dst_hbm, send_sem, recv_sem)):
            copy = pltpu.make_async_remote_copy(
                source.at[peer],
                target.at[me],
                sent.at[i - 1],
                landed.at[i - 1],
                device_id=(group, peer),
                device_id_type=mesh_ids,
            )
            copy.start()
            copies.append(copy)
    own.wait()
    own_tag.wait()
    for copy in copies:
        copy.wait()


def migrate(rows, tags):
    lanes = rows.shape[0]
    any_spec = pl.BlockSpec(memory_space=pl.ANY)
    return pl.pallas_call(
        migrate_kernel,
        in_specs=[any_spec, any_spec],
        out_specs=[any_spec, any_spec],
        out_shape=[
            jax.ShapeDtypeStruct(rows.shape, rows.dtype),
            jax.ShapeDtypeStruct(tags.shape, tags.dtype),
        ],
        scratch_shapes=[
            pltpu.SemaphoreType.DMA((lanes - 1,)),
            pltpu.SemaphoreType.DMA((lanes - 1,)),
            pltpu.SemaphoreType.DMA((lanes - 1,)),
            pltpu.SemaphoreType.DMA((lanes - 1,)),
            pltpu.SemaphoreType.DMA((2,)),
        ],
        compiler_params=pltpu.CompilerParams(collective_id=0, has_side_effects=True),
        cost_estimate=pl.CostEstimate(flops=0, transcendentals=0, bytes_accessed=2 * rows.size * rows.dtype.itemsize),
    )(rows, tags)

def project_kernel(rows_ref, weight_ref, out_ref, gathered, product, send_a, recv_a, send_b, recv_b, local_sem):
    lanes = gathered.shape[0]
    count = rows_ref.shape[0]
    block = weight_ref.shape[1]
    group = lax.axis_index("dp")
    me = lax.axis_index("ep")
    mesh_ids = pl.DeviceIdType.MESH
    barrier = pltpu.get_barrier_semaphore()
    for i in range(1, lanes):
        pl.semaphore_signal(barrier, 1, device_id=(group, lax.rem(me + i, lanes)), device_id_type=mesh_ids)
    pl.semaphore_wait(barrier, lanes - 1)
    own = pltpu.make_async_copy(rows_ref, gathered.at[me], local_sem)
    own.start()
    sends = []
    for i in range(1, lanes):
        copy = pltpu.make_async_remote_copy(
            rows_ref, gathered.at[me], send_a.at[i - 1], recv_a.at[i - 1],
            device_id=(group, lax.rem(me + i, lanes)), device_id_type=mesh_ids,
        )
        copy.start()
        sends.append(copy)
    own.wait()
    for copy in sends:
        copy.wait()
    width = gathered.shape[-1]
    stacked = gathered[...].reshape(lanes * count, width)
    product[...] = (
        jnp.dot(stacked, weight_ref[...], preferred_element_type=jnp.float32)
        .astype(product.dtype)
        .reshape(lanes, count, block)
    )
    columns = pl.ds(pl.multiple_of(me * block, block), block)
    back = pltpu.make_async_copy(product.at[me], out_ref.at[:, columns], local_sem)
    back.start()
    replies = []
    for i in range(1, lanes):
        peer = lax.rem(me + i, lanes)
        copy = pltpu.make_async_remote_copy(
            product.at[peer], out_ref.at[:, columns], send_b.at[i - 1], recv_b.at[i - 1],
            device_id=(group, peer), device_id_type=mesh_ids,
        )
        copy.start()
        replies.append(copy)
    back.wait()
    for copy in replies:
        copy.wait()


def project(rows, weight):
    lanes = lax.axis_size("ep")
    count, width = rows.shape
    block = weight.shape[1]
    vmem = pl.BlockSpec(memory_space=pltpu.VMEM)
    return pl.pallas_call(
        project_kernel,
        in_specs=[vmem, vmem],
        out_specs=vmem,
        out_shape=jax.ShapeDtypeStruct((count, lanes * block), rows.dtype),
        scratch_shapes=[
            pltpu.VMEM((lanes, count, width), rows.dtype),
            pltpu.VMEM((lanes, count, block), rows.dtype),
            pltpu.SemaphoreType.DMA((lanes - 1,)),
            pltpu.SemaphoreType.DMA((lanes - 1,)),
            pltpu.SemaphoreType.DMA((lanes - 1,)),
            pltpu.SemaphoreType.DMA((lanes - 1,)),
            pltpu.SemaphoreType.DMA,
        ],
        compiler_params=pltpu.CompilerParams(collective_id=1, has_side_effects=True),
    )(rows, weight)


def place_kernel(place_ref, in_hbm, out_hbm, held, in_sem, out_sem):
    count = in_hbm.shape[0]
    loads = []
    for j in range(count):
        load = pltpu.make_async_copy(in_hbm.at[j], held.at[j], in_sem.at[j])
        load.start()
        loads.append(load)
    stores = []
    for j in range(count):
        loads[j].wait()
        store = pltpu.make_async_copy(held.at[j], out_hbm.at[place_ref[j, 0, 0]], out_sem.at[j])
        store.start()
        stores.append(store)
    for store in stores:
        store.wait()


def place_rows(rows, places):
    count = rows.shape[0]
    any_spec = pl.BlockSpec(memory_space=pl.ANY)
    return pl.pallas_call(
        place_kernel,
        in_specs=[pl.BlockSpec(memory_space=pltpu.SMEM), any_spec],
        out_specs=any_spec,
        out_shape=jax.ShapeDtypeStruct(rows.shape, rows.dtype),
        scratch_shapes=[
            pltpu.VMEM(rows.shape, rows.dtype),
            pltpu.SemaphoreType.DMA((count,)),
            pltpu.SemaphoreType.DMA((count,)),
        ],
        compiler_params=pltpu.CompilerParams(vmem_limit_bytes=48 * 1024 * 1024),
    )(places, rows)

def rms_scale(values, gain):
    return values * lax.rsqrt(jnp.mean(values * values, -1, keepdims=True) + epsilon) * gain


def expert_apply(chosen_rows, gate_up, down_weight):
    hidden_units = down_weight.shape[0]
    joined = jnp.dot(chosen_rows, gate_up, preferred_element_type=jnp.float32)
    active = (jax.nn.silu(joined[:, :hidden_units]) * joined[:, hidden_units:]).astype(jnp.bfloat16)
    return jnp.dot(active, down_weight, preferred_element_type=jnp.float32).astype(jnp.bfloat16)


def pack(values, positions, lane_count):
    zeroed = jnp.zeros(values.shape, values.dtype)
    placed = zeroed.at[positions].set(values)
    return placed.reshape((lane_count, values.shape[0] // lane_count) + values.shape[1:])


def unpack(values):
    return values.reshape((values.shape[0] * values.shape[1],) + values.shape[2:])


def shards(
    states,
    query_rows,
    key_rows,
    value_rows,
    gate_rows,
    beta_logit,
    decay_logit,
    residual,
    route_ids,
    route_prob,
    out_weight,
    core_gain,
    moe_gain,
    gate_up,
    down_weight,
    new_home,
):
    req_count = states.shape[0]
    step_count = query_rows.shape[1]
    model_width = residual.shape[-1]
    ep_size = lax.axis_size("ep")
    dp_size = lax.axis_size("dp")
    target = new_home // req_count % ep_size
    new_place = new_home % req_count
    fresh_states, core_out = recurrence(
        target, states, query_rows, key_rows, value_rows, gate_rows, beta_logit, decay_logit, core_gain
    )
    packed_place = jnp.zeros_like(new_place).at[target].set(new_place)
    tags = jnp.broadcast_to(packed_place[:, None, None], (ep_size, 1, 128))
    moved_rows, moved_tags = migrate(fresh_states, tags)
    moved_out = place_rows(moved_rows, moved_tags)
    token_count = req_count * step_count
    core_flat = core_out.reshape(token_count, core_out.shape[-1])
    attention = project(core_flat, out_weight)
    hidden = (
        residual.reshape(token_count, model_width).astype(jnp.float32)
        + attention.astype(jnp.float32)
    ).astype(jnp.bfloat16)
    normed = rms_scale(hidden.astype(jnp.float32), moe_gain).astype(jnp.bfloat16)
    top_count = route_ids.shape[-1]
    experts = dp_size * ep_size
    capacity = (token_count * top_count + experts - 1) // experts + 1
    flat_ids = route_ids.reshape(-1)
    onehot = (flat_ids[:, None] == jnp.arange(experts, dtype=jnp.int32)[None, :]).astype(jnp.int32)
    route_rank = jnp.sum(jnp.cumsum(onehot, axis=0) * onehot, axis=1) - 1
    slot_index = flat_ids * capacity + route_rank
    slot_count = experts * capacity
    match = slot_index[None, :] == jnp.arange(slot_count, dtype=jnp.int32)[:, None]
    match = match.reshape(experts, capacity, token_count, top_count)
    pick = jnp.any(match, axis=-1).astype(jnp.bfloat16)
    lane_count = 128
    chunks = model_width // lane_count
    normed_tiles = normed.reshape(token_count, chunks, lane_count)
    outgoing = jnp.einsum(
        "esk,kcl->escl", pick, normed_tiles, preferred_element_type=jnp.float32
    ).astype(jnp.bfloat16)
    outgoing = outgoing.reshape(experts, capacity * chunks, lane_count)
    arrived = lax.all_to_all(outgoing, ("dp", "ep"), 0, 0, tiled=True)
    arrived = arrived.reshape(experts, capacity, chunks, lane_count)
    hidden_units = down_weight.shape[1]
    gate_tiles = gate_up[0].reshape(chunks, lane_count, gate_up.shape[-1])
    joined = jnp.einsum("escl,clf->esf", arrived, gate_tiles, preferred_element_type=jnp.float32)
    active = (jax.nn.silu(joined[..., :hidden_units]) * joined[..., hidden_units:]).astype(jnp.bfloat16)
    down_tiles = down_weight[0].reshape(hidden_units, chunks, lane_count)
    result = jnp.einsum(
        "esf,fcl->escl", active, down_tiles, preferred_element_type=jnp.float32
    ).astype(jnp.bfloat16)
    result = result.reshape(experts, capacity * chunks, lane_count)
    returned = lax.all_to_all(result, ("dp", "ep"), 0, 0, tiled=True)
    returned = returned.reshape(experts, capacity, chunks, lane_count)
    weights = route_prob.reshape(token_count, top_count)
    weights = weights / jnp.sum(weights, -1, keepdims=True)
    spread = jnp.sum(jnp.where(match, weights[None, None, :, :], 0.0), axis=-1)
    high = spread.astype(jnp.bfloat16)
    rest = spread - high.astype(jnp.float32)
    middle = rest.astype(jnp.bfloat16)
    low = (rest - middle.astype(jnp.float32)).astype(jnp.bfloat16)
    parts = jnp.concatenate([high, middle, low], axis=-1)
    combined = jnp.einsum("esk,escl->kcl", parts, returned, preferred_element_type=jnp.float32)
    combined = combined.reshape(3, token_count, chunks, lane_count).sum(axis=0)
    combined = combined.reshape(token_count, model_width)
    mixed_out = (
        (hidden.astype(jnp.float32) + combined)
        .astype(jnp.bfloat16)
        .reshape(req_count, step_count, model_width)
    )
    return (mixed_out, moved_out)


def solution(mesh):
    placed = (
        P(("dp", "ep"), None, None, None),
        P(("dp", "ep"), None, None),
        P(("dp", "ep"), None, None),
        P(("dp", "ep"), None, None),
        P(("dp", "ep"), None, None),
        P(("dp", "ep"), None, None),
        P(("dp", "ep"), None, None),
        P(("dp", "ep"), None, None),
        P(("dp", "ep"), None, None),
        P(("dp", "ep"), None, None),
        P(None, "ep"),
        P(),
        P(),
        P(("dp", "ep"), None, None),
        P(("dp", "ep"), None, None),
        P(("dp", "ep")),
    )
    return jax.shard_map(
        shards,
        mesh=mesh,
        in_specs=placed,
        out_specs=(P(("dp", "ep"), None, None), P(("dp", "ep"), None, None, None)),
        check_vma=False,
    )
```

```python
import jax
import jax.numpy as jnp
from jax import lax
from jax.sharding import PartitionSpec as P

import functools
from jax.experimental import pallas as pl
from jax.experimental.pallas import tpu as pltpu

epsilon = 1e-06
f32 = jnp.float32
bf16 = jnp.bfloat16


def split2(x):
    hi = x.astype(bf16)
    lo = (x - hi.astype(f32)).astype(bf16)
    return hi, lo


def recur_kernel(slot_ref, s_ref, kq_ref, v_ref, g_ref, dec_ref, beta_ref, gain_ref, so_ref, co_ref, n_ref, r_ref, u_ref, c_ref):
    heads = s_ref.shape[1]
    width = s_ref.shape[-1]
    steps = v_ref.shape[1]
    span = 2 * steps
    kq = kq_ref[0].astype(f32)
    kq = kq * lax.rsqrt(jnp.sum(kq * kq, -1, keepdims=True) + epsilon)
    row = lax.broadcasted_iota(jnp.int32, kq.shape, 0)
    kq = jnp.where(row % span >= steps, kq * width ** (-0.5), kq)
    n_ref[...] = kq
    for h in range(heads):
        p = n_ref[pl.ds(h * span, span), :]
        hi = p.astype(bf16).astype(f32)
        rest = p - hi
        mid = rest.astype(bf16).astype(f32)
        lo = rest - mid
        lhs = jnp.concatenate([hi, mid, lo], axis=0).astype(bf16)
        res = jnp.dot(lhs, s_ref[0, h], preferred_element_type=f32)
        r_ref[pl.ds(h * span, span), :] = (res[0:span] + res[span:2 * span]) + res[2 * span:3 * span]
    decay = jax.nn.sigmoid(dec_ref[0].astype(f32)).T
    strength = jax.nn.sigmoid(beta_ref[0].astype(f32)).T
    gain = gain_ref[...]
    keys = [n_ref[pl.ds(t, heads, stride=span), :] for t in range(steps)]
    queries = [n_ref[pl.ds(steps + t, heads, stride=span), :] for t in range(steps)]
    u_ref[...] = jnp.zeros(u_ref.shape, f32)
    updates = []
    carried = []
    total = None
    for t in range(steps):
        a_t = decay[:, t:t + 1]
        b_t = strength[:, t:t + 1]
        total = a_t if t == 0 else total * a_t
        carried = [c * a_t for c in carried]
        memory = total * r_ref[pl.ds(t, heads, stride=span), :]
        for j in range(t):
            kk = jnp.sum(keys[j] * keys[t], -1, keepdims=True)
            memory = memory + (carried[j] * kk) * updates[j]
        values = v_ref[0, t].astype(f32)
        update = (values - memory) * b_t
        updates.append(update)
        carried.append(jnp.ones_like(a_t))
        reading = total * r_ref[pl.ds(steps + t, heads, stride=span), :]
        for j in range(t + 1):
            qk = jnp.sum(keys[j] * queries[t], -1, keepdims=True)
            coef = qk if j == t else carried[j] * qk
            reading = reading + coef * updates[j]
        scaled = reading * lax.rsqrt(jnp.mean(reading * reading, -1, keepdims=True) + epsilon)
        gate_vals = g_ref[0, t].astype(f32)
        c_ref[pl.ds(t * heads, heads), :] = scaled * gain * (gate_vals * jax.nn.sigmoid(gate_vals))
    for j in range(steps):
        u_ref[pl.ds(j, heads, stride=span), :] = carried[j] * updates[j]
    for h in range(heads):
        co_ref[0, :, pl.ds(h * width, width)] = c_ref[pl.ds(h, steps, stride=heads), :].astype(co_ref.dtype)
    for h in range(heads):
        kt = n_ref[pl.ds(h * span, span), :].T
        w = u_ref[pl.ds(h * span, span), :]
        k_hi, k_lo = split2(kt)
        w_hi, w_lo = split2(w)
        delta = (
            jnp.dot(k_hi, w_hi, preferred_element_type=f32)
            + jnp.dot(k_hi, w_lo, preferred_element_type=f32)
            + jnp.dot(k_lo, w_hi, preferred_element_type=f32)
        )
        so_ref[0, h] = (total[h:h + 1, :] * s_ref[0, h].astype(f32) + delta).astype(so_ref.dtype)


def recurrence(slots, states, query_rows, key_rows, value_rows, gate_rows, beta_logit, decay_logit, core_gain):
    batch, heads, width, _ = states.shape
    steps = query_rows.shape[1]
    key_heads = query_rows.shape[-1] // width
    repeats = heads // key_heads
    span = 2 * steps
    kq = jnp.concatenate(
        [key_rows.reshape(batch, steps, key_heads, width), query_rows.reshape(batch, steps, key_heads, width)], axis=1
    )
    kq = jnp.repeat(kq.transpose(0, 2, 1, 3), repeats, axis=1).reshape(batch, heads * span, width)
    values = value_rows.reshape(batch, steps, heads, width)
    gates = gate_rows.reshape(batch, steps, heads, width)
    decay = decay_logit
    beta = beta_logit
    gain = core_gain.reshape(1, width)
    state_in = pl.BlockSpec((1, heads, width, width), lambda i, slot: (i, 0, 0, 0))
    state_out = pl.BlockSpec((1, heads, width, width), lambda i, slot: (slot[i], 0, 0, 0))
    row_spec = pl.BlockSpec((1, steps, heads, width), lambda i, slot: (i, 0, 0, 0))
    coef_spec = pl.BlockSpec((1, steps, heads), lambda i, slot: (i, 0, 0))
    fresh, core = pl.pallas_call(
        recur_kernel,
        grid_spec=pltpu.PrefetchScalarGridSpec(
            num_scalar_prefetch=1,
            grid=(batch,),
            in_specs=[
                state_in,
                pl.BlockSpec((1, heads * span, width), lambda i, slot: (i, 0, 0)),
                row_spec,
                row_spec,
                coef_spec,
                coef_spec,
                pl.BlockSpec((1, width), lambda i, slot: (0, 0)),
            ],
            out_specs=[state_out, pl.BlockSpec((1, steps, heads * width), lambda i, slot: (i, 0, 0))],
            scratch_shapes=[pltpu.VMEM((heads * span, width), f32)] * 3 + [pltpu.VMEM((steps * heads, width), f32)],
        ),
        out_shape=[
            jax.ShapeDtypeStruct(states.shape, bf16),
            jax.ShapeDtypeStruct((batch, steps, heads * width), bf16),
        ],
    )(slots, states, kq, values, gates, decay, beta, gain)
    return fresh, core


def unit_rows(values):
    return values * lax.rsqrt(jnp.sum(values * values, -1, keepdims=True) + epsilon)


def delta_block(
    state_in, query_rows, key_rows, value_rows, gate_rows, beta_logit, decay_logit, core_gain
):
    batch_size = state_in.shape[0]
    head_count = decay_logit.shape[-1]
    head_width = state_in.shape[-1]
    key_heads = query_rows.shape[-1] // head_width
    repeats = head_count // key_heads
    memory_state = state_in.astype(jnp.float32)
    outputs = []
    for position in range(query_rows.shape[1]):
        queries = unit_rows(
            query_rows[:, position].astype(jnp.float32).reshape(batch_size, key_heads, head_width)
        )
        queries = jnp.repeat(queries, repeats, axis=1) * head_width ** (-0.5)
        key_units = unit_rows(
            key_rows[:, position].astype(jnp.float32).reshape(batch_size, key_heads, head_width)
        )
        key_units = jnp.repeat(key_units, repeats, axis=1)
        values = (
            value_rows[:, position].astype(jnp.float32).reshape(batch_size, head_count, head_width)
        )
        decays = jax.nn.sigmoid(decay_logit[:, position].astype(jnp.float32))
        strength = jax.nn.sigmoid(beta_logit[:, position].astype(jnp.float32))
        memory_state = memory_state * decays[:, :, None, None]
        memory = jnp.einsum(
            "bhkv,bhk->bhv", memory_state, key_units, precision=lax.Precision.HIGHEST
        )
        update = (values - memory) * strength[:, :, None]
        memory_state = memory_state + key_units[:, :, :, None] * update[:, :, None, :]
        reading = jnp.einsum(
            "bhkv,bhk->bhv", memory_state, queries, precision=lax.Precision.HIGHEST
        )
        scaled = reading * lax.rsqrt(jnp.mean(reading * reading, -1, keepdims=True) + epsilon)
        gate_vals = (
            gate_rows[:, position].astype(jnp.float32).reshape(batch_size, head_count, head_width)
        )
        gated_out = scaled * core_gain * jax.nn.silu(gate_vals)
        outputs.append(gated_out.reshape(batch_size, head_count * head_width).astype(jnp.bfloat16))
    return (memory_state.astype(jnp.bfloat16), jnp.stack(outputs, axis=1))


def migrate_kernel(src_hbm, tag_hbm, dst_hbm, tag_out, send_sem, recv_sem, tag_send, tag_recv, local_sem):
    lanes = src_hbm.shape[0]
    group = lax.axis_index("dp")
    me = lax.axis_index("ep")
    mesh_ids = pl.DeviceIdType.MESH
    barrier = pltpu.get_barrier_semaphore()
    for i in range(1, lanes):
        pl.semaphore_signal(barrier, 1, device_id=(group, lax.rem(me + i, lanes)), device_id_type=mesh_ids)
    pl.semaphore_wait(barrier, lanes - 1)
    own = pltpu.make_async_copy(src_hbm.at[me], dst_hbm.at[me], local_sem.at[0])
    own.start()
    own_tag = pltpu.make_async_copy(tag_hbm.at[me], tag_out.at[me], local_sem.at[1])
    own_tag.start()
    copies = []
    for i in range(1, lanes):
        peer = lax.rem(me + i, lanes)
        for source, target, sent, landed in ((tag_hbm, tag_out, tag_send, tag_recv), (src_hbm, dst_hbm, send_sem, recv_sem)):
            copy = pltpu.make_async_remote_copy(
                source.at[peer],
                target.at[me],
                sent.at[i - 1],
                landed.at[i - 1],
                device_id=(group, peer),
                device_id_type=mesh_ids,
            )
            copy.start()
            copies.append(copy)
    own.wait()
    own_tag.wait()
    for copy in copies:
        copy.wait()


def migrate(rows, tags):
    lanes = rows.shape[0]
    any_spec = pl.BlockSpec(memory_space=pl.ANY)
    return pl.pallas_call(
        migrate_kernel,
        in_specs=[any_spec, any_spec],
        out_specs=[any_spec, any_spec],
        out_shape=[
            jax.ShapeDtypeStruct(rows.shape, rows.dtype),
            jax.ShapeDtypeStruct(tags.shape, tags.dtype),
        ],
        scratch_shapes=[
            pltpu.SemaphoreType.DMA((lanes - 1,)),
            pltpu.SemaphoreType.DMA((lanes - 1,)),
            pltpu.SemaphoreType.DMA((lanes - 1,)),
            pltpu.SemaphoreType.DMA((lanes - 1,)),
            pltpu.SemaphoreType.DMA((2,)),
        ],
        compiler_params=pltpu.CompilerParams(collective_id=0, has_side_effects=True),
        cost_estimate=pl.CostEstimate(flops=0, transcendentals=0, bytes_accessed=2 * rows.size * rows.dtype.itemsize),
    )(rows, tags)

def project_kernel(rows_ref, weight_ref, out_ref, gathered, product, send_a, recv_a, send_b, recv_b, local_sem):
    lanes = gathered.shape[0]
    count = rows_ref.shape[0]
    block = weight_ref.shape[1]
    group = lax.axis_index("dp")
    me = lax.axis_index("ep")
    mesh_ids = pl.DeviceIdType.MESH
    barrier = pltpu.get_barrier_semaphore()
    for i in range(1, lanes):
        pl.semaphore_signal(barrier, 1, device_id=(group, lax.rem(me + i, lanes)), device_id_type=mesh_ids)
    pl.semaphore_wait(barrier, lanes - 1)
    own = pltpu.make_async_copy(rows_ref, gathered.at[me], local_sem)
    own.start()
    sends = []
    for i in range(1, lanes):
        copy = pltpu.make_async_remote_copy(
            rows_ref, gathered.at[me], send_a.at[i - 1], recv_a.at[i - 1],
            device_id=(group, lax.rem(me + i, lanes)), device_id_type=mesh_ids,
        )
        copy.start()
        sends.append(copy)
    own.wait()
    for copy in sends:
        copy.wait()
    width = gathered.shape[-1]
    stacked = gathered[...].reshape(lanes * count, width)
    product[...] = (
        jnp.dot(stacked, weight_ref[...], preferred_element_type=jnp.float32)
        .astype(product.dtype)
        .reshape(lanes, count, block)
    )
    columns = pl.ds(pl.multiple_of(me * block, block), block)
    back = pltpu.make_async_copy(product.at[me], out_ref.at[:, columns], local_sem)
    back.start()
    replies = []
    for i in range(1, lanes):
        peer = lax.rem(me + i, lanes)
        copy = pltpu.make_async_remote_copy(
            product.at[peer], out_ref.at[:, columns], send_b.at[i - 1], recv_b.at[i - 1],
            device_id=(group, peer), device_id_type=mesh_ids,
        )
        copy.start()
        replies.append(copy)
    back.wait()
    for copy in replies:
        copy.wait()


def project(rows, weight):
    lanes = lax.axis_size("ep")
    count, width = rows.shape
    block = weight.shape[1]
    vmem = pl.BlockSpec(memory_space=pltpu.VMEM)
    return pl.pallas_call(
        project_kernel,
        in_specs=[vmem, vmem],
        out_specs=vmem,
        out_shape=jax.ShapeDtypeStruct((count, lanes * block), rows.dtype),
        scratch_shapes=[
            pltpu.VMEM((lanes, count, width), rows.dtype),
            pltpu.VMEM((lanes, count, block), rows.dtype),
            pltpu.SemaphoreType.DMA((lanes - 1,)),
            pltpu.SemaphoreType.DMA((lanes - 1,)),
            pltpu.SemaphoreType.DMA((lanes - 1,)),
            pltpu.SemaphoreType.DMA((lanes - 1,)),
            pltpu.SemaphoreType.DMA,
        ],
        compiler_params=pltpu.CompilerParams(collective_id=1, has_side_effects=True),
    )(rows, weight)


def place_kernel(place_ref, in_hbm, out_hbm, held, in_sem, out_sem):
    count = in_hbm.shape[0]
    loads = []
    for j in range(count):
        load = pltpu.make_async_copy(in_hbm.at[j], held.at[j], in_sem.at[j])
        load.start()
        loads.append(load)
    stores = []
    for j in range(count):
        loads[j].wait()
        store = pltpu.make_async_copy(held.at[j], out_hbm.at[place_ref[j, 0, 0]], out_sem.at[j])
        store.start()
        stores.append(store)
    for store in stores:
        store.wait()


def place_rows(rows, places):
    count = rows.shape[0]
    any_spec = pl.BlockSpec(memory_space=pl.ANY)
    return pl.pallas_call(
        place_kernel,
        in_specs=[pl.BlockSpec(memory_space=pltpu.SMEM), any_spec],
        out_specs=any_spec,
        out_shape=jax.ShapeDtypeStruct(rows.shape, rows.dtype),
        scratch_shapes=[
            pltpu.VMEM(rows.shape, rows.dtype),
            pltpu.SemaphoreType.DMA((count,)),
            pltpu.SemaphoreType.DMA((count,)),
        ],
        compiler_params=pltpu.CompilerParams(vmem_limit_bytes=48 * 1024 * 1024),
    )(places, rows)

def rms_scale(values, gain):
    return values * lax.rsqrt(jnp.mean(values * values, -1, keepdims=True) + epsilon) * gain


def expert_apply(chosen_rows, gate_up, down_weight):
    hidden_units = down_weight.shape[0]
    joined = jnp.dot(chosen_rows, gate_up, preferred_element_type=jnp.float32)
    active = (jax.nn.silu(joined[:, :hidden_units]) * joined[:, hidden_units:]).astype(jnp.bfloat16)
    return jnp.dot(active, down_weight, preferred_element_type=jnp.float32).astype(jnp.bfloat16)


def pack(values, positions, lane_count):
    zeroed = jnp.zeros(values.shape, values.dtype)
    placed = zeroed.at[positions].set(values)
    return placed.reshape((lane_count, values.shape[0] // lane_count) + values.shape[1:])


def unpack(values):
    return values.reshape((values.shape[0] * values.shape[1],) + values.shape[2:])


def shards(
    states,
    query_rows,
    key_rows,
    value_rows,
    gate_rows,
    beta_logit,
    decay_logit,
    residual,
    route_ids,
    route_prob,
    out_weight,
    core_gain,
    moe_gain,
    gate_up,
    down_weight,
    new_home,
):
    req_count = states.shape[0]
    step_count = query_rows.shape[1]
    model_width = residual.shape[-1]
    ep_size = lax.axis_size("ep")
    dp_size = lax.axis_size("dp")
    target = new_home // req_count % ep_size
    new_place = new_home % req_count
    fresh_states, core_out = recurrence(
        target, states, query_rows, key_rows, value_rows, gate_rows, beta_logit, decay_logit, core_gain
    )
    packed_place = jnp.zeros_like(new_place).at[target].set(new_place)
    tags = jnp.broadcast_to(packed_place[:, None, None], (ep_size, 1, 128))
    moved_rows, moved_tags = migrate(fresh_states, tags)
    moved_out = place_rows(moved_rows, moved_tags)
    token_count = req_count * step_count
    core_flat = core_out.reshape(token_count, core_out.shape[-1])
    attention = project(core_flat, out_weight)
    hidden = (
        residual.reshape(token_count, model_width).astype(jnp.float32)
        + attention.astype(jnp.float32)
    ).astype(jnp.bfloat16)
    normed = rms_scale(hidden.astype(jnp.float32), moe_gain).astype(jnp.bfloat16)
    top_count = route_ids.shape[-1]
    experts = dp_size * ep_size
    capacity = (token_count * top_count + experts - 1) // experts + 1
    flat_ids = route_ids.reshape(-1)
    onehot = (flat_ids[:, None] == jnp.arange(experts, dtype=jnp.int32)[None, :]).astype(jnp.int32)
    route_rank = jnp.sum(jnp.cumsum(onehot, axis=0) * onehot, axis=1) - 1
    slot_index = flat_ids * capacity + route_rank
    slot_count = experts * capacity
    match = slot_index[None, :] == jnp.arange(slot_count, dtype=jnp.int32)[:, None]
    match = match.reshape(experts, capacity, token_count, top_count)
    pick = jnp.any(match, axis=-1).astype(jnp.bfloat16)
    lane_count = 128
    chunks = model_width // lane_count
    normed_tiles = normed.reshape(token_count, chunks, lane_count)
    outgoing = jnp.einsum(
        "esk,kcl->escl", pick, normed_tiles, preferred_element_type=jnp.float32
    ).astype(jnp.bfloat16)
    outgoing = outgoing.reshape(experts, capacity * chunks, lane_count)
    arrived = lax.all_to_all(outgoing, ("dp", "ep"), 0, 0, tiled=True)
    arrived = arrived.reshape(experts, capacity, chunks, lane_count)
    hidden_units = down_weight.shape[1]
    gate_tiles = gate_up[0].reshape(chunks, lane_count, gate_up.shape[-1])
    joined = jnp.einsum("escl,clf->esf", arrived, gate_tiles, preferred_element_type=jnp.float32)
    active = (jax.nn.silu(joined[..., :hidden_units]) * joined[..., hidden_units:]).astype(jnp.bfloat16)
    down_tiles = down_weight[0].reshape(hidden_units, chunks, lane_count)
    result = jnp.einsum(
        "esf,fcl->escl", active, down_tiles, preferred_element_type=jnp.float32
    ).astype(jnp.bfloat16)
    result = result.reshape(experts, capacity * chunks, lane_count)
    returned = lax.all_to_all(result, ("dp", "ep"), 0, 0, tiled=True)
    returned = returned.reshape(experts, capacity, chunks, lane_count)
    weights = route_prob.reshape(token_count, top_count)
    weights = weights / jnp.sum(weights, -1, keepdims=True)
    spread = jnp.sum(jnp.where(match, weights[None, None, :, :], 0.0), axis=-1)
    high = spread.astype(jnp.bfloat16)
    rest = spread - high.astype(jnp.float32)
    middle = rest.astype(jnp.bfloat16)
    low = (rest - middle.astype(jnp.float32)).astype(jnp.bfloat16)
    parts = jnp.concatenate([high, middle, low], axis=-1)
    combined = jnp.einsum("esk,escl->kcl", parts, returned, preferred_element_type=jnp.float32)
    combined = combined.reshape(3, token_count, chunks, lane_count).sum(axis=0)
    combined = combined.reshape(token_count, model_width)
    mixed_out = (
        (hidden.astype(jnp.float32) + combined)
        .astype(jnp.bfloat16)
        .reshape(req_count, step_count, model_width)
    )
    return (mixed_out, moved_out)


def solution(mesh):
    placed = (
        P(("dp", "ep"), None, None, None),
        P(("dp", "ep"), None, None),
        P(("dp", "ep"), None, None),
        P(("dp", "ep"), None, None),
        P(("dp", "ep"), None, None),
        P(("dp", "ep"), None, None),
        P(("dp", "ep"), None, None),
        P(("dp", "ep"), None, None),
        P(("dp", "ep"), None, None),
        P(("dp", "ep"), None, None),
        P(None, "ep"),
        P(),
        P(),
        P(("dp", "ep"), None, None),
        P(("dp", "ep"), None, None),
        P(("dp", "ep")),
    )
    return jax.shard_map(
        shards,
        mesh=mesh,
        in_specs=placed,
        out_specs=(P(("dp", "ep"), None, None), P(("dp", "ep"), None, None, None)),
        check_vma=False,
    )
```

```python
import jax
import jax.numpy as jnp
from jax import lax
from jax.sharding import PartitionSpec as P

import functools
from jax.experimental import pallas as pl
from jax.experimental.pallas import tpu as pltpu

epsilon = 1e-06
f32 = jnp.float32
bf16 = jnp.bfloat16


def split2(x):
    hi = x.astype(bf16)
    lo = (x - hi.astype(f32)).astype(bf16)
    return hi, lo


def recur_kernel(slot_ref, s_ref, kq_ref, v_ref, g_ref, dec_ref, beta_ref, gain_ref, so_ref, co_ref, n_ref, r_ref, u_ref, c_ref):
    heads = s_ref.shape[1]
    width = s_ref.shape[-1]
    steps = v_ref.shape[1]
    span = 2 * steps
    kq = kq_ref[0].astype(f32)
    kq = kq * lax.rsqrt(jnp.sum(kq * kq, -1, keepdims=True) + epsilon)
    row = lax.broadcasted_iota(jnp.int32, kq.shape, 0)
    kq = jnp.where(row % span >= steps, kq * width ** (-0.5), kq)
    n_ref[...] = kq
    for h in range(heads):
        p = n_ref[pl.ds(h * span, span), :]
        hi = p.astype(bf16).astype(f32)
        rest = p - hi
        mid = rest.astype(bf16).astype(f32)
        lo = rest - mid
        lhs = jnp.concatenate([hi, mid, lo], axis=0).astype(bf16)
        res = jnp.dot(lhs, s_ref[0, h], preferred_element_type=f32)
        r_ref[pl.ds(h * span, span), :] = (res[0:span] + res[span:2 * span]) + res[2 * span:3 * span]
    decay = jax.nn.sigmoid(dec_ref[0].astype(f32)).T
    strength = jax.nn.sigmoid(beta_ref[0].astype(f32)).T
    gain = gain_ref[...]
    keys = [n_ref[pl.ds(t, heads, stride=span), :] for t in range(steps)]
    queries = [n_ref[pl.ds(steps + t, heads, stride=span), :] for t in range(steps)]
    u_ref[...] = jnp.zeros(u_ref.shape, f32)
    updates = []
    carried = []
    total = None
    for t in range(steps):
        a_t = decay[:, t:t + 1]
        b_t = strength[:, t:t + 1]
        total = a_t if t == 0 else total * a_t
        carried = [c * a_t for c in carried]
        memory = total * r_ref[pl.ds(t, heads, stride=span), :]
        for j in range(t):
            kk = jnp.sum(keys[j] * keys[t], -1, keepdims=True)
            memory = memory + (carried[j] * kk) * updates[j]
        values = jnp.concatenate([v_ref[0, pl.ds(t, 1), pl.ds(h * width, width)] for h in range(heads)], axis=0).astype(f32)
        update = (values - memory) * b_t
        updates.append(update)
        carried.append(jnp.ones_like(a_t))
        reading = total * r_ref[pl.ds(steps + t, heads, stride=span), :]
        for j in range(t + 1):
            qk = jnp.sum(keys[j] * queries[t], -1, keepdims=True)
            coef = qk if j == t else carried[j] * qk
            reading = reading + coef * updates[j]
        scaled = reading * lax.rsqrt(jnp.mean(reading * reading, -1, keepdims=True) + epsilon)
        gate_vals = jnp.concatenate([g_ref[0, pl.ds(t, 1), pl.ds(h * width, width)] for h in range(heads)], axis=0).astype(f32)
        c_ref[pl.ds(t * heads, heads), :] = scaled * gain * (gate_vals * jax.nn.sigmoid(gate_vals))
    for j in range(steps):
        u_ref[pl.ds(j, heads, stride=span), :] = carried[j] * updates[j]
    for h in range(heads):
        co_ref[0, :, pl.ds(h * width, width)] = c_ref[pl.ds(h, steps, stride=heads), :].astype(co_ref.dtype)
    for h in range(heads):
        kt = n_ref[pl.ds(h * span, span), :].T
        w = u_ref[pl.ds(h * span, span), :]
        k_hi, k_lo = split2(kt)
        w_hi, w_lo = split2(w)
        delta = (
            jnp.dot(k_hi, w_hi, preferred_element_type=f32)
            + jnp.dot(k_hi, w_lo, preferred_element_type=f32)
            + jnp.dot(k_lo, w_hi, preferred_element_type=f32)
        )
        so_ref[0, h] = (total[h:h + 1, :] * s_ref[0, h].astype(f32) + delta).astype(so_ref.dtype)


def recurrence(slots, states, query_rows, key_rows, value_rows, gate_rows, beta_logit, decay_logit, core_gain):
    batch, heads, width, _ = states.shape
    steps = query_rows.shape[1]
    key_heads = query_rows.shape[-1] // width
    repeats = heads // key_heads
    span = 2 * steps
    kq = jnp.concatenate(
        [key_rows.reshape(batch, steps, key_heads, width), query_rows.reshape(batch, steps, key_heads, width)], axis=1
    )
    kq = jnp.repeat(kq.transpose(0, 2, 1, 3), repeats, axis=1).reshape(batch, heads * span, width)
    values = value_rows
    gates = gate_rows
    decay = decay_logit
    beta = beta_logit
    gain = core_gain.reshape(1, width)
    state_in = pl.BlockSpec((1, heads, width, width), lambda i, slot: (i, 0, 0, 0))
    state_out = pl.BlockSpec((1, heads, width, width), lambda i, slot: (slot[i], 0, 0, 0))
    row_spec = pl.BlockSpec((1, steps, heads, width), lambda i, slot: (i, 0, 0, 0))
    coef_spec = pl.BlockSpec((1, steps, heads), lambda i, slot: (i, 0, 0))
    fresh, core = pl.pallas_call(
        recur_kernel,
        grid_spec=pltpu.PrefetchScalarGridSpec(
            num_scalar_prefetch=1,
            grid=(batch,),
            in_specs=[
                state_in,
                pl.BlockSpec((1, heads * span, width), lambda i, slot: (i, 0, 0)),
                pl.BlockSpec((1, steps, heads * width), lambda i, slot: (i, 0, 0)),
                pl.BlockSpec((1, steps, heads * width), lambda i, slot: (i, 0, 0)),
                coef_spec,
                coef_spec,
                pl.BlockSpec((1, width), lambda i, slot: (0, 0)),
            ],
            out_specs=[state_out, pl.BlockSpec((1, steps, heads * width), lambda i, slot: (i, 0, 0))],
            scratch_shapes=[pltpu.VMEM((heads * span, width), f32)] * 3 + [pltpu.VMEM((steps * heads, width), f32)],
        ),
        out_shape=[
            jax.ShapeDtypeStruct(states.shape, bf16),
            jax.ShapeDtypeStruct((batch, steps, heads * width), bf16),
        ],
    )(slots, states, kq, values, gates, decay, beta, gain)
    return fresh, core


def unit_rows(values):
    return values * lax.rsqrt(jnp.sum(values * values, -1, keepdims=True) + epsilon)


def delta_block(
    state_in, query_rows, key_rows, value_rows, gate_rows, beta_logit, decay_logit, core_gain
):
    batch_size = state_in.shape[0]
    head_count = decay_logit.shape[-1]
    head_width = state_in.shape[-1]
    key_heads = query_rows.shape[-1] // head_width
    repeats = head_count // key_heads
    memory_state = state_in.astype(jnp.float32)
    outputs = []
    for position in range(query_rows.shape[1]):
        queries = unit_rows(
            query_rows[:, position].astype(jnp.float32).reshape(batch_size, key_heads, head_width)
        )
        queries = jnp.repeat(queries, repeats, axis=1) * head_width ** (-0.5)
        key_units = unit_rows(
            key_rows[:, position].astype(jnp.float32).reshape(batch_size, key_heads, head_width)
        )
        key_units = jnp.repeat(key_units, repeats, axis=1)
        values = (
            value_rows[:, position].astype(jnp.float32).reshape(batch_size, head_count, head_width)
        )
        decays = jax.nn.sigmoid(decay_logit[:, position].astype(jnp.float32))
        strength = jax.nn.sigmoid(beta_logit[:, position].astype(jnp.float32))
        memory_state = memory_state * decays[:, :, None, None]
        memory = jnp.einsum(
            "bhkv,bhk->bhv", memory_state, key_units, precision=lax.Precision.HIGHEST
        )
        update = (values - memory) * strength[:, :, None]
        memory_state = memory_state + key_units[:, :, :, None] * update[:, :, None, :]
        reading = jnp.einsum(
            "bhkv,bhk->bhv", memory_state, queries, precision=lax.Precision.HIGHEST
        )
        scaled = reading * lax.rsqrt(jnp.mean(reading * reading, -1, keepdims=True) + epsilon)
        gate_vals = (
            gate_rows[:, position].astype(jnp.float32).reshape(batch_size, head_count, head_width)
        )
        gated_out = scaled * core_gain * jax.nn.silu(gate_vals)
        outputs.append(gated_out.reshape(batch_size, head_count * head_width).astype(jnp.bfloat16))
    return (memory_state.astype(jnp.bfloat16), jnp.stack(outputs, axis=1))


def migrate_kernel(src_hbm, tag_hbm, dst_hbm, tag_out, send_sem, recv_sem, tag_send, tag_recv, local_sem):
    lanes = src_hbm.shape[0]
    group = lax.axis_index("dp")
    me = lax.axis_index("ep")
    mesh_ids = pl.DeviceIdType.MESH
    barrier = pltpu.get_barrier_semaphore()
    for i in range(1, lanes):
        pl.semaphore_signal(barrier, 1, device_id=(group, lax.rem(me + i, lanes)), device_id_type=mesh_ids)
    pl.semaphore_wait(barrier, lanes - 1)
    own = pltpu.make_async_copy(src_hbm.at[me], dst_hbm.at[me], local_sem.at[0])
    own.start()
    own_tag = pltpu.make_async_copy(tag_hbm.at[me], tag_out.at[me], local_sem.at[1])
    own_tag.start()
    copies = []
    for i in range(1, lanes):
        peer = lax.rem(me + i, lanes)
        for source, target, sent, landed in ((tag_hbm, tag_out, tag_send, tag_recv), (src_hbm, dst_hbm, send_sem, recv_sem)):
            copy = pltpu.make_async_remote_copy(
                source.at[peer],
                target.at[me],
                sent.at[i - 1],
                landed.at[i - 1],
                device_id=(group, peer),
                device_id_type=mesh_ids,
            )
            copy.start()
            copies.append(copy)
    own.wait()
    own_tag.wait()
    for copy in copies:
        copy.wait()


def migrate(rows, tags):
    lanes = rows.shape[0]
    any_spec = pl.BlockSpec(memory_space=pl.ANY)
    return pl.pallas_call(
        migrate_kernel,
        in_specs=[any_spec, any_spec],
        out_specs=[any_spec, any_spec],
        out_shape=[
            jax.ShapeDtypeStruct(rows.shape, rows.dtype),
            jax.ShapeDtypeStruct(tags.shape, tags.dtype),
        ],
        scratch_shapes=[
            pltpu.SemaphoreType.DMA((lanes - 1,)),
            pltpu.SemaphoreType.DMA((lanes - 1,)),
            pltpu.SemaphoreType.DMA((lanes - 1,)),
            pltpu.SemaphoreType.DMA((lanes - 1,)),
            pltpu.SemaphoreType.DMA((2,)),
        ],
        compiler_params=pltpu.CompilerParams(collective_id=0, has_side_effects=True),
        cost_estimate=pl.CostEstimate(flops=0, transcendentals=0, bytes_accessed=2 * rows.size * rows.dtype.itemsize),
    )(rows, tags)

def project_kernel(rows_ref, weight_ref, out_ref, gathered, product, send_a, recv_a, send_b, recv_b, local_sem):
    lanes = gathered.shape[0]
    count = rows_ref.shape[0]
    block = weight_ref.shape[1]
    group = lax.axis_index("dp")
    me = lax.axis_index("ep")
    mesh_ids = pl.DeviceIdType.MESH
    barrier = pltpu.get_barrier_semaphore()
    for i in range(1, lanes):
        pl.semaphore_signal(barrier, 1, device_id=(group, lax.rem(me + i, lanes)), device_id_type=mesh_ids)
    pl.semaphore_wait(barrier, lanes - 1)
    own = pltpu.make_async_copy(rows_ref, gathered.at[me], local_sem)
    own.start()
    sends = []
    for i in range(1, lanes):
        copy = pltpu.make_async_remote_copy(
            rows_ref, gathered.at[me], send_a.at[i - 1], recv_a.at[i - 1],
            device_id=(group, lax.rem(me + i, lanes)), device_id_type=mesh_ids,
        )
        copy.start()
        sends.append(copy)
    own.wait()
    for copy in sends:
        copy.wait()
    width = gathered.shape[-1]
    stacked = gathered[...].reshape(lanes * count, width)
    product[...] = (
        jnp.dot(stacked, weight_ref[...], preferred_element_type=jnp.float32)
        .astype(product.dtype)
        .reshape(lanes, count, block)
    )
    columns = pl.ds(pl.multiple_of(me * block, block), block)
    back = pltpu.make_async_copy(product.at[me], out_ref.at[:, columns], local_sem)
    back.start()
    replies = []
    for i in range(1, lanes):
        peer = lax.rem(me + i, lanes)
        copy = pltpu.make_async_remote_copy(
            product.at[peer], out_ref.at[:, columns], send_b.at[i - 1], recv_b.at[i - 1],
            device_id=(group, peer), device_id_type=mesh_ids,
        )
        copy.start()
        replies.append(copy)
    back.wait()
    for copy in replies:
        copy.wait()


def project(rows, weight):
    lanes = lax.axis_size("ep")
    count, width = rows.shape
    block = weight.shape[1]
    vmem = pl.BlockSpec(memory_space=pltpu.VMEM)
    return pl.pallas_call(
        project_kernel,
        in_specs=[vmem, vmem],
        out_specs=vmem,
        out_shape=jax.ShapeDtypeStruct((count, lanes * block), rows.dtype),
        scratch_shapes=[
            pltpu.VMEM((lanes, count, width), rows.dtype),
            pltpu.VMEM((lanes, count, block), rows.dtype),
            pltpu.SemaphoreType.DMA((lanes - 1,)),
            pltpu.SemaphoreType.DMA((lanes - 1,)),
            pltpu.SemaphoreType.DMA((lanes - 1,)),
            pltpu.SemaphoreType.DMA((lanes - 1,)),
            pltpu.SemaphoreType.DMA,
        ],
        compiler_params=pltpu.CompilerParams(collective_id=1, has_side_effects=True),
    )(rows, weight)


def place_kernel(place_ref, in_hbm, out_hbm, held, in_sem, out_sem):
    count = in_hbm.shape[0]
    loads = []
    for j in range(count):
        load = pltpu.make_async_copy(in_hbm.at[j], held.at[j], in_sem.at[j])
        load.start()
        loads.append(load)
    stores = []
    for j in range(count):
        loads[j].wait()
        store = pltpu.make_async_copy(held.at[j], out_hbm.at[place_ref[j, 0, 0]], out_sem.at[j])
        store.start()
        stores.append(store)
    for store in stores:
        store.wait()


def place_rows(rows, places):
    count = rows.shape[0]
    any_spec = pl.BlockSpec(memory_space=pl.ANY)
    return pl.pallas_call(
        place_kernel,
        in_specs=[pl.BlockSpec(memory_space=pltpu.SMEM), any_spec],
        out_specs=any_spec,
        out_shape=jax.ShapeDtypeStruct(rows.shape, rows.dtype),
        scratch_shapes=[
            pltpu.VMEM(rows.shape, rows.dtype),
            pltpu.SemaphoreType.DMA((count,)),
            pltpu.SemaphoreType.DMA((count,)),
        ],
        compiler_params=pltpu.CompilerParams(vmem_limit_bytes=48 * 1024 * 1024),
    )(places, rows)

def rms_scale(values, gain):
    return values * lax.rsqrt(jnp.mean(values * values, -1, keepdims=True) + epsilon) * gain


def expert_apply(chosen_rows, gate_up, down_weight):
    hidden_units = down_weight.shape[0]
    joined = jnp.dot(chosen_rows, gate_up, preferred_element_type=jnp.float32)
    active = (jax.nn.silu(joined[:, :hidden_units]) * joined[:, hidden_units:]).astype(jnp.bfloat16)
    return jnp.dot(active, down_weight, preferred_element_type=jnp.float32).astype(jnp.bfloat16)


def pack(values, positions, lane_count):
    zeroed = jnp.zeros(values.shape, values.dtype)
    placed = zeroed.at[positions].set(values)
    return placed.reshape((lane_count, values.shape[0] // lane_count) + values.shape[1:])


def unpack(values):
    return values.reshape((values.shape[0] * values.shape[1],) + values.shape[2:])


def shards(
    states,
    query_rows,
    key_rows,
    value_rows,
    gate_rows,
    beta_logit,
    decay_logit,
    residual,
    route_ids,
    route_prob,
    out_weight,
    core_gain,
    moe_gain,
    gate_up,
    down_weight,
    new_home,
):
    req_count = states.shape[0]
    step_count = query_rows.shape[1]
    model_width = residual.shape[-1]
    ep_size = lax.axis_size("ep")
    dp_size = lax.axis_size("dp")
    target = new_home // req_count % ep_size
    new_place = new_home % req_count
    fresh_states, core_out = recurrence(
        target, states, query_rows, key_rows, value_rows, gate_rows, beta_logit, decay_logit, core_gain
    )
    packed_place = jnp.zeros_like(new_place).at[target].set(new_place)
    tags = jnp.broadcast_to(packed_place[:, None, None], (ep_size, 1, 128))
    moved_rows, moved_tags = migrate(fresh_states, tags)
    moved_out = place_rows(moved_rows, moved_tags)
    token_count = req_count * step_count
    core_flat = core_out.reshape(token_count, core_out.shape[-1])
    attention = project(core_flat, out_weight)
    hidden = (
        residual.reshape(token_count, model_width).astype(jnp.float32)
        + attention.astype(jnp.float32)
    ).astype(jnp.bfloat16)
    normed = rms_scale(hidden.astype(jnp.float32), moe_gain).astype(jnp.bfloat16)
    top_count = route_ids.shape[-1]
    experts = dp_size * ep_size
    capacity = (token_count * top_count + experts - 1) // experts + 1
    flat_ids = route_ids.reshape(-1)
    onehot = (flat_ids[:, None] == jnp.arange(experts, dtype=jnp.int32)[None, :]).astype(jnp.int32)
    route_rank = jnp.sum(jnp.cumsum(onehot, axis=0) * onehot, axis=1) - 1
    slot_index = flat_ids * capacity + route_rank
    slot_count = experts * capacity
    match = slot_index[None, :] == jnp.arange(slot_count, dtype=jnp.int32)[:, None]
    match = match.reshape(experts, capacity, token_count, top_count)
    pick = jnp.any(match, axis=-1).astype(jnp.bfloat16)
    lane_count = 128
    chunks = model_width // lane_count
    normed_tiles = normed.reshape(token_count, chunks, lane_count)
    outgoing = jnp.einsum(
        "esk,kcl->escl", pick, normed_tiles, preferred_element_type=jnp.float32
    ).astype(jnp.bfloat16)
    outgoing = outgoing.reshape(experts, capacity * chunks, lane_count)
    arrived = lax.all_to_all(outgoing, ("dp", "ep"), 0, 0, tiled=True)
    arrived = arrived.reshape(experts, capacity, chunks, lane_count)
    hidden_units = down_weight.shape[1]
    gate_tiles = gate_up[0].reshape(chunks, lane_count, gate_up.shape[-1])
    joined = jnp.einsum("escl,clf->esf", arrived, gate_tiles, preferred_element_type=jnp.float32)
    active = (jax.nn.silu(joined[..., :hidden_units]) * joined[..., hidden_units:]).astype(jnp.bfloat16)
    down_tiles = down_weight[0].reshape(hidden_units, chunks, lane_count)
    result = jnp.einsum(
        "esf,fcl->escl", active, down_tiles, preferred_element_type=jnp.float32
    ).astype(jnp.bfloat16)
    result = result.reshape(experts, capacity * chunks, lane_count)
    returned = lax.all_to_all(result, ("dp", "ep"), 0, 0, tiled=True)
    returned = returned.reshape(experts, capacity, chunks, lane_count)
    weights = route_prob.reshape(token_count, top_count)
    weights = weights / jnp.sum(weights, -1, keepdims=True)
    spread = jnp.sum(jnp.where(match, weights[None, None, :, :], 0.0), axis=-1)
    high = spread.astype(jnp.bfloat16)
    rest = spread - high.astype(jnp.float32)
    middle = rest.astype(jnp.bfloat16)
    low = (rest - middle.astype(jnp.float32)).astype(jnp.bfloat16)
    parts = jnp.concatenate([high, middle, low], axis=-1)
    combined = jnp.einsum("esk,escl->kcl", parts, returned, preferred_element_type=jnp.float32)
    combined = combined.reshape(3, token_count, chunks, lane_count).sum(axis=0)
    combined = combined.reshape(token_count, model_width)
    mixed_out = (
        (hidden.astype(jnp.float32) + combined)
        .astype(jnp.bfloat16)
        .reshape(req_count, step_count, model_width)
    )
    return (mixed_out, moved_out)


def solution(mesh):
    placed = (
        P(("dp", "ep"), None, None, None),
        P(("dp", "ep"), None, None),
        P(("dp", "ep"), None, None),
        P(("dp", "ep"), None, None),
        P(("dp", "ep"), None, None),
        P(("dp", "ep"), None, None),
        P(("dp", "ep"), None, None),
        P(("dp", "ep"), None, None),
        P(("dp", "ep"), None, None),
        P(("dp", "ep"), None, None),
        P(None, "ep"),
        P(),
        P(),
        P(("dp", "ep"), None, None),
        P(("dp", "ep"), None, None),
        P(("dp", "ep")),
    )
    return jax.shard_map(
        shards,
        mesh=mesh,
        in_specs=placed,
        out_specs=(P(("dp", "ep"), None, None), P(("dp", "ep"), None, None, None)),
        check_vma=False,
    )
```
